32 devices in a mesh: expert: 8 (over z, x), context: 2 (over core), dp: 2 (over y).
Axes of the slice: x: 2, y: 2, z: 4, core: 2. Of those that a mesh axis runs over, the one named last changes fastest.
Arguments:
- tokens: bfloat16 [2, 16, 768, 1024], P(None, ('expert', 'dp'), 'context'), may hold values from -6 to 6
- out_grad: bfloat16 [2, 16, 768, 1024], P(None, ('expert', 'dp'), 'context'), may hold values from -6 to 6
- seq_lengths: int32 [2, 16, 3], P(None, ('expert', 'dp')), may hold values from 1 to 512, 768 in all within a row
- token_order: int32 [2, 16, 768], P(None, ('expert', 'dp')), may hold values from 0 to 767, each once within a row
- expert_route: int32 [2, 16, 768, 1], P(None, ('expert', 'dp'), 'context'), may hold values from 0 to 7; in each aligned block of 384 rows (0 to 383, 384 to 767, ..., all dimensions but the last counted through in order) at most 54 rows name the same one
- mixer_gain: float32 [1024], replicated, may hold values from 0.1 to 1.9
- mixer_shift: float32 [1024], replicated, may hold values from -4 to 4
- project_in: bfloat16 [1024, 3072], replicated, may hold values from -0.25 to 0.25
- project_out: bfloat16 [1024, 1024], replicated, may hold values from -1 to 1
- expert_gain: float32 [1024], replicated, may hold values from 0.1 to 1.9
- expert_shift: float32 [1024], replicated, may hold values from -4 to 4
- router_weight: bfloat16 [1024, 8], replicated, may hold values from -0.09375 to 0.09375
- expert_in: bfloat16 [8, 1024, 4096], P('expert', ('context', 'dp')), may hold values from -0.1875 to 0.1875
- expert_out: bfloat16 [8, 4096, 1024], P('expert', ('context', 'dp')), may hold values from -0.75 to 0.75
Outputs:
- block_out: bfloat16 [2, 16, 768, 1024], P(None, ('expert', 'dp'), 'context')
- grad_tokens: float32 [2, 16, 768, 1024], P(None, ('expert', 'dp'), 'context')
- grad_mixer_gain: float32 [1024], replicated
- grad_mixer_shift: float32 [1024], replicated
- grad_project_in: float32 [1024, 3072], replicated
- grad_project_out: float32 [1024, 1024], replicated
- grad_expert_gain: float32 [1024], replicated
- grad_expert_shift: float32 [1024], replicated
- grad_router: float32 [1024, 8], replicated
- grad_expert_in: float32 [8, 1024, 4096], P('expert', ('context', 'dp'))
- grad_expert_out: float32 [8, 4096, 1024], P('expert', ('context', 'dp'))
The draws below stay inside these ranges and needn't reach their ends.
Inputs may be any that keep to these rules, and one draw needn't show every extreme that they name: `seq_lengths`: each pack's lengths add up to 768 and the longest is 512. `token_order`: each pack's rows hold each of its 768 positions once. `expert_route`: among the 384 rows of one device in one micro-batch (aligned blocks), at most 54 route to one expert.
All inputs are finite; a program needn't handle non-finite values.
Results may differ from the reference program's by a relative error of at most 0.022.
Values may be sent and summed in bfloat16 or wider, within the bound.
No kernel may reach another device: no remote copies, remote signals or barrier semaphores. Data moves between devices by JAX's collectives and lax.ppermute only.
A program may use at most 320 MiB of HBM per device.

```python
import math
from functools import partial
import jax
import jax.numpy as jnp
import numpy as np
from jax import lax

D = 1024
HEADS = 16
HEAD_DIM = 64
FF = 4096
TOK_MB = 384
MB = 2
NSEQ = 3
EXPERTS = 8
CAP = 54
CTX = 768
LONGEST = 512
PACKS = 16
N_CONTEXT = 2


def block_scale(rng, shape, split, smallest, high):
    loudness, own = 1.0, jax.random.fold_in(rng, 6)
    for position, parts in split:
        steps = jnp.exp(jax.random.uniform(jax.random.fold_in(own, position), (parts,), jnp.float32, smallest / len(split), high / len(split)))
        loudness = loudness * jnp.repeat(steps, shape[position] // parts).reshape([-1 if axis == position else 1 for axis in range(len(shape))])
    return loudness


def split_up(count, total, bound, lean):
    portions = [(1 << 20) // math.isqrt(grade ** lean) + 1 for grade in range(2, count + 1)]
    spare, counts = total - bound - (count - 1), [1] * (count - 1)
    while spare > 0:
        movable = [i for i in range(count - 1) if counts[i] < bound]
        mass, budget = sum([portions[i] for i in movable]), spare
        for i in movable:
            extra = min(bound - counts[i], max(1, budget * portions[i] // mass), spare)
            counts[i] = counts[i] + extra
            spare = spare - extra
    return np.array([bound] + counts)


def ragged_sizes(rng, amount, total, bound, slope):
    if amount == 2:
        one = jax.random.randint(rng, (), max(1, total - bound), min(bound, total - 1) + 1)
        return jnp.stack([one, total - one])
    tallies = jnp.asarray(split_up(amount, total, bound, slope), jnp.int32)
    couples = (amount - 1) // 2
    donor, receiver = tallies[1:1 + 2 * couples:2], tallies[2:2 + 2 * couples:2]
    room = jnp.minimum(donor - 1, bound - receiver)
    shifted = jax.random.randint(jax.random.fold_in(rng, 1), (couples,), 0, 1 << 20) % (room + 1)
    tallies = tallies.at[1:1 + 2 * couples:2].set(donor - shifted).at[2:2 + 2 * couples:2].set(receiver + shifted)
    return tallies[jax.random.permutation(jax.random.fold_in(rng, 2), amount)]


def routed_block(rng, own, number, rows, count, top, limit, slope):
    order = jax.random.permutation(rng, count)
    crowded, usual = load_shares(count, rows * top, limit, slope, True), load_shares(count, rows * top, limit, slope, False)
    places = jnp.arange(count)

    def named(sizes, rotation):
        used = int((sizes > 0).sum())
        fixed = max(1, used // 4)
        passed = fixed + (places - fixed + rotation * (used - fixed)) % max(1, count - fixed)
        return jnp.zeros((count,), jnp.int32).at[order[jnp.where(places < fixed, places, passed)]].set(jnp.asarray(sizes, jnp.int32))

    sizes = jnp.where(number % 4 == 0, named(crowded, number // 4), named(usual, number - number // 4 - 1))
    mixed = jax.random.permutation(jax.random.fold_in(own, 3), count)
    source_of, receiver = mixed[0:count // 2 * 2:2], mixed[1:count // 2 * 2:2]
    room = jnp.minimum(sizes[source_of] - 1, limit - sizes[receiver]) // 2
    room = jnp.where((source_of == order[0]) | (receiver == order[0]) | (sizes[receiver] == 0), 0, jnp.maximum(room, 0))
    passed = jax.random.randint(jax.random.fold_in(own, 4), (count // 2,), 0, 1 << 20) % (room + 1)
    sizes = sizes.at[source_of].add(-passed).at[receiver].add(passed)
    labels = jnp.searchsorted(jnp.cumsum(sizes), jnp.arange(rows * top), side="right").astype(jnp.int32)
    grid = labels.reshape(top, rows).T
    grid = grid[jax.random.permutation(jax.random.fold_in(own, 1), rows)]
    rotation = jax.random.randint(jax.random.fold_in(own, 2), (rows, 1), 0, top)
    return jnp.take_along_axis(grid, (jnp.arange(top)[None, :] + rotation) % top, axis=1)


def load_shares(number_of, total, bound, lean, full):
    portions = [(1 << 20) // math.isqrt(standing ** lean) + 1 for standing in range(1, number_of + 1)]
    largest = bound if full else min(bound, max(-(-total // number_of), total * portions[0] // sum(portions)))
    least = 1 if total - largest >= number_of - 1 else 0
    counts, spare = [largest] + [least] * (number_of - 1), total - largest - least * (number_of - 1)
    while spare > 0:
        free = [i for i in range(1, number_of) if counts[i] < largest] or [i for i in range(1, number_of) if counts[i] < bound]
        mass, budget = sum([portions[i] for i in free]), spare
        for i in free:
            addition = min(bound - counts[i], max(1, budget * portions[i] // mass), spare)
            counts[i] = counts[i] + addition
            spare = spare - addition
    return np.array(counts)


def centred(rng, extent, width, limit, split=(), kind=jnp.bfloat16):
    loudness = block_scale(rng, extent, split, -0.22, 0.18) if split else 1.0
    values = jax.random.normal(rng, extent, jnp.float32) * width * loudness
    return jnp.minimum(jnp.maximum(values, -limit), limit).astype(kind)


def setup_inputs(seed: int = 0) -> dict:
    key_list = jax.random.split(jax.random.key(seed), 15)
    tokens = centred(key_list[0], (MB, PACKS, CTX, D), 1.0, 6.0, ((1, 16), (2, 2)))
    out_grad = centred(key_list[1], (MB, PACKS, CTX, D), 1.0, 6.0, ((1, 16), (2, 2)))
    seq_lengths = jax.vmap(lambda own: ragged_sizes(own, NSEQ, CTX, LONGEST, 2))(jax.random.split(key_list[2], MB * PACKS)).reshape((MB, PACKS, NSEQ)).astype(jnp.int32)
    token_order = jax.vmap(lambda own: jax.random.permutation(own, CTX))(jax.random.split(key_list[3], MB * PACKS)).reshape((MB, PACKS, CTX)).astype(jnp.int32)
    expert_route_keys = jax.random.split(jax.random.fold_in(key_list[4], 1), MB * PACKS * CTX // TOK_MB)
    expert_route_turns = jax.random.permutation(jax.random.fold_in(key_list[4], 3), MB * PACKS * CTX // TOK_MB)
    expert_route = jax.vmap(lambda own, number: routed_block(jax.random.fold_in(key_list[4], 2), own, number, TOK_MB, EXPERTS, 1, CAP, 2))(expert_route_keys, expert_route_turns).reshape((MB, PACKS, CTX, 1))
    mixer_gain = jnp.clip(1.0 + 0.18 * jax.random.normal(key_list[5], (D,), jnp.float32), 0.1, 1.9)
    mixer_shift = centred(key_list[6], (D,), 0.3, 4.0, (), jnp.float32)
    project_in = centred(key_list[7], (D, 3 * D), (D // 2) ** -0.5, 0.25)
    project_out = centred(key_list[8], (D, D), (D // 32) ** -0.5, 1.0)
    expert_gain = jnp.clip(1.0 + 0.18 * jax.random.normal(key_list[9], (D,), jnp.float32), 0.1, 1.9)
    expert_shift = centred(key_list[10], (D,), 0.3, 4.0, (), jnp.float32)
    router_weight = centred(key_list[11], (D, EXPERTS), (4 * D) ** -0.5, 0.09375)
    expert_in = centred(key_list[12], (EXPERTS, D, FF), D ** -0.5, 0.1875, ((0, 8), (1, 4)))
    expert_out = centred(key_list[13], (EXPERTS, FF, D), (max(1, FF // (EXPERTS * EXPERTS))) ** -0.5, 0.75, ((0, 8), (1, 4)))
    return {"tokens": tokens, "out_grad": out_grad, "seq_lengths": seq_lengths, "token_order": token_order, "expert_route": expert_route, "mixer_gain": mixer_gain, "mixer_shift": mixer_shift, "project_in": project_in, "project_out": project_out, "expert_gain": expert_gain, "expert_shift": expert_shift, "router_weight": router_weight, "expert_in": expert_in, "expert_out": expert_out}


EPS = 1e-05
HIGH = lax.Precision.HIGHEST

@jax.custom_vjp
def low(v):
    return lax.optimization_barrier(v.astype(jnp.bfloat16)).astype(jnp.float32)

@jax.custom_vjp
def low_back(v):
    return v

def low_keep(v):
    return (low(v), None)

def low_pass(kept, grad):
    return (grad,)

def back_keep(v):
    return (v, None)

def back_low(kept, grad):
    return (low(grad),)
low.defvjp(low_keep, low_pass)
low_back.defvjp(back_keep, back_low)

def layer_norm(values, gain, shift):
    center = values - lax.optimization_barrier(jnp.mean(values, axis=-1, keepdims=True))
    return center * lax.rsqrt(lax.optimization_barrier(jnp.mean(center * center, axis=-1, keepdims=True)) + EPS) * gain + shift

def attend_block(block, keys, values, key_positions, key_segments):
    query, query_positions, query_segments = block
    scores = low_back(jnp.einsum('qhd,khd->hqk', query, keys, precision=HIGH) * 0.125)
    allowed = (key_positions[None, :] <= query_positions[:, None]) & (key_segments[None, :] == query_segments[:, None])
    scores = jnp.where(allowed[None], scores, -1e+30)
    weights = low(jax.nn.softmax(scores, axis=-1))
    return jnp.einsum('hqk,khd->qhd', weights, values, precision=HIGH)

def pick_rows(source, index):
    return source[index]

def pack_forward(params, inputs, positions, segments, onehot, table, target):
    mixer_gain, mixer_shift, project_in, project_out, expert_gain, expert_shift, router_weight, expert_in, expert_out = params
    normed = low(layer_norm(inputs, mixer_gain, mixer_shift))
    joined = low(low_back(jnp.dot(normed, project_in, precision=HIGH)))
    query = joined[:, :D].reshape(CTX, HEADS, HEAD_DIM)
    keys = joined[:, D:2 * D].reshape(CTX, HEADS, HEAD_DIM)
    values = joined[:, 2 * D:].reshape(CTX, HEADS, HEAD_DIM)
    height = math.gcd(CTX, 512)
    blocks = CTX // height
    attend = jax.checkpoint(partial(attend_block, keys=keys, values=values, key_positions=positions, key_segments=segments))
    attended = lax.map(attend, (query.reshape(blocks, height, HEADS, HEAD_DIM), positions.reshape(blocks, height), segments.reshape(blocks, height)))
    mixed = low(low_back(attended.reshape(CTX, D)))
    middle = inputs + jnp.dot(mixed, project_out, precision=HIGH)
    second = low(layer_norm(middle, expert_gain, expert_shift))
    shares = jax.nn.softmax(jnp.dot(second, router_weight, precision=HIGH), axis=-1)
    gate = lax.optimization_barrier(jnp.sum(shares * onehot, axis=-1, keepdims=True))
    padded = jnp.concatenate([second.reshape(N_CONTEXT, TOK_MB, D), jnp.zeros((N_CONTEXT, 1, D), jnp.float32)], axis=1)
    sent = low_back(jax.vmap(pick_rows)(padded, table))
    sent = sent.reshape(N_CONTEXT, EXPERTS, CAP, D).transpose(1, 0, 2, 3).reshape(EXPERTS, N_CONTEXT * CAP, D)
    inner = low_back(jnp.einsum('erd,edf->erf', sent, expert_in, precision=HIGH))
    active = low(jax.nn.gelu(inner, approximate=True))
    result = low(low_back(jnp.einsum('erf,efd->erd', active, expert_out, precision=HIGH)))
    result = result.reshape(EXPERTS, N_CONTEXT, CAP, D).transpose(1, 0, 2, 3).reshape(N_CONTEXT, EXPERTS * CAP, D)
    picked = jax.vmap(pick_rows)(result, target).reshape(CTX, D)
    return middle + gate * picked

def route_tables(route):
    onehot = (route[:, None] == jnp.arange(EXPERTS, dtype=jnp.int32)[None, :]).astype(jnp.int32)
    blocked = onehot.reshape(N_CONTEXT, TOK_MB, EXPERTS)
    earlier = jnp.cumsum(blocked, axis=1).astype(jnp.int32) - blocked
    slot = lax.optimization_barrier(jnp.sum(earlier * blocked, axis=2)).astype(jnp.int32)
    target = (route.reshape(N_CONTEXT, TOK_MB) * CAP + slot).astype(jnp.int32)
    table = jnp.full((N_CONTEXT, EXPERTS * CAP), TOK_MB, jnp.int32)
    rows_of = jnp.broadcast_to(jnp.arange(TOK_MB, dtype=jnp.int32)[None, :], (N_CONTEXT, TOK_MB))
    table = table.at[jnp.arange(N_CONTEXT, dtype=jnp.int32)[:, None], target].set(rows_of)
    return (onehot.astype(jnp.float32), table, target)

def reference(tokens, out_grad, seq_lengths, token_order, expert_route, mixer_gain, mixer_shift, project_in, project_out, expert_gain, expert_shift, router_weight, expert_in, expert_out):
    params = tuple((weight.astype(jnp.float32) for weight in (mixer_gain, mixer_shift, project_in, project_out, expert_gain, expert_shift, router_weight, expert_in, expert_out)))
    inputs = tokens.astype(jnp.float32).reshape(MB * PACKS, CTX, D)
    cotangents = out_grad.astype(jnp.float32).reshape(MB * PACKS, CTX, D)
    lengths = seq_lengths.reshape(MB * PACKS, NSEQ)
    orders = token_order.reshape(MB * PACKS, CTX)
    routes = expert_route.reshape(MB * PACKS, CTX)

    def one_pack(totals, pack):
        values, cotangent, length_row, order, route = pack
        ends = jnp.cumsum(length_row).astype(jnp.int32)
        segments = lax.optimization_barrier(jnp.sum((order[:, None] >= ends[None, :]).astype(jnp.int32), axis=1)).astype(jnp.int32)
        onehot, table, target = route_tables(route)
        forward = partial(pack_forward, positions=order, segments=segments, onehot=onehot, table=table, target=target)
        output, pullback = jax.vjp(forward, params, values)
        weight_grads, input_grads = pullback(cotangent)
        return (jax.tree.map(jnp.add, totals, weight_grads), (output.astype(jnp.bfloat16), input_grads))
    totals, (outputs, input_grads) = lax.scan(one_pack, jax.tree.map(jnp.zeros_like, params), (inputs, cotangents, lengths, orders, routes))
    return (outputs.reshape(MB, PACKS, CTX, D), input_grads.reshape(MB, PACKS, CTX, D), totals[0], totals[1], totals[2], totals[3], totals[4], totals[5], totals[6], totals[7], totals[8])
```

```python
from functools import partial

import jax
import jax.numpy as jnp
from jax import lax
from jax.sharding import PartitionSpec as P
from jax.experimental import pallas as pl
from jax.experimental.pallas import tpu as pltpu
bf=jnp.bfloat16; f32=jnp.float32
NT=(((1,),(1,)),((),()))
TN=(((0,),(0,)),((),()))
NN=(((1,),(0,)),((),()))
def mm(a,b,dims): return lax.dot_general(a,b,dims,preferred_element_type=f32)

def fwd_body(rb, bias_ref, q_ref, ko_ref, vo_ref, kx_ref, vx_ref, o_ref, ol_ref, lse_ref):
    i=pl.program_id(0)
    rows=q_ref.shape[0]
    lane=lax.broadcasted_iota(jnp.int32,(1,128),1)
    masks=[(lane<64).astype(bf)*0.125,(lane>=64).astype(bf)*0.125]
    ko=ko_ref[...]; vo=vo_ref[...]; kx=kx_ref[...]; vx=vx_ref[...]
    for r in range(0,rows,rb):
        q=q_ref[r:r+rb,:]
        bo=bias_ref[r:r+rb,:rows]; bx=bias_ref[r:r+rb,rows:]
        outs=[]
        old=lse_ref[r:r+rb,:]
        for j in range(2):
            qj=q*masks[j]
            so=mm(qj,ko,NT)+bo
            sx=mm(qj,kx,NT)+bx
            m=jnp.maximum(jnp.max(so,-1,keepdims=True),jnp.max(sx,-1,keepdims=True))
            po=jnp.exp(so-m); px=jnp.exp(sx-m)
            l=jnp.sum(po,-1,keepdims=True)+jnp.sum(px,-1,keepdims=True)
            w=mm(po.astype(bf),vo,NN)+mm(px.astype(bf),vx,NN)
            outs.append(w/l)
            old=jnp.where(lane==2*i+j,m+jnp.log(l),old)
        lse_ref[r:r+rb,:]=old
        o=jnp.where(lane<64,outs[0],outs[1])
        o_ref[r:r+rb,:]=o
        ol_ref[r:r+rb,:]=o.astype(bf)

def attn_fwd(joined, other, bias, mb, rb=None):
    rows=bias.shape[0]; nx=other.shape[0]; D=other.shape[1]//2; G=D//128
    flops=4*rows*(rows+nx)*D
    rb=rb or rows
    return pl.pallas_call(partial(fwd_body,rb),
        grid=(G,),
        in_specs=[pl.BlockSpec(bias.shape,lambda i:(0,0)),
            pl.BlockSpec((rows,128),lambda i:(mb,i)),
            pl.BlockSpec((rows,128),lambda i:(mb,G+i)),
            pl.BlockSpec((rows,128),lambda i:(mb,2*G+i)),
            pl.BlockSpec((nx,128),lambda i:(0,i)),
            pl.BlockSpec((nx,128),lambda i:(0,G+i))],
        out_specs=[pl.BlockSpec((rows,128),lambda i:(0,i)),pl.BlockSpec((rows,128),lambda i:(0,i)),pl.BlockSpec((rows,128),lambda i:(0,0))],
        out_shape=[jax.ShapeDtypeStruct((rows,D),f32),jax.ShapeDtypeStruct((rows,D),bf),jax.ShapeDtypeStruct((rows,128),f32)],
        cost_estimate=pl.CostEstimate(flops=flops*4,transcendentals=16*rows*(rows+nx),bytes_accessed=rows*D*16),
        name="attn_fwd")(bias,joined,joined,joined,other,other)

def bwd_body(kb, biast_ref, lse_ref, q_ref, ko_ref, vo_ref, kx_ref, vx_ref, do_ref, o_ref, dq_ref, dko_ref, dx_ref):
    i=pl.program_id(0)
    rows=q_ref.shape[0]; nx=kx_ref.shape[0]
    lane=lax.broadcasted_iota(jnp.int32,(1,128),1)
    masks=[(lane<64).astype(bf),(lane>=64).astype(bf)]
    q=q_ref[...]; do=do_ref[...]
    prod=do.astype(f32)*o_ref[...]
    qs=[q*(m*0.125) for m in masks]; dos=[do*m for m in masks]
    sel=(lax.broadcasted_iota(jnp.int32,(8,128),1)//64==lax.broadcasted_iota(jnp.int32,(8,128),0)).astype(f32)
    delta=lax.dot_general(sel,prod,NT,precision=lax.Precision.HIGHEST,preferred_element_type=f32)
    lses=[lse_ref[pl.ds(2*i+j,1),:] for j in range(2)]
    dq=[None,None]
    for (kr,vr,base,cnt,own) in ((ko_ref,vo_ref,0,rows,True),(kx_ref,vx_ref,rows,nx,False)):
        for b in range(0,cnt,kb):
            k=kr[b:b+kb,:]; v=vr[b:b+kb,:]
            bt=biast_ref[base+b:base+b+kb,:]
            dk=dv=None
            for j in range(2):
                s=mm(k,qs[j],NT)+bt
                p=jnp.exp(s-lses[j])
                dp=mm(v,dos[j],NT)
                ds=(p*(dp-delta[j:j+1,:])).astype(bf)
                a=mm(p.astype(bf),dos[j],NN); c=mm(ds,qs[j],NN)
                dv=a if dv is None else dv+a
                dk=c if dk is None else dk+c
                e=mm(ds,k,TN)
                dq[j]=e if dq[j] is None else dq[j]+e
            if own:
                dko_ref[0,b:b+kb,:]=dk; dko_ref[1,b:b+kb,:]=dv
            else:
                dx_ref[0,b:b+kb,:]=dk.astype(bf); dx_ref[1,b:b+kb,:]=dv.astype(bf)
    dq_ref[...]=(jnp.where(lane<64,dq[0],dq[1])*0.125).astype(bf)

def attn_bwd(joined, other, biast, lset, do, o, mb, kb=None):
    rows=biast.shape[1]; nx=other.shape[0]; D=other.shape[1]//2; G=D//128
    flops=10*rows*(rows+nx)*D
    kb=kb or rows
    return pl.pallas_call(partial(bwd_body,kb),
        grid=(G,),
        in_specs=[pl.BlockSpec(biast.shape,lambda i:(0,0)),
            pl.BlockSpec(lset.shape,lambda i:(0,0)),
            pl.BlockSpec((rows,128),lambda i:(mb,i)),
            pl.BlockSpec((rows,128),lambda i:(mb,G+i)),
            pl.BlockSpec((rows,128),lambda i:(mb,2*G+i)),
            pl.BlockSpec((nx,128),lambda i:(0,i)),
            pl.BlockSpec((nx,128),lambda i:(0,G+i)),
            pl.BlockSpec((rows,128),lambda i:(0,i)),
            pl.BlockSpec((rows,128),lambda i:(0,i))],
        out_specs=[pl.BlockSpec((rows,128),lambda i:(0,i)),pl.BlockSpec((2,rows,128),lambda i:(0,0,i)),pl.BlockSpec((2,nx,128),lambda i:(0,0,i))],
        out_shape=[jax.ShapeDtypeStruct((rows,D),bf),jax.ShapeDtypeStruct((2,rows,D),f32),jax.ShapeDtypeStruct((2,nx,D),bf)],
        cost_estimate=pl.CostEstimate(flops=flops*4,transcendentals=16*rows*(rows+nx),bytes_accessed=rows*D*30),
        name="attn_bwd")(biast,lset,joined,joined,joined,other,other,do,o)

C0=0.7978845608028654; C1=0.044715
def exp_body(x_ref, g_ref, wi_ref, wo_ref, *refs):
    act_ref, ig_ref, b_ref, accr, accd = refs[-5:]
    f=pl.program_id(0)
    x=x_ref[...]; g=g_ref[...]; wi=wi_ref[...]; wo=wo_ref[...]
    v=mm(x,wi,NN)
    ag=mm(g,wo,NT)
    v2=v*v
    t=jnp.tanh(C0*(v*(1.0+C1*v2)))
    h=0.5*(1.0+t)
    act=(v*h).astype(bf)
    dg=h+(0.5*C0)*v*(1.0-t*t)*(1.0+(3*C1)*v2)
    ig=(ag*dg).astype(bf)
    act_ref[...]=act; ig_ref[...]=ig
    r=mm(act,wo,NN); d=mm(ig,wi,NT)
    @pl.when(f==0)
    def _(): accr[...]=r; accd[...]=d
    @pl.when(f>0)
    def _(): accr[...]+=r; accd[...]+=d
    @pl.when(f==pl.num_programs(0)-1)
    def _():
        size=b_ref.shape[1]//2
        for e in range(b_ref.shape[0]):
            b_ref[e,:size,:]=accr[e*size:(e+1)*size,:].astype(bf)
            b_ref[e,size:,:]=accd[e*size:(e+1)*size,:].astype(bf)

def expert(x, g, wi, wo, prev, mb, nmb, experts, fb=512):
    rows,D=x.shape; FF=wi.shape[1]
    blk=pl.BlockSpec((rows,fb),lambda f:(mb,f))
    anyspec=pl.BlockSpec(memory_space=pl.ANY)
    ex=() if prev is None else prev
    return pl.pallas_call(exp_body, grid=(FF//fb,),
        in_specs=[pl.BlockSpec((rows,D),lambda f:(0,0)),pl.BlockSpec((rows,D),lambda f:(0,0)),
                  pl.BlockSpec((D,fb),lambda f:(0,f)),pl.BlockSpec((fb,D),lambda f:(f,0))]+[anyspec]*len(ex),
        out_specs=[blk,blk,pl.BlockSpec((experts,2*rows//experts,D),lambda f:(0,0,0))],
        out_shape=[jax.ShapeDtypeStruct((nmb*rows,FF),bf)]*2+[jax.ShapeDtypeStruct((experts,2*rows//experts,D),bf)],
        scratch_shapes=[pltpu.VMEM((rows,D),f32)]*2,
        input_output_aliases={} if prev is None else {4:0,5:1},
        cost_estimate=pl.CostEstimate(flops=8*rows*D*FF,transcendentals=rows*FF,bytes_accessed=4*D*FF+4*rows*FF),
        name="expert")(x,g,wi,wo,*ex)

def merge_body(count, dq_ref, own_ref, *refs):
    j=pl.program_id(0); out_ref=refs[-1]
    @pl.when(j==0)
    def _(): out_ref[...]=dq_ref[...]
    @pl.when(j>0)
    def _():
        total=own_ref[0]
        for r in refs[:count]: total=total+r[0].astype(f32)
        out_ref[...]=total.astype(bf)

def merge(dq, own, parts, prev, mb, nmb):
    rows,D=dq.shape
    three=pl.BlockSpec((1,rows,D),lambda j:(jnp.maximum(j-1,0),0,0))
    ex=[] if prev is None else [prev]
    return pl.pallas_call(partial(merge_body,len(parts)), grid=(3,),
        in_specs=[pl.BlockSpec((rows,D),lambda j:(0,0)),three]+[three]*len(parts)+[pl.BlockSpec(memory_space=pl.ANY)]*len(ex),
        out_specs=pl.BlockSpec((rows,D),lambda j:(mb,j)),
        out_shape=jax.ShapeDtypeStruct((nmb*rows,3*D),bf),
        input_output_aliases={} if prev is None else {2+len(parts):0},
        cost_estimate=pl.CostEstimate(flops=rows*D*4,transcendentals=0,bytes_accessed=rows*D*22),
        name="merge")(dq,own,*parts,*ex)


HEADS = 16
EPS = 1e-05
HIGH = lax.Precision.HIGHEST


def layer_norm(values, gain, shift):
    center = values - jnp.mean(values, axis=-1, keepdims=True)
    scale = lax.rsqrt(jnp.mean(center * center, axis=-1, keepdims=True) + EPS)
    normal = center * scale
    return (normal * gain + shift, normal, scale)


def norm_back(grad, normal, scale, gain):
    scaled = grad * gain
    inner = (
        scaled
        - jnp.mean(scaled, axis=-1, keepdims=True)
        - normal * jnp.mean(scaled * normal, axis=-1, keepdims=True)
    )
    return (inner * scale, jnp.sum(grad * normal, axis=0), jnp.sum(grad, axis=0))


def swap(values, axis, bit):
    return lax.ppermute(values, axis, [(i, i ^ bit) for i in range(lax.axis_size(axis))])


def bits_of(axis):
    count = lax.axis_size(axis)
    assert count & (count - 1) == 0
    return [(axis, 1 << i) for i in range(count.bit_length() - 1)]


def halve(values, steps, slot):
    sent, kept = [], []
    for value, order in zip(values, steps):
        axis, bit = order[slot]
        high = (lax.axis_index(axis) // bit) % 2
        half = value.shape[0] // 2
        part = lax.dynamic_slice_in_dim(value, (1 - high) * half, half)
        kept.append(lax.dynamic_slice_in_dim(value, high * half, half))
        sent.append(swap(part, axis, bit))
    return [a + b for a, b in zip(kept, sent)]


def double(values, steps, slot):
    sent = [swap(value, *order[slot]) for value, order in zip(values, steps)]
    joined = []
    for value, other, order in zip(values, sent, steps):
        axis, bit = order[slot]
        high = (lax.axis_index(axis) // bit) % 2
        joined.append(
            jnp.concatenate(
                [jnp.where(high == 0, value, other), jnp.where(high == 0, other, value)], axis=0
            )
        )
    return joined


def sum_everywhere(whole, widths, held=()):
    near = bits_of("context")
    for slot in range(len(near)):
        whole = halve([whole], [near], slot)[0]
    chunks, start = [], 0
    for width in widths:
        chunks.append(whole[:, start : start + width])
        start += width
    expert = bits_of("expert")
    orders = [
        expert[:1] + bits_of("dp") + expert[1:],
        bits_of("dp") + expert,
        expert[1:] + expert[:1] + bits_of("dp"),
    ][: len(widths)]
    count = len(orders[0])
    for slot in range(count):
        chunks = list(lax.optimization_barrier(tuple(halve(chunks, orders, slot))))
    for slot in reversed(range(count)):
        chunks = list(lax.optimization_barrier(tuple(double(chunks, orders, slot))))
        if slot == 1 and held:
            held = tuple(h.astype(f32) for h in held)
            chunks, held = lax.optimization_barrier((chunks, held))
    whole = chunks[0] if len(chunks) == 1 else jnp.concatenate(chunks, axis=1)
    for slot in reversed(range(len(near))):
        whole = double([whole], [near], slot)[0]
    return whole, held


def sum_small(values):
    for axis in ("context", "dp", "expert"):
        for _, bit in bits_of(axis):
            values = values + swap(values, axis, bit)
    return values


def local(
    tokens,
    out_grad,
    seq_lengths,
    token_order,
    expert_route,
    mixer_gain,
    mixer_shift,
    project_in,
    project_out,
    expert_gain,
    expert_shift,
    router_weight,
    expert_in,
    expert_out,
):
    micro, rows, model = tokens.shape[0], tokens.shape[2], tokens.shape[3]
    contexts = lax.axis_size("context")
    here = lax.axis_index("context")
    experts = expert_in.shape[0] * lax.axis_size("expert")
    capacity = 9 * rows // (8 * experts)
    block = (capacity + 2 + 7) // 8 * 8
    slots = experts * block

    full_in = lax.all_gather(expert_in[0], ("context", "dp"), axis=0, tiled=True)
    full_out = lax.all_gather(expert_out[0], ("context", "dp"), axis=0, tiled=True)

    router_float = router_weight.astype(f32)
    expert_ids = jnp.arange(experts, dtype=jnp.int32)
    slot_ids = jnp.arange(slots, dtype=jnp.int32)

    routes, ranks, places, place_two = [], [], [], []
    sent_grads = []
    for m in range(micro):
        route = expert_route[m, 0, :, 0]
        choose_int = (route[:, None] == expert_ids[None, :]).astype(jnp.int32)
        earlier = jnp.cumsum(choose_int, axis=0) - choose_int
        rank = jnp.sum(earlier * choose_int, axis=1)
        place = (route * block + rank)[None, :] == slot_ids[:, None]
        routes.append(route)
        ranks.append(rank)
        places.append(place.astype(bf))
        target = (route * (2 * block) + rank)[None, :]
        wide = jnp.arange(2 * slots, dtype=jnp.int32)[:, None]
        place_two.append(((target == wide).astype(bf), (target + block == wide).astype(bf)))
        sent_grads.append(
            jnp.dot(places[m], out_grad[m, 0], preferred_element_type=f32)
            .astype(bf)
            .reshape(experts, 1, block, model)
        )
    sent_grads, tokens = lax.optimization_barrier((jnp.concatenate(sent_grads, axis=1), tokens))
    grads_there = lax.all_to_all(sent_grads, "expert", split_axis=0, concat_axis=0, tiled=True)

    flat = tokens.reshape(micro * rows, model).astype(f32)
    normed, normal_one, scale_one = layer_norm(flat, mixer_gain, mixer_shift)
    normed_low = lax.optimization_barrier(normed.astype(bf))
    joined = jnp.dot(normed_low, project_in, preferred_element_type=f32).astype(bf)
    others, biases = [], []
    for m in range(micro):
        pairs = joined[m * rows : (m + 1) * rows, model:]
        parts = [
            lax.ppermute(pairs, "context", [(i, (i + s) % contexts) for i in range(contexts)])
            for s in range(1, contexts)
        ]
        others.append(parts[0] if contexts == 2 else jnp.concatenate(parts, axis=0))
        positions = token_order[m, 0]
        ends = jnp.cumsum(seq_lengths[m, 0])
        segments = jnp.sum((positions[:, None] >= ends[None, :]).astype(jnp.int32), axis=1)
        owners = [(here - s + contexts) % contexts for s in range(contexts)]
        key_positions = jnp.concatenate(
            [lax.dynamic_slice_in_dim(positions, o * rows, rows) for o in owners]
        )
        key_segments = jnp.concatenate(
            [lax.dynamic_slice_in_dim(segments, o * rows, rows) for o in owners]
        )
        query_positions, query_segments = key_positions[:rows], key_segments[:rows]
        biases.append(
            (
                jnp.where(
                    (key_positions[None, :] <= query_positions[:, None])
                    & (key_segments[None, :] == query_segments[:, None]),
                    0.0,
                    -1e30,
                ).astype(f32),
                jnp.where(
                    (key_positions[:, None] <= query_positions[None, :])
                    & (key_segments[:, None] == query_segments[None, :]),
                    0.0,
                    -1e30,
                ).astype(f32),
            )
        )

    saved = []
    before = grads_there
    for m in range(micro):
        attended, mixed_low, lse = attn_fwd(joined, others[m], biases[m][0], m)
        log_total = lse[:, :HEADS].T
        middle = flat[m * rows : (m + 1) * rows] + jnp.dot(
            mixed_low, project_out, preferred_element_type=f32
        )
        second, normal_two, scale_two = layer_norm(middle, expert_gain, expert_shift)
        second_low = second.astype(bf)
        shares = jax.nn.softmax(
            jnp.dot(second_low, router_weight, preferred_element_type=f32), axis=-1
        )
        choose_float = (routes[m][:, None] == expert_ids[None, :]).astype(f32)
        gate = jnp.sum(shares * choose_float, axis=1)
        gate_high = gate.astype(bf)
        gate_low = (gate - gate_high.astype(f32)).astype(bf)
        slot_expert, slot_row = slot_ids // block, slot_ids % block
        mine = slot_expert[:, None] == routes[m][None, :]
        gates = jnp.where(
            mine & (slot_row == capacity)[:, None],
            gate_high[None, :],
            jnp.where(mine & (slot_row == capacity + 1)[:, None], gate_low[None, :], jnp.zeros((), bf)),
        )
        ladder = (ranks[m][:, None] == jnp.arange(model, dtype=jnp.int32)[None, :]).astype(bf)
        sent = jnp.dot(
            jnp.concatenate([places[m], gates], axis=1),
            jnp.concatenate([second_low, ladder], axis=0),
            preferred_element_type=f32,
        ).astype(bf)
        if m + 1 < micro:
            sent, others[m + 1] = lax.optimization_barrier((sent, others[m + 1]))
        sent, before = lax.optimization_barrier((sent, before))
        if m == 0:
            grads_there = before
        else:
            saved[m - 1][-1] = before
        there = lax.all_to_all(
            sent.reshape(experts, block, model), "expert", split_axis=0, concat_axis=0, tiled=True
        )
        before = there
        saved.append(
            [attended, mixed_low, log_total, middle, second_low, normal_two, scale_two, shares,
             choose_float, gate, there]
        )

    whole = lax.optimization_barrier(tuple(state[-1] for state in saved))
    for m in range(micro):
        saved[m][-1] = whole[m]
    kept = None
    rows_there, scaled_there, returned = [], [], []
    for m in range(micro):
        there = saved[m][-1]
        gate_there = there[:, capacity, :block].astype(f32) + there[:, capacity + 1, :block].astype(f32)
        scaled = (gate_there[:, :, None] * grads_there[:, m].astype(f32)).astype(bf)
        there = there.reshape(slots, model)
        scaled = scaled.reshape(slots, model)
        active, inner_grad, back = expert(
            there, scaled, full_in, full_out, kept, m, micro, experts
        )
        if m + 1 < micro:
            back, saved[m + 1][-1] = lax.optimization_barrier((back, saved[m + 1][-1]))
        kept = (active, inner_grad)
        rows_there.append(there)
        scaled_there.append(scaled)
        returned.append(
            lax.all_to_all(back, "expert", split_axis=0, concat_axis=0, tiled=True).reshape(
                2 * slots, model
            )
        )
    active, inner_grad = kept
    rows_there = jnp.concatenate(rows_there, axis=0)
    scaled_there = jnp.concatenate(scaled_there, axis=0)
    in_term = lax.dot_general(rows_there, inner_grad, TN, preferred_element_type=f32).astype(bf)
    out_term = lax.dot_general(active, scaled_there, TN, preferred_element_type=f32).astype(bf)
    in_term, out_term, returned[0] = lax.optimization_barrier((in_term, out_term, returned[0]))
    grad_in = lax.psum_scatter(in_term, ("context", "dp"), scatter_dimension=0, tiled=True)
    grad_out_weight = lax.psum_scatter(out_term, ("context", "dp"), scatter_dimension=0, tiled=True)

    outputs, middle_grads, branches, joined_grad = [], [], [], None
    small = None
    for m in range(micro):
        (attended, mixed_low, log_total, middle, second_low, normal_two, scale_two, shares,
         choose_float, gate, _) = saved[m]
        grad_out = out_grad[m, 0].astype(f32)
        picked = lax.dot_general(place_two[m][0], returned[m], TN, preferred_element_type=f32)
        outputs.append((middle + gate[:, None] * picked).astype(bf))
        gate_grad = jnp.sum(grad_out * picked, axis=1)
        logit_grad = gate_grad[:, None] * gate[:, None] * (choose_float - shares)
        router_term = jnp.einsum("td,te->de", second_low.astype(f32), logit_grad, precision=HIGH)
        second_grad = jnp.einsum("te,de->td", logit_grad, router_float, precision=HIGH)
        second_grad = second_grad + lax.dot_general(
            place_two[m][1], returned[m], TN, preferred_element_type=f32
        )
        middle_part, gain_two, shift_two = norm_back(second_grad, normal_two, scale_two, expert_gain)
        middle_grad = grad_out + middle_part
        branch = middle_grad.astype(bf)
        mixed_grad = lax.dot_general(branch, project_out, NT, preferred_element_type=f32).astype(bf)
        query_grad, own, away = attn_bwd(
            joined, others[m], biases[m][1], log_total, mixed_grad, attended, m
        )
        if m + 1 < micro:
            own, away, returned[m + 1] = lax.optimization_barrier((own, away, returned[m + 1]))
        parts = [
            lax.ppermute(
                away[:, (s - 1) * rows : s * rows] if contexts > 2 else away,
                "context",
                [(i, (i - s) % contexts) for i in range(contexts)],
            )
            for s in range(1, contexts)
        ]
        joined_grad = merge(query_grad, own, parts, joined_grad, m, micro)
        middle_grads.append(middle_grad)
        branches.append(branch)
        terms = (gain_two, shift_two, router_term)
        small = terms if small is None else tuple(a + b for a, b in zip(small, terms))

    mixed_all = jnp.concatenate([s[1] for s in saved], axis=0)
    out_sum = lax.dot_general(
        mixed_all, jnp.concatenate(branches, axis=0), TN, preferred_element_type=f32
    ).astype(bf)
    out_sum, _ = sum_everywhere(out_sum, (model // 2, model // 2))

    in_sum = lax.dot_general(normed_low, joined_grad, TN, preferred_element_type=f32).astype(bf)
    in_sum, joined_grad = lax.optimization_barrier((in_sum, joined_grad))
    third = 3 * model // 6
    in_sum, (grad_in, grad_out_weight) = sum_everywhere(
        in_sum,
        ((3 * model - third) // 2, (3 * model - third) // 2, third),
        (grad_in, grad_out_weight),
    )
    normed_grad = lax.dot_general(joined_grad, project_in, NT, preferred_element_type=f32)
    input_part, gain_one, shift_one = norm_back(normed_grad, normal_one, scale_one, mixer_gain)
    grad_tokens = jnp.concatenate(middle_grads, axis=0) + input_part
    small = jnp.concatenate(
        [gain_one[None], shift_one[None], small[0][None], small[1][None], small[2].T], axis=0
    )
    small = sum_small(small)
    return (
        jnp.stack(outputs)[:, None],
        grad_tokens.reshape(micro, 1, rows, model),
        small[0],
        small[1],
        in_sum.astype(f32),
        out_sum.astype(f32),
        small[2],
        small[3],
        small[4:].T,
        grad_in[None],
        grad_out_weight[None],
    )


def solution(mesh):
    tokens = P(None, ("expert", "dp"), "context", None)
    packs = P(None, ("expert", "dp"), None)
    weights = P("expert", ("context", "dp"), None)
    in_specs = (tokens, tokens, packs, packs, tokens) + (P(),) * 7 + (weights, weights)
    out_specs = (tokens, tokens) + (P(),) * 7 + (weights, weights)
    return jax.shard_map(local, mesh=mesh, in_specs=in_specs, out_specs=out_specs, check_vma=False)
```

```python
from functools import partial

import jax
import jax.numpy as jnp
from jax import lax
from jax.sharding import PartitionSpec as P
from jax.experimental import pallas as pl
from jax.experimental.pallas import tpu as pltpu
bf=jnp.bfloat16; f32=jnp.float32
NT=(((1,),(1,)),((),()))
TN=(((0,),(0,)),((),()))
NN=(((1,),(0,)),((),()))
def mm(a,b,dims): return lax.dot_general(a,b,dims,preferred_element_type=f32)

def fwd_body(rb, bias_ref, q_ref, ko_ref, vo_ref, kx_ref, vx_ref, o_ref, ol_ref, lse_ref):
    i=pl.program_id(0)
    rows=q_ref.shape[0]
    lane=lax.broadcasted_iota(jnp.int32,(1,128),1)
    masks=[(lane<64).astype(bf)*0.125,(lane>=64).astype(bf)*0.125]
    ko=ko_ref[...]; vo=vo_ref[...]; kx=kx_ref[...]; vx=vx_ref[...]
    for r in range(0,rows,rb):
        q=q_ref[r:r+rb,:]
        bo=bias_ref[r:r+rb,:rows]; bx=bias_ref[r:r+rb,rows:]
        outs=[]
        old=lse_ref[r:r+rb,:]
        for j in range(2):
            qj=q*masks[j]
            so=mm(qj,ko,NT)+bo
            sx=mm(qj,kx,NT)+bx
            m=jnp.maximum(jnp.max(so,-1,keepdims=True),jnp.max(sx,-1,keepdims=True))
            po=jnp.exp(so-m); px=jnp.exp(sx-m)
            l=jnp.sum(po,-1,keepdims=True)+jnp.sum(px,-1,keepdims=True)
            w=mm(po.astype(bf),vo,NN)+mm(px.astype(bf),vx,NN)
            outs.append(w/l)
            old=jnp.where(lane==2*i+j,m+jnp.log(l),old)
        lse_ref[r:r+rb,:]=old
        o=jnp.where(lane<64,outs[0],outs[1])
        o_ref[r:r+rb,:]=o
        ol_ref[r:r+rb,:]=o.astype(bf)

def attn_fwd(joined, other, bias, mb, rb=None):
    rows=bias.shape[0]; nx=other.shape[0]; D=other.shape[1]//2; G=D//128
    flops=4*rows*(rows+nx)*D
    rb=rb or rows
    return pl.pallas_call(partial(fwd_body,rb),
        grid=(G,),
        in_specs=[pl.BlockSpec(bias.shape,lambda i:(0,0)),
            pl.BlockSpec((rows,128),lambda i:(mb,i)),
            pl.BlockSpec((rows,128),lambda i:(mb,G+i)),
            pl.BlockSpec((rows,128),lambda i:(mb,2*G+i)),
            pl.BlockSpec((nx,128),lambda i:(0,i)),
            pl.BlockSpec((nx,128),lambda i:(0,G+i))],
        out_specs=[pl.BlockSpec((rows,128),lambda i:(0,i)),pl.BlockSpec((rows,128),lambda i:(0,i)),pl.BlockSpec((rows,128),lambda i:(0,0))],
        out_shape=[jax.ShapeDtypeStruct((rows,D),f32),jax.ShapeDtypeStruct((rows,D),bf),jax.ShapeDtypeStruct((rows,128),f32)],
        cost_estimate=pl.CostEstimate(flops=rows,transcendentals=0,bytes_accessed=rows),
        name="attn_fwd")(bias,joined,joined,joined,other,other)

def bwd_body(kb, biast_ref, lse_ref, q_ref, ko_ref, vo_ref, kx_ref, vx_ref, do_ref, o_ref, dq_ref, dko_ref, dx_ref):
    i=pl.program_id(0)
    rows=q_ref.shape[0]; nx=kx_ref.shape[0]
    lane=lax.broadcasted_iota(jnp.int32,(1,128),1)
    masks=[(lane<64).astype(bf),(lane>=64).astype(bf)]
    q=q_ref[...]; do=do_ref[...]
    prod=do.astype(f32)*o_ref[...]
    qs=[q*(m*0.125) for m in masks]; dos=[do*m for m in masks]
    sel=(lax.broadcasted_iota(jnp.int32,(8,128),1)//64==lax.broadcasted_iota(jnp.int32,(8,128),0)).astype(f32)
    delta=lax.dot_general(sel,prod,NT,precision=lax.Precision.HIGHEST,preferred_element_type=f32)
    lses=[lse_ref[pl.ds(2*i+j,1),:] for j in range(2)]
    dq=[None,None]
    for (kr,vr,base,cnt,own) in ((ko_ref,vo_ref,0,rows,True),(kx_ref,vx_ref,rows,nx,False)):
        for b in range(0,cnt,kb):
            k=kr[b:b+kb,:]; v=vr[b:b+kb,:]
            bt=biast_ref[base+b:base+b+kb,:]
            dk=dv=None
            for j in range(2):
                s=mm(k,qs[j],NT)+bt
                p=jnp.exp(s-lses[j])
                dp=mm(v,dos[j],NT)
                ds=(p*(dp-delta[j:j+1,:])).astype(bf)
                a=mm(p.astype(bf),dos[j],NN); c=mm(ds,qs[j],NN)
                dv=a if dv is None else dv+a
                dk=c if dk is None else dk+c
                e=mm(ds,k,TN)
                dq[j]=e if dq[j] is None else dq[j]+e
            if own:
                dko_ref[0,b:b+kb,:]=dk.astype(bf); dko_ref[1,b:b+kb,:]=dv.astype(bf)
            else:
                dx_ref[0,b:b+kb,:]=dk.astype(bf); dx_ref[1,b:b+kb,:]=dv.astype(bf)
    dq_ref[...]=(jnp.where(lane<64,dq[0],dq[1])*0.125).astype(bf)

def attn_bwd(joined, other, biast, lset, do, o, mb, kb=None):
    rows=biast.shape[1]; nx=other.shape[0]; D=other.shape[1]//2; G=D//128
    flops=10*rows*(rows+nx)*D
    kb=kb or rows
    return pl.pallas_call(partial(bwd_body,kb),
        grid=(G,),
        in_specs=[pl.BlockSpec(biast.shape,lambda i:(0,0)),
            pl.BlockSpec(lset.shape,lambda i:(0,0)),
            pl.BlockSpec((rows,128),lambda i:(mb,i)),
            pl.BlockSpec((rows,128),lambda i:(mb,G+i)),
            pl.BlockSpec((rows,128),lambda i:(mb,2*G+i)),
            pl.BlockSpec((nx,128),lambda i:(0,i)),
            pl.BlockSpec((nx,128),lambda i:(0,G+i)),
            pl.BlockSpec((rows,128),lambda i:(0,i)),
            pl.BlockSpec((rows,128),lambda i:(0,i))],
        out_specs=[pl.BlockSpec((rows,128),lambda i:(0,i)),pl.BlockSpec((2,rows,128),lambda i:(0,0,i)),pl.BlockSpec((2,nx,128),lambda i:(0,0,i))],
        out_shape=[jax.ShapeDtypeStruct((rows,D),bf),jax.ShapeDtypeStruct((2,rows,D),bf),jax.ShapeDtypeStruct((2,nx,D),bf)],
        cost_estimate=pl.CostEstimate(flops=flops*4,transcendentals=16*rows*(rows+nx),bytes_accessed=rows*D*30),
        name="attn_bwd")(biast,lset,joined,joined,joined,other,other,do,o)

C0=0.7978845608028654; C1=0.044715
def exp_body(x_ref, g_ref, wi_ref, wo_ref, *refs):
    act_ref, ig_ref, b_ref, accr, accd = refs[-5:]
    f=pl.program_id(0)
    x=x_ref[...]; g=g_ref[...]; wi=wi_ref[...].reshape(x_ref.shape[1],wi_ref.shape[3]); wo=wo_ref[0,0]
    v=mm(x,wi,NN)
    ag=mm(g,wo,NT)
    v2=v*v
    t=jnp.tanh(C0*(v*(1.0+C1*v2)))
    h=0.5*(1.0+t)
    act=(v*h).astype(bf)
    dg=h+(0.5*C0)*v*(1.0-t*t)*(1.0+(3*C1)*v2)
    ig=(ag*dg).astype(bf)
    act_ref[...]=act; ig_ref[...]=ig
    r=mm(act,wo,NN); d=mm(ig,wi,NT)
    @pl.when(f==0)
    def _(): accr[...]=r; accd[...]=d
    @pl.when(f>0)
    def _(): accr[...]+=r; accd[...]+=d
    @pl.when(f==pl.num_programs(0)-1)
    def _():
        size=b_ref.shape[1]//2
        for e in range(b_ref.shape[0]):
            b_ref[e,:size,:]=accr[e*size:(e+1)*size,:].astype(bf)
            b_ref[e,size:,:]=accd[e*size:(e+1)*size,:].astype(bf)

def expert(x, g, weights, prev, mb, nmb, experts, fb=512):
    rows,D=x.shape; n,deep,_=weights.shape; part=deep//2; FF=part*n; per=D//fb
    blk=pl.BlockSpec((rows,fb),lambda f:(mb,f))
    anyspec=pl.BlockSpec(memory_space=pl.ANY)
    ex=() if prev is None else prev
    return pl.pallas_call(exp_body, grid=(FF//fb,),
        in_specs=[pl.BlockSpec((rows,D),lambda f:(0,0)),pl.BlockSpec((rows,D),lambda f:(0,0)),
                  pl.BlockSpec((n,1,D//n,fb),lambda f:(0,f//per,0,f%per)),
                  pl.BlockSpec((1,1,fb,D),lambda f:(f//(part//fb),part//fb+f%(part//fb),0,0))]+[anyspec]*len(ex),
        out_specs=[blk,blk,pl.BlockSpec((experts,2*rows//experts,D),lambda f:(0,0,0))],
        out_shape=[jax.ShapeDtypeStruct((nmb*rows,FF),bf)]*2+[jax.ShapeDtypeStruct((experts,2*rows//experts,D),bf)],
        scratch_shapes=[pltpu.VMEM((rows,D),f32)]*2,
        input_output_aliases={} if prev is None else {4:0,5:1},
        cost_estimate=pl.CostEstimate(flops=8*rows*D*FF,transcendentals=rows*FF,bytes_accessed=4*D*FF+4*rows*FF),
        name="expert")(x,g,weights.reshape(n,2*FF//D,D//n,D),weights.reshape(n,deep//fb,fb,D),*ex)

def in_grads_body(count, *refs):
    in_ref, turned=refs[-2:]; xs=refs[:count]; ig_ref=refs[count]
    n=in_ref.shape[0]; rows,D=xs[0].shape
    @pl.when(pl.program_id(0)==0)
    def _():
        turned[...]=jnp.concatenate([r[...] for r in xs],axis=0).T
    t=mm(turned[...],ig_ref[...],NN).astype(bf)
    for q in range(n): in_ref[q,0,:,:]=t[q*(D//n):(q+1)*(D//n),:]

def in_grads(xs, ig, n, fb=512):
    rows,D=xs[0].shape; FF=ig.shape[1]; per=D//fb; count=len(xs)
    return pl.pallas_call(partial(in_grads_body,count), grid=(FF//fb,),
        in_specs=[pl.BlockSpec((rows,D),lambda f:(0,0))]*count+[pl.BlockSpec((count*rows,fb),lambda f:(0,f))],
        out_specs=pl.BlockSpec((n,1,D//n,fb),lambda f:(0,f//per,0,f%per)),
        out_shape=jax.ShapeDtypeStruct((n,FF//D,D//n,D),bf),
        scratch_shapes=[pltpu.VMEM((D,count*rows),bf)],
        cost_estimate=pl.CostEstimate(flops=2*count*rows*D*FF,transcendentals=0,bytes_accessed=2*D*FF+2*count*rows*FF),
        name="in_grads")(*xs,ig)

def out_grads_body(count, *refs):
    out_ref, stacked=refs[-2:]; gs=refs[:count]; act_ref=refs[count]; rows=gs[0].shape[0]
    @pl.when(pl.program_id(0)==0)
    def _():
        for m in range(count): stacked[m*rows:(m+1)*rows,:]=gs[m][...]
    out_ref[...]=mm(act_ref[...],stacked[...],TN).astype(bf)

def out_grads(gs, act, fb=512):
    rows,D=gs[0].shape; FF=act.shape[1]; count=len(gs)
    return pl.pallas_call(partial(out_grads_body,count), grid=(FF//fb,),
        in_specs=[pl.BlockSpec((rows,D),lambda f:(0,0))]*count+[pl.BlockSpec((count*rows,fb),lambda f:(0,f))],
        out_specs=pl.BlockSpec((fb,D),lambda f:(f,0)),
        out_shape=jax.ShapeDtypeStruct((FF,D),bf),
        scratch_shapes=[pltpu.VMEM((count*rows,D),bf)],
        cost_estimate=pl.CostEstimate(flops=2*count*rows*D*FF,transcendentals=0,bytes_accessed=2*D*FF+2*count*rows*FF),
        name="out_grads")(*gs,act)

def project_body(count, parts, first, per, high_ref, x_ref, *refs):
    j=pl.program_id(0)
    joined_ref,keep_ref,send_ref,turned=refs[-4:]
    half=keep_ref.shape[0]
    @pl.when(j==0)
    def _(): turned[...]=x_ref[...].T
    rows=x_ref.shape[0]//count
    for m in range(count):
        own=refs[m*(2+parts):(m+1)*(2+parts)]
        @pl.when(j+first<per)
        def _(): joined_ref[m*rows:(m+1)*rows,:]=own[0][...]
        @pl.when(j+first>=per)
        def _():
            total=own[1][0].astype(f32)
            for r in own[2:]: total=total+r[0].astype(f32)
            joined_ref[m*rows:(m+1)*rows,:]=total.astype(bf)
    high=high_ref[0]
    right=joined_ref[...]
    send_ref[...]=mm(turned[pl.ds(pl.multiple_of((1-high)*half,half),half),:],right,NN).astype(bf)
    keep_ref[...]=mm(turned[pl.ds(pl.multiple_of(high*half,half),half),:],right,NN).astype(bf)

def project_grads(x, groups, high, first, steps, prev, fb=512):
    rows,D=x.shape; count=len(groups); R=rows//count; per=D//fb; parts=len(groups[0][2])
    three=pl.BlockSpec((1,R,fb),lambda j,h:(jnp.maximum((j+first)//per-1,0),0,jnp.where(j+first<per,0,(j+first)%per)))
    specs=[pl.BlockSpec((rows,D),lambda j,h:(0,0))]; args=[x]
    for dq,own,away in groups:
        specs+=[pl.BlockSpec((R,fb),lambda j,h:(0,jnp.minimum(j+first,per-1))),three]+[three]*parts
        args+=[dq,own]+list(away)
    if prev is not None:
        specs.append(pl.BlockSpec(memory_space=pl.ANY)); args.append(prev)
    return pl.pallas_call(partial(project_body,count,parts,first,per),
        grid_spec=pltpu.PrefetchScalarGridSpec(num_scalar_prefetch=1,grid=(steps,),in_specs=specs,
            out_specs=[pl.BlockSpec((rows,fb),lambda j,h:(0,j+first)),pl.BlockSpec((D//2,fb),lambda j,h:(0,j)),pl.BlockSpec((D//2,fb),lambda j,h:(0,j))],
            scratch_shapes=[pltpu.VMEM((D,rows),bf)]),
        out_shape=[jax.ShapeDtypeStruct((rows,3*D),bf)]+[jax.ShapeDtypeStruct((D//2,steps*fb),bf)]*2,
        input_output_aliases={} if prev is None else {len(args):0},
        cost_estimate=pl.CostEstimate(flops=6*rows*D*D,transcendentals=0,bytes_accessed=rows*D*16+6*D*D),
        name="project_grads")(high,*args)

def widen_body(count, per, high_ref, *refs):
    out_ref=refs[-1]; i=pl.program_id(0)
    @pl.when(i//per==high_ref[0])
    def _():
        start=0
        for r in refs[:count]:
            out_ref[:,start:start+r.shape[1]]=r[...].astype(f32); start+=r.shape[1]
    @pl.when(i//per!=high_ref[0])
    def _():
        start=0
        for r in refs[count:2*count]:
            out_ref[:,start:start+r.shape[1]]=r[...].astype(f32); start+=r.shape[1]

def widen(mine, other, high, rb=256):
    half=mine[0].shape[0]; per=half//rb; width=sum(m.shape[1] for m in mine)
    own=lambda i,h:(jnp.where(i//per==h[0],i%per,jnp.where(h[0]==0,per-1,0)),0)
    away=lambda i,h:(jnp.where(i//per!=h[0],i%per,jnp.where(h[0]==1,per-1,0)),0)
    return pl.pallas_call(partial(widen_body,len(mine),per),
        grid_spec=pltpu.PrefetchScalarGridSpec(num_scalar_prefetch=1,grid=(2*per,),
            in_specs=[pl.BlockSpec((rb,m.shape[1]),own) for m in mine]+[pl.BlockSpec((rb,m.shape[1]),away) for m in mine],
            out_specs=pl.BlockSpec((rb,width),lambda i,h:(i,0))),
        out_shape=jax.ShapeDtypeStruct((2*half,width),f32),
        cost_estimate=pl.CostEstimate(flops=half*width,transcendentals=0,bytes_accessed=half*width*12),
        name="widen")(high,*mine,*other)


HEADS = 16
EPS = 1e-05
HIGH = lax.Precision.HIGHEST


def layer_norm(values, gain, shift):
    center = values - jnp.mean(values, axis=-1, keepdims=True)
    scale = lax.rsqrt(jnp.mean(center * center, axis=-1, keepdims=True) + EPS)
    normal = center * scale
    return (normal * gain + shift, normal, scale)


def norm_back(grad, normal, scale, gain):
    scaled = grad * gain
    inner = (
        scaled
        - jnp.mean(scaled, axis=-1, keepdims=True)
        - normal * jnp.mean(scaled * normal, axis=-1, keepdims=True)
    )
    return (inner * scale, jnp.sum(grad * normal, axis=0), jnp.sum(grad, axis=0))


def swap(values, axis, bit):
    return lax.ppermute(values, axis, [(i, i ^ bit) for i in range(lax.axis_size(axis))])


def bits_of(axis):
    count = lax.axis_size(axis)
    assert count & (count - 1) == 0
    return [(axis, 1 << i) for i in range(count.bit_length() - 1)]


def halve(values, steps, slot):
    sent, kept = [], []
    for value, order in zip(values, steps):
        axis, bit = order[slot]
        high = (lax.axis_index(axis) // bit) % 2
        half = value.shape[0] // 2
        part = lax.dynamic_slice_in_dim(value, (1 - high) * half, half)
        kept.append(lax.dynamic_slice_in_dim(value, high * half, half))
        sent.append(swap(part, axis, bit))
    return [a + b for a, b in zip(kept, sent)]


def double(values, steps, slot):
    sent = [swap(value, *order[slot]) for value, order in zip(values, steps)]
    joined = []
    for value, other, order in zip(values, sent, steps):
        axis, bit = order[slot]
        high = (lax.axis_index(axis) // bit) % 2
        joined.append(
            jnp.concatenate(
                [jnp.where(high == 0, value, other), jnp.where(high == 0, other, value)], axis=0
            )
        )
    return joined


def local(
    tokens,
    out_grad,
    seq_lengths,
    token_order,
    expert_route,
    mixer_gain,
    mixer_shift,
    project_in,
    project_out,
    expert_gain,
    expert_shift,
    router_weight,
    expert_in,
    expert_out,
):
    micro, rows, model = tokens.shape[0], tokens.shape[2], tokens.shape[3]
    contexts = lax.axis_size("context")
    here = lax.axis_index("context")
    experts = expert_in.shape[0] * lax.axis_size("expert")
    capacity = 9 * rows // (8 * experts)
    block = (capacity + 2 + 7) // 8 * 8
    slots = experts * block

    devices = contexts * lax.axis_size("dp")
    hidden = expert_in.shape[2]
    blocks = [expert_in[0][:, k : k + model] for k in range(0, hidden, model)]
    weights = lax.all_gather(
        jnp.concatenate(blocks + [expert_out[0]], axis=0), ("context", "dp"), axis=0
    )

    router_float = router_weight.astype(f32)
    expert_ids = jnp.arange(experts, dtype=jnp.int32)
    slot_ids = jnp.arange(slots, dtype=jnp.int32)

    routes, ranks, places, place_two = [], [], [], []
    sent_grads = []
    for m in range(micro):
        route = expert_route[m, 0, :, 0]
        choose_int = (route[:, None] == expert_ids[None, :]).astype(jnp.int32)
        earlier = jnp.cumsum(choose_int, axis=0) - choose_int
        rank = jnp.sum(earlier * choose_int, axis=1)
        place = (route * block + rank)[None, :] == slot_ids[:, None]
        routes.append(route)
        ranks.append(rank)
        places.append(place.astype(bf))
        target = (route * (2 * block) + rank)[None, :]
        wide = jnp.arange(2 * slots, dtype=jnp.int32)[:, None]
        place_two.append(((target == wide).astype(bf), (target + block == wide).astype(bf)))
        sent_grads.append(
            jnp.dot(places[m], out_grad[m, 0], preferred_element_type=f32)
            .astype(bf)
            .reshape(experts, 1, block, model)
        )
    sent_grads, tokens = lax.optimization_barrier((jnp.concatenate(sent_grads, axis=1), tokens))
    grads_there = lax.all_to_all(sent_grads, "expert", split_axis=0, concat_axis=0, tiled=True)

    flat = tokens.reshape(micro * rows, model)
    normed, normal_one, scale_one = layer_norm(flat.astype(f32), mixer_gain, mixer_shift)
    normed_low = lax.optimization_barrier(normed.astype(bf))
    joined = jnp.dot(normed_low, project_in, preferred_element_type=f32).astype(bf)
    others, biases = [], []
    for m in range(micro):
        pairs = joined[m * rows : (m + 1) * rows, model:]
        parts = [
            lax.ppermute(pairs, "context", [(i, (i + s) % contexts) for i in range(contexts)])
            for s in range(1, contexts)
        ]
        others.append(parts[0] if contexts == 2 else jnp.concatenate(parts, axis=0))
        positions = token_order[m, 0]
        ends = jnp.cumsum(seq_lengths[m, 0])
        segments = jnp.sum((positions[:, None] >= ends[None, :]).astype(jnp.int32), axis=1)
        owners = [(here - s + contexts) % contexts for s in range(contexts)]
        key_positions = jnp.concatenate(
            [lax.dynamic_slice_in_dim(positions, o * rows, rows) for o in owners]
        )
        key_segments = jnp.concatenate(
            [lax.dynamic_slice_in_dim(segments, o * rows, rows) for o in owners]
        )
        query_positions, query_segments = key_positions[:rows], key_segments[:rows]
        biases.append(
            (
                jnp.where(
                    (key_positions[None, :] <= query_positions[:, None])
                    & (key_segments[None, :] == query_segments[:, None]),
                    0.0,
                    -1e30,
                ).astype(f32),
                jnp.where(
                    (key_positions[:, None] <= query_positions[None, :])
                    & (key_segments[:, None] == query_segments[None, :]),
                    0.0,
                    -1e30,
                ).astype(f32),
            )
        )

    saved = []
    before = grads_there
    for m in range(micro):
        attended, mixed_low, lse = attn_fwd(joined, others[m], biases[m][0], m)
        log_total = lse[:, :HEADS].T
        middle = flat[m * rows : (m + 1) * rows].astype(f32) + jnp.dot(
            mixed_low, project_out, preferred_element_type=f32
        )
        second, normal_two, scale_two = layer_norm(middle, expert_gain, expert_shift)
        second_low = second.astype(bf)
        shares = jax.nn.softmax(
            jnp.dot(second_low, router_weight, preferred_element_type=f32), axis=-1
        )
        choose_float = (routes[m][:, None] == expert_ids[None, :]).astype(f32)
        gate = jnp.sum(shares * choose_float, axis=1)
        gate_high = gate.astype(bf)
        gate_low = (gate - gate_high.astype(f32)).astype(bf)
        slot_expert, slot_row = slot_ids // block, slot_ids % block
        mine = slot_expert[:, None] == routes[m][None, :]
        gates = jnp.where(
            mine & (slot_row == capacity)[:, None],
            gate_high[None, :],
            jnp.where(mine & (slot_row == capacity + 1)[:, None], gate_low[None, :], jnp.zeros((), bf)),
        )
        ladder = (ranks[m][:, None] == jnp.arange(model, dtype=jnp.int32)[None, :]).astype(bf)
        sent = jnp.dot(
            jnp.concatenate([places[m], gates], axis=1),
            jnp.concatenate([second_low, ladder], axis=0),
            preferred_element_type=f32,
        ).astype(bf)
        if m + 1 < micro:
            sent, others[m + 1] = lax.optimization_barrier((sent, others[m + 1]))
        sent, before = lax.optimization_barrier((sent, before))
        if m == 0:
            grads_there = before
        else:
            saved[m - 1][-1] = before
        there = lax.all_to_all(
            sent.reshape(experts, block, model), "expert", split_axis=0, concat_axis=0, tiled=True
        )
        before = there
        saved.append(
            [attended, mixed_low, log_total, middle, second_low, normal_two, scale_two, shares,
             choose_float, gate, there]
        )

    kept = None
    rows_there, scaled_there, returned = [], [], []
    for m in range(micro):
        there = saved[m][-1]
        gate_there = there[:, capacity, :block].astype(f32) + there[:, capacity + 1, :block].astype(f32)
        scaled = (gate_there[:, :, None] * grads_there[:, m].astype(f32)).astype(bf)
        there = there.reshape(slots, model)
        scaled = scaled.reshape(slots, model)
        active, inner_grad, back = expert(there, scaled, weights, kept, m, micro, experts)
        if m + 1 < micro:
            back, saved[m + 1][-1] = lax.optimization_barrier((back, saved[m + 1][-1]))
        kept = (active, inner_grad)
        rows_there.append(there)
        scaled_there.append(scaled)
        returned.append(
            lax.all_to_all(back, "expert", split_axis=0, concat_axis=0, tiled=True).reshape(
                2 * slots, model
            )
        )
    active, inner_grad = kept
    out_term = out_grads(scaled_there, active)
    out_term, inner_grad, returned[0] = lax.optimization_barrier((out_term, inner_grad, returned[0]))
    in_term = in_grads(rows_there, inner_grad, devices)
    in_term, place_two[0] = lax.optimization_barrier((in_term, place_two[0]))
    grad_in = lax.psum_scatter(in_term, ("context", "dp"), scatter_dimension=0, tiled=True)[0]
    grad_out_weight = lax.psum_scatter(
        out_term, ("context", "dp"), scatter_dimension=0, tiled=True
    )

    outputs, middle_grads, branches, groups = [], [], [], []
    small = None
    for m in range(micro):
        (attended, mixed_low, log_total, middle, second_low, normal_two, scale_two, shares,
         choose_float, gate, _) = saved[m]
        grad_out = out_grad[m, 0].astype(f32)
        picked = lax.dot_general(place_two[m][0], returned[m], TN, preferred_element_type=f32)
        outputs.append((middle + gate[:, None] * picked).astype(bf))
        gate_grad = jnp.sum(grad_out * picked, axis=1)
        logit_grad = gate_grad[:, None] * gate[:, None] * (choose_float - shares)
        router_term = jnp.einsum("td,te->de", second_low.astype(f32), logit_grad, precision=HIGH)
        second_grad = jnp.einsum("te,de->td", logit_grad, router_float, precision=HIGH)
        second_grad = second_grad + lax.dot_general(
            place_two[m][1], returned[m], TN, preferred_element_type=f32
        )
        middle_part, gain_two, shift_two = norm_back(second_grad, normal_two, scale_two, expert_gain)
        middle_grad = grad_out + middle_part
        branch = middle_grad.astype(bf)
        mixed_grad = lax.dot_general(branch, project_out, NT, preferred_element_type=f32).astype(bf)
        query_grad, own, away = attn_bwd(
            joined, others[m], biases[m][1], log_total, mixed_grad, attended, m
        )
        parts = [
            lax.ppermute(
                away[:, (s - 1) * rows : s * rows] if contexts > 2 else away,
                "context",
                [(i, (i - s) % contexts) for i in range(contexts)],
            )
            for s in range(1, contexts)
        ]
        groups.append([query_grad, own, parts])
        if m + 1 < micro:
            query_grad, place_two[m + 1] = lax.optimization_barrier((query_grad, place_two[m + 1]))
            groups[m][0] = query_grad
        middle_grads.append(middle_grad)
        branches.append(branch)
        terms = (gain_two, shift_two, router_term)
        small = terms if small is None else tuple(a + b for a, b in zip(small, terms))

    mixed_all = jnp.concatenate([s[1] for s in saved], axis=0)
    out_sum = lax.dot_general(
        mixed_all, jnp.concatenate(branches, axis=0), TN, preferred_element_type=f32
    ).astype(bf)
    out_sum, groups[-1][2][0] = lax.optimization_barrier((out_sum, groups[-1][2][0]))
    near, expert_bits, dp_bits = bits_of("context"), bits_of("expert"), bits_of("dp")
    high = (here % 2).astype(jnp.int32).reshape(1)
    halves, joined_grad = [], None
    for first in (0, 3):
        joined_grad, kept, sent = project_grads(normed_low, groups, high, first, 3, joined_grad)
        halves.append(kept + swap(sent, *near[0]))
    halves.append(halve([out_sum], [near], 0)[0])
    for slot in range(1, len(near)):
        halves = halve(halves, [near] * 3, slot)
    chunks = tuple(halves)

    orders = (
        expert_bits[:1] + dp_bits + expert_bits[1:],
        expert_bits[1:2] + expert_bits[:1] + dp_bits + expert_bits[2:],
        dp_bits + expert_bits[1:] + expert_bits[:1],
    )
    count = len(orders[0])
    for slot in range(count):
        chunks = halve(chunks, orders, slot)
        if slot == 0:
            chunks, joined_grad = lax.optimization_barrier((chunks, joined_grad))
            normed_grad = lax.dot_general(joined_grad, project_in, NT, preferred_element_type=f32)
            input_part, gain_one, shift_one = norm_back(normed_grad, normal_one, scale_one, mixer_gain)
            grad_tokens = jnp.concatenate(middle_grads, axis=0) + input_part
            small = jnp.concatenate(
                [gain_one[None], shift_one[None], small[0][None], small[1][None], small[2].T], axis=0
            )
        elif slot == 1:
            chunks, small, grad_tokens = lax.optimization_barrier((chunks, small, grad_tokens))
        else:
            chunks = lax.optimization_barrier(chunks)
    steps = dp_bits + expert_bits + near
    for index in range(count):
        chunks = double(chunks, orders, count - 1 - index)
        small = small + swap(small, *steps[index])
        chunks, small = lax.optimization_barrier((chunks, small))
        if index == 0:
            chunks, grad_in, grad_out_weight = lax.optimization_barrier(
                (chunks, grad_in, grad_out_weight)
            )
            grad_in = jnp.concatenate([grad_in[k] for k in range(grad_in.shape[0])], axis=1).astype(f32)
            grad_out_weight = grad_out_weight.astype(f32)
        if index == count - 2:
            chunks, grad_in, grad_out_weight = lax.optimization_barrier(
                (chunks, grad_in, grad_out_weight)
            )
    for slot in reversed(range(1, len(near))):
        chunks = double(chunks, (near,) * 3, slot)
        small = small + swap(small, *near[slot])
    small = small + swap(small, *near[0])
    others = [swap(chunk, *near[0]) for chunk in chunks]
    out_sum = widen(chunks[2:], others[2:], high)
    in_sum = widen(chunks[:2], others[:2], high)
    return (
        jnp.stack(outputs)[:, None],
        grad_tokens.reshape(micro, 1, rows, model),
        small[0],
        small[1],
        in_sum,
        out_sum,
        small[2],
        small[3],
        small[4:].T,
        grad_in[None],
        grad_out_weight[None],
    )


def solution(mesh):
    tokens = P(None, ("expert", "dp"), "context", None)
    packs = P(None, ("expert", "dp"), None)
    weights = P("expert", ("context", "dp"), None)
    in_specs = (tokens, tokens, packs, packs, tokens) + (P(),) * 7 + (weights, weights)
    out_specs = (tokens, tokens) + (P(),) * 7 + (weights, weights)
    return jax.shard_map(local, mesh=mesh, in_specs=in_specs, out_specs=out_specs, check_vma=False)
```

```python
from functools import partial

import jax
import jax.numpy as jnp
from jax import lax
from jax.sharding import PartitionSpec as P
from jax.experimental import pallas as pl
from jax.experimental.pallas import tpu as pltpu
bf=jnp.bfloat16; f32=jnp.float32
NT=(((1,),(1,)),((),()))
TN=(((0,),(0,)),((),()))
NN=(((1,),(0,)),((),()))
def mm(a,b,dims): return lax.dot_general(a,b,dims,preferred_element_type=f32)

def fwd_body(rb, bias_ref, q_ref, ko_ref, vo_ref, kx_ref, vx_ref, o_ref, ol_ref, lse_ref):
    i=pl.program_id(0)
    rows=q_ref.shape[0]
    lane=lax.broadcasted_iota(jnp.int32,(1,128),1)
    masks=[(lane<64).astype(bf)*0.125,(lane>=64).astype(bf)*0.125]
    ko=ko_ref[...]; vo=vo_ref[...]; kx=kx_ref[...]; vx=vx_ref[...]
    for r in range(0,rows,rb):
        q=q_ref[r:r+rb,:]
        bo=bias_ref[r:r+rb,:rows]; bx=bias_ref[r:r+rb,rows:]
        outs=[]
        old=lse_ref[r:r+rb,:]
        for j in range(2):
            qj=q*masks[j]
            so=mm(qj,ko,NT)+bo
            sx=mm(qj,kx,NT)+bx
            m=jnp.maximum(jnp.max(so,-1,keepdims=True),jnp.max(sx,-1,keepdims=True))
            po=jnp.exp(so-m); px=jnp.exp(sx-m)
            l=jnp.sum(po,-1,keepdims=True)+jnp.sum(px,-1,keepdims=True)
            w=mm(po.astype(bf),vo,NN)+mm(px.astype(bf),vx,NN)
            outs.append(w/l)
            old=jnp.where(lane==2*i+j,m+jnp.log(l),old)
        lse_ref[r:r+rb,:]=old
        o=jnp.where(lane<64,outs[0],outs[1])
        o_ref[r:r+rb,:]=o
        ol_ref[r:r+rb,:]=o.astype(bf)

def attn_fwd(joined, other, bias, mb, rb=None):
    rows=bias.shape[0]; nx=other.shape[0]; D=other.shape[1]//2; G=D//128
    flops=4*rows*(rows+nx)*D
    rb=rb or rows
    return pl.pallas_call(partial(fwd_body,rb),
        grid=(G,),
        in_specs=[pl.BlockSpec(bias.shape,lambda i:(0,0)),
            pl.BlockSpec((rows,128),lambda i:(mb,i)),
            pl.BlockSpec((rows,128),lambda i:(mb,G+i)),
            pl.BlockSpec((rows,128),lambda i:(mb,2*G+i)),
            pl.BlockSpec((nx,128),lambda i:(0,i)),
            pl.BlockSpec((nx,128),lambda i:(0,G+i))],
        out_specs=[pl.BlockSpec((rows,128),lambda i:(0,i)),pl.BlockSpec((rows,128),lambda i:(0,i)),pl.BlockSpec((rows,128),lambda i:(0,0))],
        out_shape=[jax.ShapeDtypeStruct((rows,D),f32),jax.ShapeDtypeStruct((rows,D),bf),jax.ShapeDtypeStruct((rows,128),f32)],
        cost_estimate=pl.CostEstimate(flops=rows,transcendentals=0,bytes_accessed=rows),
        name="attn_fwd")(bias,joined,joined,joined,other,other)

def bwd_body(kb, biast_ref, lse_ref, q_ref, ko_ref, vo_ref, kx_ref, vx_ref, do_ref, o_ref, dq_ref, dko_ref, dx_ref):
    i=pl.program_id(0)
    rows=q_ref.shape[0]; nx=kx_ref.shape[0]
    lane=lax.broadcasted_iota(jnp.int32,(1,128),1)
    masks=[(lane<64).astype(bf),(lane>=64).astype(bf)]
    q=q_ref[...]; do=do_ref[...]
    prod=do.astype(f32)*o_ref[...]
    q2=jnp.concatenate([q*(m*0.125) for m in masks],axis=0)
    do2=jnp.concatenate([do*m for m in masks],axis=0)
    sel=(lax.broadcasted_iota(jnp.int32,(8,128),1)//64==lax.broadcasted_iota(jnp.int32,(8,128),0)).astype(f32)
    delta=lax.dot_general(sel,prod,NT,precision=lax.Precision.HIGHEST,preferred_element_type=f32)
    delta=jnp.concatenate([delta[0:1,:],delta[1:2,:]],axis=1)
    lse=jnp.concatenate([lse_ref[pl.ds(2*i+j,1),:] for j in range(2)],axis=1)
    ks=jnp.concatenate([ko_ref[...],kx_ref[...]],axis=0)
    vs=jnp.concatenate([vo_ref[...],vx_ref[...]],axis=0)
    dq=None
    for b in range(0,rows+nx,kb):
        k=ks[b:b+kb,:]; v=vs[b:b+kb,:]
        bt=biast_ref[b:b+kb,:]
        s=mm(k,q2,NT)+jnp.concatenate([bt,bt],axis=1)
        p=jnp.exp(s-lse)
        dp=mm(v,do2,NT)
        ds=(p*(dp-delta)).astype(bf)
        dv=mm(p.astype(bf),do2,NN).astype(bf)
        dk=mm(ds,q2,NN).astype(bf)
        e=mm(ds,k,TN)
        dq=e if dq is None else dq+e
        cut=min(max(rows-b,0),kb)
        if cut:
            dko_ref[0,b:b+cut,:]=dk[:cut]; dko_ref[1,b:b+cut,:]=dv[:cut]
        if cut<kb:
            at=b+cut-rows
            dx_ref[0,at:at+kb-cut,:]=dk[cut:]; dx_ref[1,at:at+kb-cut,:]=dv[cut:]
    dq_ref[...]=(jnp.where(lane<64,dq[:rows],dq[rows:])*0.125).astype(bf)

def attn_bwd(joined, other, biast, lset, do, o, mb, kb=None):
    rows=biast.shape[1]; nx=other.shape[0]; D=other.shape[1]//2; G=D//128
    flops=10*rows*(rows+nx)*D
    kb=kb or rows
    return pl.pallas_call(partial(bwd_body,kb),
        grid=(G,),
        in_specs=[pl.BlockSpec(biast.shape,lambda i:(0,0)),
            pl.BlockSpec(lset.shape,lambda i:(0,0)),
            pl.BlockSpec((rows,128),lambda i:(mb,i)),
            pl.BlockSpec((rows,128),lambda i:(mb,G+i)),
            pl.BlockSpec((rows,128),lambda i:(mb,2*G+i)),
            pl.BlockSpec((nx,128),lambda i:(0,i)),
            pl.BlockSpec((nx,128),lambda i:(0,G+i)),
            pl.BlockSpec((rows,128),lambda i:(0,i)),
            pl.BlockSpec((rows,128),lambda i:(0,i))],
        out_specs=[pl.BlockSpec((rows,128),lambda i:(0,i)),pl.BlockSpec((2,rows,128),lambda i:(0,0,i)),pl.BlockSpec((2,nx,128),lambda i:(0,0,i))],
        out_shape=[jax.ShapeDtypeStruct((rows,D),bf),jax.ShapeDtypeStruct((2,rows,D),bf),jax.ShapeDtypeStruct((2,nx,D),bf)],
        cost_estimate=pl.CostEstimate(flops=flops*4,transcendentals=16*rows*(rows+nx),bytes_accessed=rows*D*30),
        name="attn_bwd")(biast,lset,joined,joined,joined,other,other,do,o)

C0=0.7978845608028654; C1=0.044715
def exp_body(x_ref, g_ref, wi_ref, wo_ref, *refs):
    act_ref, ig_ref, b_ref, accr, accd = refs[-5:]
    f=pl.program_id(0)
    x=x_ref[...]; g=g_ref[...]; wi=wi_ref[...].reshape(x_ref.shape[1],wi_ref.shape[3]); wo=wo_ref[0,0]
    v=mm(x,wi,NN)
    ag=mm(g,wo,NT)
    v2=v*v
    t=jnp.tanh(C0*(v*(1.0+C1*v2)))
    h=0.5*(1.0+t)
    act=(v*h).astype(bf)
    dg=h+(0.5*C0)*v*(1.0-t*t)*(1.0+(3*C1)*v2)
    ig=(ag*dg).astype(bf)
    act_ref[...]=act; ig_ref[...]=ig
    r=mm(act,wo,NN); d=mm(ig,wi,NT)
    @pl.when(f==0)
    def _(): accr[...]=r; accd[...]=d
    @pl.when(f>0)
    def _(): accr[...]+=r; accd[...]+=d
    @pl.when(f==pl.num_programs(0)-1)
    def _():
        size=b_ref.shape[1]//2
        for e in range(b_ref.shape[0]):
            b_ref[e,:size,:]=accr[e*size:(e+1)*size,:].astype(bf)
            b_ref[e,size:,:]=accd[e*size:(e+1)*size,:].astype(bf)

def expert(x, g, weights, prev, mb, nmb, experts, fb=512):
    rows,D=x.shape; n,deep,_=weights.shape; part=deep//2; FF=part*n; per=D//fb
    blk=pl.BlockSpec((rows,fb),lambda f:(mb,f))
    anyspec=pl.BlockSpec(memory_space=pl.ANY)
    ex=() if prev is None else prev
    return pl.pallas_call(exp_body, grid=(FF//fb,),
        in_specs=[pl.BlockSpec((rows,D),lambda f:(0,0)),pl.BlockSpec((rows,D),lambda f:(0,0)),
                  pl.BlockSpec((n,1,D//n,fb),lambda f:(0,f//per,0,f%per)),
                  pl.BlockSpec((1,1,fb,D),lambda f:(f//(part//fb),part//fb+f%(part//fb),0,0))]+[anyspec]*len(ex),
        out_specs=[blk,blk,pl.BlockSpec((experts,2*rows//experts,D),lambda f:(0,0,0))],
        out_shape=[jax.ShapeDtypeStruct((nmb*rows,FF),bf)]*2+[jax.ShapeDtypeStruct((experts,2*rows//experts,D),bf)],
        scratch_shapes=[pltpu.VMEM((rows,D),f32)]*2,
        input_output_aliases={} if prev is None else {4:0,5:1},
        cost_estimate=pl.CostEstimate(flops=8*rows*D*FF,transcendentals=rows*FF,bytes_accessed=4*D*FF+4*rows*FF),
        name="expert")(x,g,weights.reshape(n,2*FF//D,D//n,D),weights.reshape(n,deep//fb,fb,D),*ex)

def in_grads_body(count, *refs):
    in_ref, turned=refs[-2:]; xs=refs[:count]; ig_ref=refs[count]
    n=in_ref.shape[0]; rows,D=xs[0].shape
    @pl.when(pl.program_id(0)==0)
    def _():
        turned[...]=jnp.concatenate([r[...] for r in xs],axis=0).T
    t=mm(turned[...],ig_ref[...],NN).astype(bf)
    for q in range(n): in_ref[q,0,:,:]=t[q*(D//n):(q+1)*(D//n),:]

def in_grads(xs, ig, n, fb=512):
    rows,D=xs[0].shape; FF=ig.shape[1]; per=D//fb; count=len(xs)
    return pl.pallas_call(partial(in_grads_body,count), grid=(FF//fb,),
        in_specs=[pl.BlockSpec((rows,D),lambda f:(0,0))]*count+[pl.BlockSpec((count*rows,fb),lambda f:(0,f))],
        out_specs=pl.BlockSpec((n,1,D//n,fb),lambda f:(0,f//per,0,f%per)),
        out_shape=jax.ShapeDtypeStruct((n,FF//D,D//n,D),bf),
        scratch_shapes=[pltpu.VMEM((D,count*rows),bf)],
        cost_estimate=pl.CostEstimate(flops=2*count*rows*D*FF,transcendentals=0,bytes_accessed=2*D*FF+2*count*rows*FF),
        name="in_grads")(*xs,ig)

def out_grads_body(count, *refs):
    out_ref, stacked=refs[-2:]; gs=refs[:count]; act_ref=refs[count]; rows=gs[0].shape[0]
    @pl.when(pl.program_id(0)==0)
    def _():
        for m in range(count): stacked[m*rows:(m+1)*rows,:]=gs[m][...]
    out_ref[...]=mm(act_ref[...],stacked[...],TN).astype(bf)

def out_grads(gs, act, fb=512):
    rows,D=gs[0].shape; FF=act.shape[1]; count=len(gs)
    return pl.pallas_call(partial(out_grads_body,count), grid=(FF//fb,),
        in_specs=[pl.BlockSpec((rows,D),lambda f:(0,0))]*count+[pl.BlockSpec((count*rows,fb),lambda f:(0,f))],
        out_specs=pl.BlockSpec((fb,D),lambda f:(f,0)),
        out_shape=jax.ShapeDtypeStruct((FF,D),bf),
        scratch_shapes=[pltpu.VMEM((count*rows,D),bf)],
        cost_estimate=pl.CostEstimate(flops=2*count*rows*D*FF,transcendentals=0,bytes_accessed=2*D*FF+2*count*rows*FF),
        name="out_grads")(*gs,act)

def project_body(count, parts, first, per, high_ref, x_ref, *refs):
    j=pl.program_id(0)
    joined_ref,keep_ref,send_ref,turned=refs[-4:]
    half=keep_ref.shape[0]
    @pl.when(j==0)
    def _(): turned[...]=x_ref[...].T
    rows=x_ref.shape[0]//count
    for m in range(count):
        own=refs[m*(2+parts):(m+1)*(2+parts)]
        @pl.when(j+first<per)
        def _(): joined_ref[m*rows:(m+1)*rows,:]=own[0][...]
        @pl.when(j+first>=per)
        def _():
            total=own[1][0].astype(f32)
            for r in own[2:]: total=total+r[0].astype(f32)
            joined_ref[m*rows:(m+1)*rows,:]=total.astype(bf)
    high=high_ref[0]
    right=joined_ref[...]
    send_ref[...]=mm(turned[pl.ds(pl.multiple_of((1-high)*half,half),half),:],right,NN).astype(bf)
    keep_ref[...]=mm(turned[pl.ds(pl.multiple_of(high*half,half),half),:],right,NN).astype(bf)

def project_grads(x, groups, high, first, steps, prev, fb=512):
    rows,D=x.shape; count=len(groups); R=rows//count; per=D//fb; parts=len(groups[0][2])
    three=pl.BlockSpec((1,R,fb),lambda j,h:(jnp.maximum((j+first)//per-1,0),0,jnp.where(j+first<per,0,(j+first)%per)))
    specs=[pl.BlockSpec((rows,D),lambda j,h:(0,0))]; args=[x]
    for dq,own,away in groups:
        specs+=[pl.BlockSpec((R,fb),lambda j,h:(0,jnp.minimum(j+first,per-1))),three]+[three]*parts
        args+=[dq,own]+list(away)
    if prev is not None:
        specs.append(pl.BlockSpec(memory_space=pl.ANY)); args.append(prev)
    return pl.pallas_call(partial(project_body,count,parts,first,per),
        grid_spec=pltpu.PrefetchScalarGridSpec(num_scalar_prefetch=1,grid=(steps,),in_specs=specs,
            out_specs=[pl.BlockSpec((rows,fb),lambda j,h:(0,j+first)),pl.BlockSpec((D//2,fb),lambda j,h:(0,j)),pl.BlockSpec((D//2,fb),lambda j,h:(0,j))],
            scratch_shapes=[pltpu.VMEM((D,rows),bf)]),
        out_shape=[jax.ShapeDtypeStruct((rows,3*D),bf)]+[jax.ShapeDtypeStruct((D//2,steps*fb),bf)]*2,
        input_output_aliases={} if prev is None else {len(args):0},
        cost_estimate=pl.CostEstimate(flops=6*rows*D*D,transcendentals=0,bytes_accessed=rows*D*16+6*D*D),
        name="project_grads")(high,*args)

def widen_body(count, per, high_ref, *refs):
    out_ref=refs[-1]; i=pl.program_id(0)
    @pl.when(i//per==high_ref[0])
    def _():
        start=0
        for r in refs[:count]:
            out_ref[:,start:start+r.shape[1]]=r[...].astype(f32); start+=r.shape[1]
    @pl.when(i//per!=high_ref[0])
    def _():
        start=0
        for r in refs[count:2*count]:
            out_ref[:,start:start+r.shape[1]]=r[...].astype(f32); start+=r.shape[1]

def widen(mine, other, high, rb=256):
    half=mine[0].shape[0]; per=half//rb; width=sum(m.shape[1] for m in mine)
    own=lambda i,h:(jnp.where(i//per==h[0],i%per,jnp.where(h[0]==0,per-1,0)),0)
    away=lambda i,h:(jnp.where(i//per!=h[0],i%per,jnp.where(h[0]==1,per-1,0)),0)
    return pl.pallas_call(partial(widen_body,len(mine),per),
        grid_spec=pltpu.PrefetchScalarGridSpec(num_scalar_prefetch=1,grid=(2*per,),
            in_specs=[pl.BlockSpec((rb,m.shape[1]),own) for m in mine]+[pl.BlockSpec((rb,m.shape[1]),away) for m in mine],
            out_specs=pl.BlockSpec((rb,width),lambda i,h:(i,0))),
        out_shape=jax.ShapeDtypeStruct((2*half,width),f32),
        cost_estimate=pl.CostEstimate(flops=half*width,transcendentals=0,bytes_accessed=half*width*12),
        name="widen")(high,*mine,*other)


HEADS = 16
EPS = 1e-05
HIGH = lax.Precision.HIGHEST


def layer_norm(values, gain, shift):
    center = values - jnp.mean(values, axis=-1, keepdims=True)
    scale = lax.rsqrt(jnp.mean(center * center, axis=-1, keepdims=True) + EPS)
    normal = center * scale
    return (normal * gain + shift, normal, scale)


def norm_back(grad, normal, scale, gain):
    scaled = grad * gain
    inner = (
        scaled
        - jnp.mean(scaled, axis=-1, keepdims=True)
        - normal * jnp.mean(scaled * normal, axis=-1, keepdims=True)
    )
    return (inner * scale, jnp.sum(grad * normal, axis=0), jnp.sum(grad, axis=0))


def swap(values, axis, bit):
    return lax.ppermute(values, axis, [(i, i ^ bit) for i in range(lax.axis_size(axis))])


def bits_of(axis):
    count = lax.axis_size(axis)
    assert count & (count - 1) == 0
    return [(axis, 1 << i) for i in range(count.bit_length() - 1)]


def cut(values, steps, slot):
    sent, kept = [], []
    for value, order in zip(values, steps):
        axis, bit = order[slot]
        high = (lax.axis_index(axis) // bit) % 2
        half = value.shape[0] // 2
        sent.append(lax.dynamic_slice_in_dim(value, (1 - high) * half, half))
        kept.append(lax.dynamic_slice_in_dim(value, high * half, half))
    return tuple(sent), tuple(kept)


def halve(values, steps, slot):
    sent, kept = cut(values, steps, slot)
    return [a + swap(b, *order[slot]) for a, b, order in zip(kept, sent, steps)]


def double(values, steps, slot):
    sent = [swap(value, *order[slot]) for value, order in zip(values, steps)]
    joined = []
    for value, other, order in zip(values, sent, steps):
        axis, bit = order[slot]
        high = (lax.axis_index(axis) // bit) % 2
        joined.append(
            jnp.concatenate(
                [jnp.where(high == 0, value, other), jnp.where(high == 0, other, value)], axis=0
            )
        )
    return joined


def local(
    tokens,
    out_grad,
    seq_lengths,
    token_order,
    expert_route,
    mixer_gain,
    mixer_shift,
    project_in,
    project_out,
    expert_gain,
    expert_shift,
    router_weight,
    expert_in,
    expert_out,
):
    micro, rows, model = tokens.shape[0], tokens.shape[2], tokens.shape[3]
    contexts = lax.axis_size("context")
    here = lax.axis_index("context")
    experts = expert_in.shape[0] * lax.axis_size("expert")
    capacity = 9 * rows // (8 * experts)
    block = (capacity + 2 + 7) // 8 * 8
    slots = experts * block

    devices = contexts * lax.axis_size("dp")
    hidden = expert_in.shape[2]
    blocks = [expert_in[0][:, k : k + model] for k in range(0, hidden, model)]
    weights = lax.all_gather(
        jnp.concatenate(blocks + [expert_out[0]], axis=0), ("context", "dp"), axis=0
    )

    router_float = router_weight.astype(f32)
    expert_ids = jnp.arange(experts, dtype=jnp.int32)
    slot_ids = jnp.arange(slots, dtype=jnp.int32)

    routes, ranks, places, place_two = [], [], [], []
    sent_grads = []
    for m in range(micro):
        route = expert_route[m, 0, :, 0]
        choose_int = (route[:, None] == expert_ids[None, :]).astype(jnp.int32)
        earlier = jnp.cumsum(choose_int, axis=0) - choose_int
        rank = jnp.sum(earlier * choose_int, axis=1)
        place = (route * block + rank)[None, :] == slot_ids[:, None]
        routes.append(route)
        ranks.append(rank)
        places.append(place.astype(bf))
        target = (route * (2 * block) + rank)[None, :]
        wide = jnp.arange(2 * slots, dtype=jnp.int32)[:, None]
        place_two.append(((target == wide).astype(bf), (target + block == wide).astype(bf)))
        sent_grads.append(
            jnp.dot(places[m], out_grad[m, 0], preferred_element_type=f32)
            .astype(bf)
            .reshape(experts, 1, block, model)
        )
    sent_grads, tokens = lax.optimization_barrier((jnp.concatenate(sent_grads, axis=1), tokens))
    grads_there = lax.all_to_all(sent_grads, "expert", split_axis=0, concat_axis=0, tiled=True)

    flat = tokens.reshape(micro * rows, model)
    normed, normal_one, scale_one = layer_norm(flat.astype(f32), mixer_gain, mixer_shift)
    normed_low = lax.optimization_barrier(normed.astype(bf))
    joined = jnp.dot(normed_low, project_in, preferred_element_type=f32).astype(bf)
    others, biases = [], []
    for m in range(micro):
        pairs = joined[m * rows : (m + 1) * rows, model:]
        parts = [
            lax.ppermute(pairs, "context", [(i, (i + s) % contexts) for i in range(contexts)])
            for s in range(1, contexts)
        ]
        others.append(parts[0] if contexts == 2 else jnp.concatenate(parts, axis=0))
        positions = token_order[m, 0]
        ends = jnp.cumsum(seq_lengths[m, 0])
        segments = jnp.sum((positions[:, None] >= ends[None, :]).astype(jnp.int32), axis=1)
        owners = [(here - s + contexts) % contexts for s in range(contexts)]
        key_positions = jnp.concatenate(
            [lax.dynamic_slice_in_dim(positions, o * rows, rows) for o in owners]
        )
        key_segments = jnp.concatenate(
            [lax.dynamic_slice_in_dim(segments, o * rows, rows) for o in owners]
        )
        query_positions, query_segments = key_positions[:rows], key_segments[:rows]
        biases.append(
            (
                jnp.where(
                    (key_positions[None, :] <= query_positions[:, None])
                    & (key_segments[None, :] == query_segments[:, None]),
                    0.0,
                    -1e30,
                ).astype(f32),
                jnp.where(
                    (key_positions[:, None] <= query_positions[None, :])
                    & (key_segments[:, None] == query_segments[None, :]),
                    0.0,
                    -1e30,
                ).astype(f32),
            )
        )

    saved = []
    before = grads_there
    for m in range(micro):
        attended, mixed_low, lse = attn_fwd(joined, others[m], biases[m][0], m)
        log_total = lse[:, :HEADS].T
        middle = flat[m * rows : (m + 1) * rows].astype(f32) + jnp.dot(
            mixed_low, project_out, preferred_element_type=f32
        )
        second, normal_two, scale_two = layer_norm(middle, expert_gain, expert_shift)
        second_low = second.astype(bf)
        shares = jax.nn.softmax(
            jnp.dot(second_low, router_weight, preferred_element_type=f32), axis=-1
        )
        choose_float = (routes[m][:, None] == expert_ids[None, :]).astype(f32)
        gate = jnp.sum(shares * choose_float, axis=1)
        gate_high = gate.astype(bf)
        gate_low = (gate - gate_high.astype(f32)).astype(bf)
        slot_expert, slot_row = slot_ids // block, slot_ids % block
        mine = slot_expert[:, None] == routes[m][None, :]
        gates = jnp.where(
            mine & (slot_row == capacity)[:, None],
            gate_high[None, :],
            jnp.where(mine & (slot_row == capacity + 1)[:, None], gate_low[None, :], jnp.zeros((), bf)),
        )
        ladder = (ranks[m][:, None] == jnp.arange(model, dtype=jnp.int32)[None, :]).astype(bf)
        sent = jnp.dot(
            jnp.concatenate([places[m], gates], axis=1),
            jnp.concatenate([second_low, ladder], axis=0),
            preferred_element_type=f32,
        ).astype(bf)
        if m + 1 < micro:
            sent, others[m + 1] = lax.optimization_barrier((sent, others[m + 1]))
        if m + 1 == micro:
            logs = tuple(state[2] for state in saved) + (log_total,)
            sent, logs, turned = lax.optimization_barrier((sent, logs, tuple(b[1] for b in biases)))
            log_total = logs[-1]
            for n in range(m):
                saved[n][2] = logs[n]
            biases = [(b[0], t) for b, t in zip(biases, turned)]
        sent, before = lax.optimization_barrier((sent, before))
        if m == 0:
            grads_there = before
        else:
            saved[m - 1][-1] = before
        there = lax.all_to_all(
            sent.reshape(experts, block, model), "expert", split_axis=0, concat_axis=0, tiled=True
        )
        before = there
        saved.append(
            [attended, mixed_low, log_total, middle, second_low, normal_two, scale_two, shares,
             choose_float, gate, there]
        )

    kept = None
    rows_there, scaled_there, returned = [], [], []
    for m in range(micro):
        there = saved[m][-1]
        gate_there = there[:, capacity, :block].astype(f32) + there[:, capacity + 1, :block].astype(f32)
        scaled = (gate_there[:, :, None] * grads_there[:, m].astype(f32)).astype(bf)
        there = there.reshape(slots, model)
        scaled = scaled.reshape(slots, model)
        active, inner_grad, back = expert(there, scaled, weights, kept, m, micro, experts)
        if m + 1 < micro:
            back, saved[m + 1][-1] = lax.optimization_barrier((back, saved[m + 1][-1]))
        kept = (active, inner_grad)
        rows_there.append(there)
        scaled_there.append(scaled)
        returned.append(
            lax.all_to_all(back, "expert", split_axis=0, concat_axis=0, tiled=True).reshape(
                2 * slots, model
            )
        )
    active, inner_grad = kept
    out_term = out_grads(scaled_there, active)
    out_term, inner_grad, returned[0] = lax.optimization_barrier((out_term, inner_grad, returned[0]))
    grad_out_weight = lax.psum_scatter(
        out_term, ("context", "dp"), scatter_dimension=0, tiled=True
    )

    outputs, middle_grads, branches, groups = [], [], [], []
    small = None
    for m in range(micro):
        (attended, mixed_low, log_total, middle, second_low, normal_two, scale_two, shares,
         choose_float, gate, _) = saved[m]
        grad_out = out_grad[m, 0].astype(f32)
        picked = lax.dot_general(place_two[m][0], returned[m], TN, preferred_element_type=f32)
        outputs.append((middle + gate[:, None] * picked).astype(bf))
        gate_grad = jnp.sum(grad_out * picked, axis=1)
        logit_grad = gate_grad[:, None] * gate[:, None] * (choose_float - shares)
        router_term = jnp.einsum("td,te->de", second_low.astype(f32), logit_grad, precision=HIGH)
        second_grad = jnp.einsum("te,de->td", logit_grad, router_float, precision=HIGH)
        second_grad = second_grad + lax.dot_general(
            place_two[m][1], returned[m], TN, preferred_element_type=f32
        )
        middle_part, gain_two, shift_two = norm_back(second_grad, normal_two, scale_two, expert_gain)
        middle_grad = grad_out + middle_part
        branch = middle_grad.astype(bf)
        mixed_grad = lax.dot_general(branch, project_out, NT, preferred_element_type=f32).astype(bf)
        query_grad, own, away = attn_bwd(
            joined, others[m], biases[m][1], log_total, mixed_grad, attended, m
        )
        parts = [
            lax.ppermute(
                away[:, (s - 1) * rows : s * rows] if contexts > 2 else away,
                "context",
                [(i, (i - s) % contexts) for i in range(contexts)],
            )
            for s in range(1, contexts)
        ]
        groups.append([query_grad, own, parts])
        if m == 0:
            inner_grad, query_grad = lax.optimization_barrier((inner_grad, query_grad))
            in_term = in_grads(rows_there, inner_grad, devices)
        if m + 1 < micro:
            in_term, query_grad, place_two[m + 1] = lax.optimization_barrier(
                (in_term, query_grad, place_two[m + 1])
            )
            groups[m][0] = query_grad
        middle_grads.append(middle_grad)
        branches.append(branch)
        terms = (gain_two, shift_two, router_term)
        small = terms if small is None else tuple(a + b for a, b in zip(small, terms))

    mixed_all = jnp.concatenate([s[1] for s in saved], axis=0)
    out_sum = lax.dot_general(
        mixed_all, jnp.concatenate(branches, axis=0), TN, preferred_element_type=f32
    ).astype(bf)
    out_sum, groups[-1][2][0] = lax.optimization_barrier((out_sum, groups[-1][2][0]))
    near, expert_bits, dp_bits = bits_of("context"), bits_of("expert"), bits_of("dp")
    high = (here % 2).astype(jnp.int32).reshape(1)
    halves, joined_grad = [], None
    for first in (0, 3):
        joined_grad, kept, sent = project_grads(normed_low, groups, high, first, 3, joined_grad)
        if first == 0:
            kept, in_term, grad_out_weight = lax.optimization_barrier(
                (kept, in_term, grad_out_weight)
            )
            grad_in = lax.psum_scatter(in_term, ("context", "dp"), scatter_dimension=0, tiled=True)[0]
        halves.append(kept + swap(sent, *near[0]))
    halves.append(halve([out_sum], [near], 0)[0])
    for slot in range(1, len(near)):
        halves = halve(halves, [near] * 3, slot)
    chunks = tuple(halves)

    orders = (
        expert_bits[:1] + dp_bits + expert_bits[1:],
        expert_bits[1:2] + expert_bits[:1] + dp_bits + expert_bits[2:],
        dp_bits + expert_bits[1:] + expert_bits[:1],
    )
    count = len(orders[0])
    steps = near + dp_bits + expert_bits
    for slot in range(count - 1):
        chunks = halve(chunks, orders, slot)
        if slot == 0:
            chunks, joined_grad = lax.optimization_barrier((chunks, joined_grad))
            normed_grad = lax.dot_general(joined_grad, project_in, NT, preferred_element_type=f32)
            input_part, gain_one, shift_one = norm_back(normed_grad, normal_one, scale_one, mixer_gain)
            grad_tokens = jnp.concatenate(middle_grads, axis=0) + input_part
            small = jnp.concatenate(
                [gain_one[None], shift_one[None], small[0][None], small[1][None], small[2].T], axis=0
            )
        elif slot == 1:
            chunks, small, grad_tokens = lax.optimization_barrier((chunks, small, grad_tokens))
        else:
            small = small + swap(small, *steps.pop())
            chunks, small = lax.optimization_barrier((chunks, small))
    small = small + swap(small, *steps.pop())
    chunks, small = lax.optimization_barrier(
        (tuple(chunk + swap(chunk, *order[-1]) for chunk, order in zip(chunks, orders)), small)
    )
    for slot in reversed(range(count - 1)):
        chunks = double(chunks, orders, slot)
        if steps:
            small = small + swap(small, *steps.pop())
        if slot:
            chunks, small = lax.optimization_barrier((tuple(chunks), small))
        if slot == count - 2:
            chunks, grad_in, grad_out_weight = lax.optimization_barrier(
                (chunks, grad_in, grad_out_weight)
            )
            grad_in = jnp.concatenate([grad_in[k] for k in range(grad_in.shape[0])], axis=1).astype(f32)
            grad_out_weight = grad_out_weight.astype(f32)
        if slot == 1:
            chunks, grad_in, grad_out_weight = lax.optimization_barrier(
                (chunks, grad_in, grad_out_weight)
            )
    assert not steps
    for slot in reversed(range(1, len(near))):
        chunks = double(chunks, (near,) * 3, slot)
    out_sum = widen(chunks[2:], [swap(chunks[2], *near[0])], high)
    first, last, out_sum = lax.optimization_barrier((chunks[0], chunks[1], out_sum))
    in_sum = widen([first, last], [swap(first, *near[0]), swap(last, *near[0])], high)
    return (
        jnp.stack(outputs)[:, None],
        grad_tokens.reshape(micro, 1, rows, model),
        small[0],
        small[1],
        in_sum,
        out_sum,
        small[2],
        small[3],
        small[4:].T,
        grad_in[None],
        grad_out_weight[None],
    )


def solution(mesh):
    tokens = P(None, ("expert", "dp"), "context", None)
    packs = P(None, ("expert", "dp"), None)
    weights = P("expert", ("context", "dp"), None)
    in_specs = (tokens, tokens, packs, packs, tokens) + (P(),) * 7 + (weights, weights)
    out_specs = (tokens, tokens) + (P(),) * 7 + (weights, weights)
    return jax.shard_map(local, mesh=mesh, in_specs=in_specs, out_specs=out_specs, check_vma=False)
```

```python
from functools import partial

import jax
import jax.numpy as jnp
from jax import lax
from jax.sharding import PartitionSpec as P
from jax.experimental import pallas as pl
from jax.experimental.pallas import tpu as pltpu
bf=jnp.bfloat16; f32=jnp.float32
NT=(((1,),(1,)),((),()))
TN=(((0,),(0,)),((),()))
NN=(((1,),(0,)),((),()))
def mm(a,b,dims): return lax.dot_general(a,b,dims,preferred_element_type=f32)

def fwd_body(rb, bias_ref, q_ref, ko_ref, vo_ref, kx_ref, vx_ref, o_ref, ol_ref, lse_ref):
    i=pl.program_id(0)
    rows=q_ref.shape[0]
    lane=lax.broadcasted_iota(jnp.int32,(1,128),1)
    masks=[(lane<64).astype(bf)*0.125,(lane>=64).astype(bf)*0.125]
    ko=ko_ref[...]; vo=vo_ref[...]; kx=kx_ref[...]; vx=vx_ref[...]
    for r in range(0,rows,rb):
        q=q_ref[r:r+rb,:]
        bo=bias_ref[r:r+rb,:rows]; bx=bias_ref[r:r+rb,rows:]
        outs=[]
        old=lse_ref[r:r+rb,:]
        for j in range(2):
            qj=q*masks[j]
            so=mm(qj,ko,NT)+bo
            sx=mm(qj,kx,NT)+bx
            m=jnp.maximum(jnp.max(so,-1,keepdims=True),jnp.max(sx,-1,keepdims=True))
            po=jnp.exp(so-m); px=jnp.exp(sx-m)
            l=jnp.sum(po,-1,keepdims=True)+jnp.sum(px,-1,keepdims=True)
            w=mm(po.astype(bf),vo,NN)+mm(px.astype(bf),vx,NN)
            outs.append(w/l)
            old=jnp.where(lane==2*i+j,m+jnp.log(l),old)
        lse_ref[r:r+rb,:]=old
        o=jnp.where(lane<64,outs[0],outs[1])
        o_ref[r:r+rb,:]=o
        ol_ref[r:r+rb,:]=o.astype(bf)

def attn_fwd(joined, other, bias, mb, rb=None):
    rows=bias.shape[0]; nx=other.shape[0]; D=other.shape[1]//2; G=D//128
    flops=4*rows*(rows+nx)*D
    rb=rb or rows
    return pl.pallas_call(partial(fwd_body,rb),
        grid=(G,),
        in_specs=[pl.BlockSpec(bias.shape,lambda i:(0,0)),
            pl.BlockSpec((rows,128),lambda i:(mb,i)),
            pl.BlockSpec((rows,128),lambda i:(mb,G+i)),
            pl.BlockSpec((rows,128),lambda i:(mb,2*G+i)),
            pl.BlockSpec((nx,128),lambda i:(0,i)),
            pl.BlockSpec((nx,128),lambda i:(0,G+i))],
        out_specs=[pl.BlockSpec((rows,128),lambda i:(0,i)),pl.BlockSpec((rows,128),lambda i:(0,i)),pl.BlockSpec((rows,128),lambda i:(0,0))],
        out_shape=[jax.ShapeDtypeStruct((rows,D),f32),jax.ShapeDtypeStruct((rows,D),bf),jax.ShapeDtypeStruct((rows,128),f32)],
        cost_estimate=pl.CostEstimate(flops=rows,transcendentals=0,bytes_accessed=rows),
        name="attn_fwd")(bias,joined,joined,joined,other,other)

def bwd_body(kb, biast_ref, lse_ref, q_ref, ko_ref, vo_ref, kx_ref, vx_ref, do_ref, o_ref, dq_ref, dko_ref, dx_ref):
    i=pl.program_id(0)
    rows=q_ref.shape[0]; nx=kx_ref.shape[0]
    lane=lax.broadcasted_iota(jnp.int32,(1,128),1)
    masks=[(lane<64).astype(bf),(lane>=64).astype(bf)]
    q=q_ref[...]; do=do_ref[...]
    prod=do.astype(f32)*o_ref[...]
    q2=jnp.concatenate([q*(m*0.125) for m in masks],axis=0)
    do2=jnp.concatenate([do*m for m in masks],axis=0)
    sel=(lax.broadcasted_iota(jnp.int32,(8,128),1)//64==lax.broadcasted_iota(jnp.int32,(8,128),0)).astype(f32)
    delta=lax.dot_general(sel,prod,NT,precision=lax.Precision.HIGHEST,preferred_element_type=f32)
    delta=jnp.concatenate([delta[0:1,:],delta[1:2,:]],axis=1)
    lse=jnp.concatenate([lse_ref[pl.ds(2*i+j,1),:] for j in range(2)],axis=1)
    ks=jnp.concatenate([ko_ref[...],kx_ref[...]],axis=0)
    vs=jnp.concatenate([vo_ref[...],vx_ref[...]],axis=0)
    dq=None
    for b in range(0,rows+nx,kb):
        k=ks[b:b+kb,:]; v=vs[b:b+kb,:]
        bt=biast_ref[b:b+kb,:]
        s=mm(k,q2,NT)+jnp.concatenate([bt,bt],axis=1)
        p=jnp.exp(s-lse)
        dp=mm(v,do2,NT)
        ds=(p*(dp-delta)).astype(bf)
        dv=mm(p.astype(bf),do2,NN).astype(bf)
        dk=mm(ds,q2,NN).astype(bf)
        e=mm(k,ds,TN)
        dq=e if dq is None else dq+e
        cut=min(max(rows-b,0),kb)
        if cut:
            dko_ref[0,b:b+cut,:]=dk[:cut]; dko_ref[1,b:b+cut,:]=dv[:cut]
        if cut<kb:
            at=b+cut-rows
            dx_ref[0,at:at+kb-cut,:]=dk[cut:]; dx_ref[1,at:at+kb-cut,:]=dv[cut:]
    dq=dq.T
    dq_ref[...]=(jnp.where(lane<64,dq[:rows],dq[rows:])*0.125).astype(bf)

def attn_bwd(joined, other, biast, lset, do, o, mb, kb=None):
    rows=biast.shape[1]; nx=other.shape[0]; D=other.shape[1]//2; G=D//128
    flops=10*rows*(rows+nx)*D
    kb=kb or 2*rows
    return pl.pallas_call(partial(bwd_body,kb),
        grid=(G,),
        in_specs=[pl.BlockSpec(biast.shape,lambda i:(0,0)),
            pl.BlockSpec(lset.shape,lambda i:(0,0)),
            pl.BlockSpec((rows,128),lambda i:(mb,i)),
            pl.BlockSpec((rows,128),lambda i:(mb,G+i)),
            pl.BlockSpec((rows,128),lambda i:(mb,2*G+i)),
            pl.BlockSpec((nx,128),lambda i:(0,i)),
            pl.BlockSpec((nx,128),lambda i:(0,G+i)),
            pl.BlockSpec((rows,128),lambda i:(0,i)),
            pl.BlockSpec((rows,128),lambda i:(0,i))],
        out_specs=[pl.BlockSpec((rows,128),lambda i:(0,i)),pl.BlockSpec((2,rows,128),lambda i:(0,0,i)),pl.BlockSpec((2,nx,128),lambda i:(0,0,i))],
        out_shape=[jax.ShapeDtypeStruct((rows,D),bf),jax.ShapeDtypeStruct((2,rows,D),bf),jax.ShapeDtypeStruct((2,nx,D),bf)],
        cost_estimate=pl.CostEstimate(flops=flops*4,transcendentals=16*rows*(rows+nx),bytes_accessed=rows*D*30),
        name="attn_bwd")(biast,lset,joined,joined,joined,other,other,do,o)

C0=0.7978845608028654; C1=0.044715
def exp_body(capacity, x_ref, g_ref, wi_ref, wo_ref, *refs):
    act_ref, ig_ref, b_ref, s_ref, accr, accd = refs[-6:]
    f=pl.program_id(0)
    @pl.when(f==0)
    def _():
        size=g_ref.shape[2]
        eye=lax.broadcasted_iota(jnp.int32,(size,128),0)==lax.broadcasted_iota(jnp.int32,(size,128),1)
        for e in range(g_ref.shape[0]):
            at=e*size+capacity
            gate=x_ref[at:at+1,:128].astype(f32)+x_ref[at+1:at+2,:128].astype(f32)
            column=jnp.sum(jnp.where(eye,gate,0.0),axis=1,keepdims=True)
            s_ref[e*size:(e+1)*size,:]=(column*g_ref[e,0].astype(f32)).astype(bf)
    x=x_ref[...]; g=s_ref[...]; wi=wi_ref[...].reshape(x_ref.shape[1],wi_ref.shape[3]); wo=wo_ref[0,0]
    v=mm(x,wi,NN)
    ag=mm(g,wo,NT)
    v2=v*v
    t=jnp.tanh(C0*(v*(1.0+C1*v2)))
    h=0.5*(1.0+t)
    act=(v*h).astype(bf)
    dg=h+(0.5*C0)*v*(1.0-t*t)*(1.0+(3*C1)*v2)
    ig=(ag*dg).astype(bf)
    act_ref[...]=act; ig_ref[...]=ig
    r=mm(act,wo,NN); d=mm(ig,wi,NT)
    @pl.when(f==0)
    def _(): accr[...]=r; accd[...]=d
    @pl.when(f>0)
    def _(): accr[...]+=r; accd[...]+=d
    @pl.when(f==pl.num_programs(0)-1)
    def _():
        size=b_ref.shape[1]//2
        for e in range(b_ref.shape[0]):
            b_ref[e,:size,:]=accr[e*size:(e+1)*size,:].astype(bf)
            b_ref[e,size:,:]=accd[e*size:(e+1)*size,:].astype(bf)

def expert(x, g, weights, prev, mb, nmb, capacity, fb=512):
    rows,D=x.shape; experts,_,size,_=g.shape; n,deep,_=weights.shape; part=deep//2; FF=part*n; per=D//fb
    blk=pl.BlockSpec((rows,fb),lambda f:(mb,f))
    anyspec=pl.BlockSpec(memory_space=pl.ANY)
    ex=() if prev is None else prev
    return pl.pallas_call(partial(exp_body,capacity), grid=(FF//fb,),
        in_specs=[pl.BlockSpec((rows,D),lambda f:(0,0)),pl.BlockSpec((experts,1,size,D),lambda f:(0,mb,0,0)),
                  pl.BlockSpec((n,1,D//n,fb),lambda f:(0,f//per,0,f%per)),
                  pl.BlockSpec((1,1,fb,D),lambda f:(f//(part//fb),part//fb+f%(part//fb),0,0))]+[anyspec]*len(ex),
        out_specs=[blk,blk,pl.BlockSpec((experts,2*size,D),lambda f:(0,0,0)),pl.BlockSpec((rows,D),lambda f:(0,0))],
        out_shape=[jax.ShapeDtypeStruct((nmb*rows,FF),bf)]*2+[jax.ShapeDtypeStruct((experts,2*size,D),bf),jax.ShapeDtypeStruct((rows,D),bf)],
        scratch_shapes=[pltpu.VMEM((rows,D),f32)]*2,
        input_output_aliases={} if prev is None else {4:0,5:1},
        cost_estimate=pl.CostEstimate(flops=8*rows*D*FF,transcendentals=rows*FF,bytes_accessed=4*D*FF+4*rows*FF),
        name="expert")(x,g,weights.reshape(n,2*FF//D,D//n,D),weights.reshape(n,deep//fb,fb,D),*ex)

def in_grads_body(count, *refs):
    in_ref, turned=refs[-2:]; xs=refs[:count]; ig_ref=refs[count]
    n=in_ref.shape[0]; rows,D=xs[0].shape
    @pl.when(pl.program_id(0)==0)
    def _():
        turned[...]=jnp.concatenate([r[...] for r in xs],axis=0).T
    t=mm(turned[...],ig_ref[...],NN).astype(bf)
    for q in range(n): in_ref[q,0,:,:]=t[q*(D//n):(q+1)*(D//n),:]

def in_grads(xs, ig, n, fb=512):
    rows,D=xs[0].shape; FF=ig.shape[1]; per=D//fb; count=len(xs)
    return pl.pallas_call(partial(in_grads_body,count), grid=(FF//fb,),
        in_specs=[pl.BlockSpec((rows,D),lambda f:(0,0))]*count+[pl.BlockSpec((count*rows,fb),lambda f:(0,f))],
        out_specs=pl.BlockSpec((n,1,D//n,fb),lambda f:(0,f//per,0,f%per)),
        out_shape=jax.ShapeDtypeStruct((n,FF//D,D//n,D),bf),
        scratch_shapes=[pltpu.VMEM((D,count*rows),bf)],
        cost_estimate=pl.CostEstimate(flops=2*count*rows*D*FF,transcendentals=0,bytes_accessed=2*D*FF+2*count*rows*FF),
        name="in_grads")(*xs,ig)

def out_grads_body(count, *refs):
    out_ref, stacked=refs[-2:]; gs=refs[:count]; act_ref=refs[count]; rows=gs[0].shape[0]
    @pl.when(pl.program_id(0)==0)
    def _():
        for m in range(count): stacked[m*rows:(m+1)*rows,:]=gs[m][...]
    out_ref[...]=mm(act_ref[...],stacked[...],TN).astype(bf)

def out_grads(gs, act, fb=512):
    rows,D=gs[0].shape; FF=act.shape[1]; count=len(gs)
    return pl.pallas_call(partial(out_grads_body,count), grid=(FF//fb,),
        in_specs=[pl.BlockSpec((rows,D),lambda f:(0,0))]*count+[pl.BlockSpec((count*rows,fb),lambda f:(0,f))],
        out_specs=pl.BlockSpec((fb,D),lambda f:(f,0)),
        out_shape=jax.ShapeDtypeStruct((FF,D),bf),
        scratch_shapes=[pltpu.VMEM((count*rows,D),bf)],
        cost_estimate=pl.CostEstimate(flops=2*count*rows*D*FF,transcendentals=0,bytes_accessed=2*D*FF+2*count*rows*FF),
        name="out_grads")(*gs,act)

def project_body(count, parts, per, high_ref, x_ref, *refs):
    j=pl.program_id(0)
    joined_ref,*outs,turned=refs[-6:]
    half=outs[0].shape[0]
    @pl.when(j==0)
    def _(): turned[...]=x_ref[...].T
    rows=x_ref.shape[0]//count
    for m in range(count):
        own=refs[m*(2+parts):(m+1)*(2+parts)]
        @pl.when(j<per)
        def _(): joined_ref[m*rows:(m+1)*rows,:]=own[0][...]
        @pl.when(j>=per)
        def _():
            total=own[1][0].astype(f32)
            for r in own[2:]: total=total+r[0].astype(f32)
            joined_ref[m*rows:(m+1)*rows,:]=total.astype(bf)
    high=high_ref[0]
    right=joined_ref[...]
    send=mm(turned[pl.ds(pl.multiple_of((1-high)*half,half),half),:],right,NN).astype(bf)
    keep=mm(turned[pl.ds(pl.multiple_of(high*half,half),half),:],right,NN).astype(bf)
    middle=pl.num_programs(0)//2
    @pl.when(j<middle)
    def _(): outs[0][...]=keep; outs[1][...]=send
    @pl.when(j>=middle)
    def _(): outs[2][...]=keep; outs[3][...]=send

def project_grads(x, groups, high, fb=512):
    rows,D=x.shape; count=len(groups); R=rows//count; per=D//fb; parts=len(groups[0][2]); steps=3*per; middle=steps//2
    three=pl.BlockSpec((1,R,fb),lambda j,h:(jnp.maximum(j//per-1,0),0,jnp.where(j<per,0,j%per)))
    specs=[pl.BlockSpec((rows,D),lambda j,h:(0,0))]; args=[x]
    for dq,own,away in groups:
        specs+=[pl.BlockSpec((R,fb),lambda j,h:(0,jnp.minimum(j,per-1))),three]+[three]*parts
        args+=[dq,own]+list(away)
    early=pl.BlockSpec((D//2,fb),lambda j,h:(0,jnp.minimum(j,middle-1)))
    late=pl.BlockSpec((D//2,fb),lambda j,h:(0,jnp.maximum(j-middle,0)))
    return pl.pallas_call(partial(project_body,count,parts,per),
        grid_spec=pltpu.PrefetchScalarGridSpec(num_scalar_prefetch=1,grid=(steps,),in_specs=specs,
            out_specs=[pl.BlockSpec((rows,fb),lambda j,h:(0,j)),early,early,late,late],
            scratch_shapes=[pltpu.VMEM((D,rows),bf)]),
        out_shape=[jax.ShapeDtypeStruct((rows,3*D),bf)]+[jax.ShapeDtypeStruct((D//2,middle*fb),bf)]*4,
        cost_estimate=pl.CostEstimate(flops=6*rows*D*D,transcendentals=0,bytes_accessed=rows*D*16+6*D*D),
        name="project_grads")(high,*args)

def widen_body(count, high_ref, *refs):
    out_ref=refs[-1]; start=0
    for r in refs[:count]:
        out_ref[:,start:start+r.shape[1]]=r[...].astype(f32); start+=r.shape[1]

def widen(values, high, prev=None):
    half=values[0].shape[0]; rb=half if len(values)==1 else half//2; per=half//rb; width=sum(v.shape[1] for v in values); count=len(values)
    ex=[] if prev is None else [prev]
    return pl.pallas_call(partial(widen_body,count),
        grid_spec=pltpu.PrefetchScalarGridSpec(num_scalar_prefetch=1,grid=(per,),
            in_specs=[pl.BlockSpec((rb,v.shape[1]),lambda i,h:(i,0)) for v in values]+[pl.BlockSpec(memory_space=pl.ANY)]*len(ex),
            out_specs=pl.BlockSpec((rb,width),lambda i,h:(h[0]*per+i,0))),
        out_shape=jax.ShapeDtypeStruct((2*half,width),f32),
        input_output_aliases={} if prev is None else {1+count:0},
        cost_estimate=pl.CostEstimate(flops=half*width,transcendentals=0,bytes_accessed=half*width*6),
        name="widen")(high,*values,*ex)

def stack_body(in_ref, out_ref, both_ref):
    both_ref[0,0,:,:]=in_ref[...]; both_ref[1,0,:,:]=out_ref[...]

def stack(first, second):
    short,FF=first.shape; D=second.shape[1]; count=FF//D
    both=pl.pallas_call(stack_body, grid=(count,),
        in_specs=[pl.BlockSpec((short,D),lambda k:(0,k)),pl.BlockSpec((short,D),lambda k:(k,0))],
        out_specs=pl.BlockSpec((2,1,short,D),lambda k:(0,k,0,0)),
        out_shape=jax.ShapeDtypeStruct((2,count,short,D),bf),
        cost_estimate=pl.CostEstimate(flops=0,transcendentals=0,bytes_accessed=8*short*FF),
        name="stack")(first,second)
    return both.reshape(2*count*short,D)


HEADS = 16
EPS = 1e-05
HIGH = lax.Precision.HIGHEST


def layer_norm(values, gain, shift):
    center = values - jnp.mean(values, axis=-1, keepdims=True)
    scale = lax.rsqrt(jnp.mean(center * center, axis=-1, keepdims=True) + EPS)
    normal = center * scale
    return (normal * gain + shift, normal, scale)


def norm_back(grad, normal, scale, gain):
    scaled = grad * gain
    inner = (
        scaled
        - jnp.mean(scaled, axis=-1, keepdims=True)
        - normal * jnp.mean(scaled * normal, axis=-1, keepdims=True)
    )
    return (inner * scale, jnp.sum(grad * normal, axis=0), jnp.sum(grad, axis=0))


def swap(values, axis, bit):
    return lax.ppermute(values, axis, [(i, i ^ bit) for i in range(lax.axis_size(axis))])


def bits_of(axis):
    count = lax.axis_size(axis)
    assert count & (count - 1) == 0
    return [(axis, 1 << i) for i in range(count.bit_length() - 1)]


def cut(values, steps, slot):
    sent, kept = [], []
    for value, order in zip(values, steps):
        axis, bit = order[slot]
        high = (lax.axis_index(axis) // bit) % 2
        half = value.shape[0] // 2
        sent.append(lax.dynamic_slice_in_dim(value, (1 - high) * half, half))
        kept.append(lax.dynamic_slice_in_dim(value, high * half, half))
    return tuple(sent), tuple(kept)


def halve(values, steps, slot):
    sent, kept = cut(values, steps, slot)
    return [a + swap(b, *order[slot]) for a, b, order in zip(kept, sent, steps)]


def join(value, other, step):
    axis, bit = step
    high = (lax.axis_index(axis) // bit) % 2
    return jnp.concatenate(
        [jnp.where(high == 0, value, other), jnp.where(high == 0, other, value)], axis=0
    )


def double(values, steps, slot):
    sent = [swap(value, *order[slot]) for value, order in zip(values, steps)]
    return [join(v, o, order[slot]) for v, o, order in zip(values, sent, steps)]


def local(
    tokens,
    out_grad,
    seq_lengths,
    token_order,
    expert_route,
    mixer_gain,
    mixer_shift,
    project_in,
    project_out,
    expert_gain,
    expert_shift,
    router_weight,
    expert_in,
    expert_out,
):
    micro, rows, model = tokens.shape[0], tokens.shape[2], tokens.shape[3]
    contexts = lax.axis_size("context")
    here = lax.axis_index("context")
    experts = expert_in.shape[0] * lax.axis_size("expert")
    capacity = 9 * rows // (8 * experts)
    block = (capacity + 2 + 7) // 8 * 8
    slots = experts * block

    devices = contexts * lax.axis_size("dp")
    weights = lax.all_gather(stack(expert_in[0], expert_out[0]), ("context", "dp"), axis=0)

    router_float = router_weight.astype(f32)
    expert_ids = jnp.arange(experts, dtype=jnp.int32)
    slot_ids = jnp.arange(slots, dtype=jnp.int32)

    routes, ranks, places, place_two = [], [], [], []
    sent_grads = []
    for m in range(micro):
        route = expert_route[m, 0, :, 0]
        choose_int = (route[:, None] == expert_ids[None, :]).astype(jnp.int32)
        earlier = jnp.cumsum(choose_int, axis=0) - choose_int
        rank = jnp.sum(earlier * choose_int, axis=1)
        place = (route * block + rank)[None, :] == slot_ids[:, None]
        routes.append(route)
        ranks.append(rank)
        places.append(place.astype(bf))
        sent_grads.append(
            jnp.dot(places[m], out_grad[m, 0], preferred_element_type=f32)
            .astype(bf)
            .reshape(experts, 1, block, model)
        )
    sent_grads, tokens = lax.optimization_barrier((jnp.concatenate(sent_grads, axis=1), tokens))
    grads_there = lax.all_to_all(sent_grads, "expert", split_axis=0, concat_axis=0, tiled=True)

    flat = tokens.reshape(micro * rows, model)
    normed, normal_one, scale_one = layer_norm(flat.astype(f32), mixer_gain, mixer_shift)
    normed_low = lax.optimization_barrier(normed.astype(bf))
    joined = jnp.dot(normed_low, project_in, preferred_element_type=f32).astype(bf)
    others, biases = [], []
    for m in range(micro):
        pairs = joined[m * rows : (m + 1) * rows, model:]
        parts = [
            lax.ppermute(pairs, "context", [(i, (i + s) % contexts) for i in range(contexts)])
            for s in range(1, contexts)
        ]
        others.append(parts[0] if contexts == 2 else jnp.concatenate(parts, axis=0))
        positions = token_order[m, 0]
        ends = jnp.cumsum(seq_lengths[m, 0])
        segments = jnp.sum((positions[:, None] >= ends[None, :]).astype(jnp.int32), axis=1)
        owners = [(here - s + contexts) % contexts for s in range(contexts)]
        key_positions = jnp.concatenate(
            [lax.dynamic_slice_in_dim(positions, o * rows, rows) for o in owners]
        )
        key_segments = jnp.concatenate(
            [lax.dynamic_slice_in_dim(segments, o * rows, rows) for o in owners]
        )
        query_positions, query_segments = key_positions[:rows], key_segments[:rows]
        biases.append(
            (
                jnp.where(
                    (key_positions[None, :] <= query_positions[:, None])
                    & (key_segments[None, :] == query_segments[:, None]),
                    0.0,
                    -1e30,
                ).astype(f32),
                (key_positions, key_segments),
            )
        )

    saved = []
    before = grads_there
    for m in range(micro):
        attended, mixed_low, lse = attn_fwd(joined, others[m], biases[m][0], m)
        log_total = lse[:, :HEADS].T
        middle = flat[m * rows : (m + 1) * rows].astype(f32) + jnp.dot(
            mixed_low, project_out, preferred_element_type=f32
        )
        second, normal_two, scale_two = layer_norm(middle, expert_gain, expert_shift)
        second_low = second.astype(bf)
        shares = jax.nn.softmax(
            jnp.dot(second_low, router_weight, preferred_element_type=f32), axis=-1
        )
        choose_float = (routes[m][:, None] == expert_ids[None, :]).astype(f32)
        gate = jnp.sum(shares * choose_float, axis=1)
        gate_high = gate.astype(bf)
        gate_low = (gate - gate_high.astype(f32)).astype(bf)
        slot_expert, slot_row = slot_ids // block, slot_ids % block
        mine = slot_expert[:, None] == routes[m][None, :]
        gates = jnp.where(
            mine & (slot_row == capacity)[:, None],
            gate_high[None, :],
            jnp.where(mine & (slot_row == capacity + 1)[:, None], gate_low[None, :], jnp.zeros((), bf)),
        )
        ladder = (ranks[m][:, None] == jnp.arange(model, dtype=jnp.int32)[None, :]).astype(bf)
        sent = jnp.dot(
            jnp.concatenate([places[m], gates], axis=1),
            jnp.concatenate([second_low, ladder], axis=0),
            preferred_element_type=f32,
        ).astype(bf)
        if m + 1 < micro:
            sent, others[m + 1] = lax.optimization_barrier((sent, others[m + 1]))
        if m + 1 == micro:
            logs = tuple(state[2] for state in saved) + (log_total,)
            attended, targets, places_in_pack, logs = lax.optimization_barrier(
                (attended, tuple(r * (2 * block) + k for r, k in zip(routes, ranks)),
                 tuple(b[1] for b in biases), logs)
            )
            wide = jnp.arange(2 * slots, dtype=jnp.int32)[:, None]
            place_two = [
                ((t[None, :] == wide).astype(bf), (t[None, :] + block == wide).astype(bf))
                for t in targets
            ]
            turned = [
                jnp.where(
                    (p[:, None] <= p[None, :rows]) & (g[:, None] == g[None, :rows]), 0.0, -1e30
                ).astype(f32)
                for p, g in places_in_pack
            ]
            sent, logs, turned, place_two = lax.optimization_barrier(
                (sent, logs, turned, place_two)
            )
            place_two = list(place_two)
            log_total = logs[-1]
            for n in range(m):
                saved[n][2] = logs[n]
            biases = [(b[0], t) for b, t in zip(biases, turned)]
        sent, before = lax.optimization_barrier((sent, before))
        if m == 0:
            grads_there = before
        else:
            saved[m - 1][-1] = before
        there = lax.all_to_all(
            sent.reshape(experts, block, model), "expert", split_axis=0, concat_axis=0, tiled=True
        )
        before = there
        saved.append(
            [attended, mixed_low, log_total, middle, second_low, normal_two, scale_two, shares,
             choose_float, gate, there]
        )

    kept = None
    rows_there, scaled_there, returned = [], [], []
    for m in range(micro):
        there = saved[m][-1]
        there = there.reshape(slots, model)
        active, inner_grad, back, scaled = expert(
            there, grads_there, weights, kept, m, micro, capacity
        )
        if m + 1 < micro:
            back, saved[m + 1][-1] = lax.optimization_barrier((back, saved[m + 1][-1]))
        kept = (active, inner_grad)
        rows_there.append(there)
        scaled_there.append(scaled)
        returned.append(
            lax.all_to_all(back, "expert", split_axis=0, concat_axis=0, tiled=True).reshape(
                2 * slots, model
            )
        )
    active, inner_grad = kept
    out_term = out_grads(scaled_there, active)
    out_term, inner_grad, returned[0] = lax.optimization_barrier((out_term, inner_grad, returned[0]))
    grad_out_weight = lax.psum_scatter(
        out_term, ("context", "dp"), scatter_dimension=0, tiled=True
    )

    outputs, middle_grads, branches, groups = [], [], [], []
    small = None
    for m in range(micro):
        (attended, mixed_low, log_total, middle, second_low, normal_two, scale_two, shares,
         choose_float, gate, _) = saved[m]
        grad_out = out_grad[m, 0].astype(f32)
        picked = lax.dot_general(place_two[m][0], returned[m], TN, preferred_element_type=f32)
        outputs.append((middle + gate[:, None] * picked).astype(bf))
        gate_grad = jnp.sum(grad_out * picked, axis=1)
        logit_grad = gate_grad[:, None] * gate[:, None] * (choose_float - shares)
        router_term = jnp.einsum("td,te->de", second_low.astype(f32), logit_grad, precision=HIGH)
        second_grad = jnp.einsum("te,de->td", logit_grad, router_float, precision=HIGH)
        second_grad = second_grad + lax.dot_general(
            place_two[m][1], returned[m], TN, preferred_element_type=f32
        )
        middle_part, gain_two, shift_two = norm_back(second_grad, normal_two, scale_two, expert_gain)
        middle_grad = grad_out + middle_part
        branch = middle_grad.astype(bf)
        mixed_grad = lax.dot_general(branch, project_out, NT, preferred_element_type=f32).astype(bf)
        query_grad, own, away = attn_bwd(
            joined, others[m], biases[m][1], log_total, mixed_grad, attended, m
        )
        parts = [
            lax.ppermute(
                away[:, (s - 1) * rows : s * rows] if contexts > 2 else away,
                "context",
                [(i, (i - s) % contexts) for i in range(contexts)],
            )
            for s in range(1, contexts)
        ]
        groups.append([query_grad, own, parts])
        if m == 0:
            inner_grad, query_grad = lax.optimization_barrier((inner_grad, query_grad))
            in_term = in_grads(rows_there, inner_grad, devices)
        if m + 1 < micro:
            in_term, query_grad, place_two[m + 1] = lax.optimization_barrier(
                (in_term, query_grad, place_two[m + 1])
            )
            groups[m][0] = query_grad
        middle_grads.append(middle_grad)
        branches.append(branch)
        terms = (gain_two, shift_two, router_term)
        small = terms if small is None else tuple(a + b for a, b in zip(small, terms))

    mixed_all = jnp.concatenate([s[1] for s in saved], axis=0)
    out_sum = lax.dot_general(
        mixed_all, jnp.concatenate(branches, axis=0), TN, preferred_element_type=f32
    ).astype(bf)
    near, expert_bits, dp_bits = bits_of("context"), bits_of("expert"), bits_of("dp")
    sent, kept = cut([out_sum], [near], 0)
    sent, kept, groups[-1][2][0] = lax.optimization_barrier((sent, kept, groups[-1][2][0]))
    out_half = kept[0] + swap(sent[0], *near[0])
    high = (here % 2).astype(jnp.int32).reshape(1)
    joined_grad, kept, sent, kept_too, sent_too = project_grads(normed_low, groups, high)
    kept, in_term, grad_out_weight, out_half = lax.optimization_barrier(
        (kept, in_term, grad_out_weight, out_half)
    )
    grad_in = lax.psum_scatter(in_term, ("context", "dp"), scatter_dimension=0, tiled=True)[0]
    halves = [kept + swap(sent, *near[0]), kept_too + swap(sent_too, *near[0])]
    halves.append(out_half)
    for slot in range(1, len(near)):
        halves = halve(halves, [near] * 3, slot)
    chunks = tuple(halves)

    orders = (
        expert_bits[:1] + dp_bits + expert_bits[1:],
        expert_bits[1:2] + expert_bits[:1] + dp_bits + expert_bits[2:],
        dp_bits + expert_bits[1:] + expert_bits[:1],
    )
    count = len(orders[0])
    steps = near + dp_bits + expert_bits
    for slot in range(count - 1):
        chunks = halve(chunks, orders, slot)
        if slot == 0:
            chunks, joined_grad = lax.optimization_barrier((chunks, joined_grad))
            normed_grad = lax.dot_general(joined_grad, project_in, NT, preferred_element_type=f32)
            input_part, gain_one, shift_one = norm_back(normed_grad, normal_one, scale_one, mixer_gain)
            grad_tokens = jnp.concatenate(middle_grads, axis=0) + input_part
            small = jnp.concatenate(
                [gain_one[None], shift_one[None], small[0][None], small[1][None], small[2].T], axis=0
            )
        elif slot == 1:
            chunks, small, grad_tokens = lax.optimization_barrier((chunks, small, grad_tokens))
        else:
            small = small + swap(small, *steps.pop())
            chunks, small = lax.optimization_barrier((chunks, small))
    small = small + swap(small, *steps.pop())
    chunks, small = lax.optimization_barrier(
        (tuple(chunk + swap(chunk, *order[-1]) for chunk, order in zip(chunks, orders)), small)
    )
    for slot in reversed(range(count - 1)):
        chunks = double(chunks, orders, slot)
        if steps:
            small = small + swap(small, *steps.pop())
        chunks, small = lax.optimization_barrier((tuple(chunks), small))
        if slot == count - 2:
            chunks, grad_in, grad_out_weight = lax.optimization_barrier(
                (chunks, grad_in, grad_out_weight)
            )
            grad_in = jnp.concatenate([grad_in[k] for k in range(grad_in.shape[0])], axis=1).astype(f32)
            grad_out_weight = grad_out_weight.astype(f32)
        if slot == 1:
            chunks, grad_in, grad_out_weight = lax.optimization_barrier(
                (chunks, grad_in, grad_out_weight)
            )
    assert not steps
    for slot in reversed(range(1, len(near))):
        chunks = double(chunks, (near,) * 3, slot)
    arrived = [swap(chunk, *near[0]) for chunk in chunks]
    out_sum = widen(chunks[2:], high)
    in_sum = widen(chunks[:2], high)
    arrived, out_sum, in_sum = lax.optimization_barrier((arrived, out_sum, in_sum))
    out_sum = widen(arrived[2:], 1 - high, out_sum)
    in_sum = widen(arrived[:2], 1 - high, in_sum)
    return (
        jnp.stack(outputs)[:, None],
        grad_tokens.reshape(micro, 1, rows, model),
        small[0],
        small[1],
        in_sum,
        out_sum,
        small[2],
        small[3],
        small[4:].T,
        grad_in[None],
        grad_out_weight[None],
    )


def solution(mesh):
    tokens = P(None, ("expert", "dp"), "context", None)
    packs = P(None, ("expert", "dp"), None)
    weights = P("expert", ("context", "dp"), None)
    in_specs = (tokens, tokens, packs, packs, tokens) + (P(),) * 7 + (weights, weights)
    out_specs = (tokens, tokens) + (P(),) * 7 + (weights, weights)
    return jax.shard_map(local, mesh=mesh, in_specs=in_specs, out_specs=out_specs, check_vma=False)
```

```python
from functools import partial

import jax
import jax.numpy as jnp
from jax import lax
from jax.sharding import PartitionSpec as P
from jax.experimental import pallas as pl
from jax.experimental.pallas import tpu as pltpu
bf=jnp.bfloat16; f32=jnp.float32
NT=(((1,),(1,)),((),()))
TN=(((0,),(0,)),((),()))
NN=(((1,),(0,)),((),()))
def mm(a,b,dims): return lax.dot_general(a,b,dims,preferred_element_type=f32)

def fwd_body(rb, bias_ref, q_ref, ko_ref, vo_ref, kx_ref, vx_ref, o_ref, ol_ref, lse_ref):
    i=pl.program_id(0)
    rows=q_ref.shape[0]
    lane=lax.broadcasted_iota(jnp.int32,(1,128),1)
    masks=[(lane<64).astype(bf)*0.125,(lane>=64).astype(bf)*0.125]
    ko=ko_ref[...]; vo=vo_ref[...]; kx=kx_ref[...]; vx=vx_ref[...]
    for r in range(0,rows,rb):
        q=q_ref[r:r+rb,:]
        bo=bias_ref[r:r+rb,:rows]; bx=bias_ref[r:r+rb,rows:]
        outs=[]
        old=lse_ref[r:r+rb,:]
        for j in range(2):
            qj=q*masks[j]
            so=mm(qj,ko,NT)+bo
            sx=mm(qj,kx,NT)+bx
            m=jnp.maximum(jnp.max(so,-1,keepdims=True),jnp.max(sx,-1,keepdims=True))
            po=jnp.exp(so-m); px=jnp.exp(sx-m)
            l=jnp.sum(po,-1,keepdims=True)+jnp.sum(px,-1,keepdims=True)
            w=mm(po.astype(bf),vo,NN)+mm(px.astype(bf),vx,NN)
            outs.append(w/l)
            old=jnp.where(lane==2*i+j,m+jnp.log(l),old)
        lse_ref[r:r+rb,:]=old
        o=jnp.where(lane<64,outs[0],outs[1])
        o_ref[r:r+rb,:]=o
        ol_ref[r:r+rb,:]=o.astype(bf)

def attn_fwd(joined, other, bias, mb, rb=None):
    rows=bias.shape[0]; nx=other.shape[0]; D=other.shape[1]//2; G=D//128
    flops=4*rows*(rows+nx)*D
    rb=rb or rows
    return pl.pallas_call(partial(fwd_body,rb),
        grid=(G,),
        in_specs=[pl.BlockSpec(bias.shape,lambda i:(0,0)),
            pl.BlockSpec((rows,128),lambda i:(mb,i)),
            pl.BlockSpec((rows,128),lambda i:(mb,G+i)),
            pl.BlockSpec((rows,128),lambda i:(mb,2*G+i)),
            pl.BlockSpec((nx,128),lambda i:(0,i)),
            pl.BlockSpec((nx,128),lambda i:(0,G+i))],
        out_specs=[pl.BlockSpec((rows,128),lambda i:(0,i)),pl.BlockSpec((rows,128),lambda i:(0,i)),pl.BlockSpec((rows,128),lambda i:(0,0))],
        out_shape=[jax.ShapeDtypeStruct((rows,D),f32),jax.ShapeDtypeStruct((rows,D),bf),jax.ShapeDtypeStruct((rows,128),f32)],
        cost_estimate=pl.CostEstimate(flops=rows,transcendentals=0,bytes_accessed=rows),
        name="attn_fwd")(bias,joined,joined,joined,other,other)

def bwd_body(kb, biast_ref, lse_ref, q_ref, ko_ref, vo_ref, kx_ref, vx_ref, do_ref, o_ref, dq_ref, dko_ref, dx_ref):
    i=pl.program_id(0)
    rows=q_ref.shape[0]; nx=kx_ref.shape[0]
    lane=lax.broadcasted_iota(jnp.int32,(1,128),1)
    masks=[(lane<64).astype(bf),(lane>=64).astype(bf)]
    q=q_ref[...]; do=do_ref[...]
    prod=do.astype(f32)*o_ref[...]
    q2=jnp.concatenate([q*(m*0.125) for m in masks],axis=0)
    do2=jnp.concatenate([do*m for m in masks],axis=0)
    sel=(lax.broadcasted_iota(jnp.int32,(8,128),1)//64==lax.broadcasted_iota(jnp.int32,(8,128),0)).astype(f32)
    delta=lax.dot_general(sel,prod,NT,precision=lax.Precision.HIGHEST,preferred_element_type=f32)
    delta=jnp.concatenate([delta[0:1,:],delta[1:2,:]],axis=1)
    lse=jnp.concatenate([lse_ref[pl.ds(2*i+j,1),:] for j in range(2)],axis=1)
    ks=jnp.concatenate([ko_ref[...],kx_ref[...]],axis=0)
    vs=jnp.concatenate([vo_ref[...],vx_ref[...]],axis=0)
    dq=None
    for b in range(0,rows+nx,kb):
        k=ks[b:b+kb,:]; v=vs[b:b+kb,:]
        bt=biast_ref[b:b+kb,:]
        s=mm(k,q2,NT)+jnp.concatenate([bt,bt],axis=1)
        p=jnp.exp(s-lse)
        dp=mm(v,do2,NT)
        ds=(p*(dp-delta)).astype(bf)
        dv=mm(p.astype(bf),do2,NN).astype(bf)
        dk=mm(ds,q2,NN).astype(bf)
        e=mm(k,ds,TN)
        dq=e if dq is None else dq+e
        cut=min(max(rows-b,0),kb)
        if cut:
            dko_ref[0,b:b+cut,:]=dk[:cut]; dko_ref[1,b:b+cut,:]=dv[:cut]
        if cut<kb:
            at=b+cut-rows
            dx_ref[0,at:at+kb-cut,:]=dk[cut:]; dx_ref[1,at:at+kb-cut,:]=dv[cut:]
    dq=dq.T
    dq_ref[...]=(jnp.where(lane<64,dq[:rows],dq[rows:])*0.125).astype(bf)

def attn_bwd(joined, other, biast, lset, do, o, mb, kb=None):
    rows=biast.shape[1]; nx=other.shape[0]; D=other.shape[1]//2; G=D//128
    flops=10*rows*(rows+nx)*D
    kb=kb or 2*rows
    return pl.pallas_call(partial(bwd_body,kb),
        grid=(G,),
        in_specs=[pl.BlockSpec(biast.shape,lambda i:(0,0)),
            pl.BlockSpec(lset.shape,lambda i:(0,0)),
            pl.BlockSpec((rows,128),lambda i:(mb,i)),
            pl.BlockSpec((rows,128),lambda i:(mb,G+i)),
            pl.BlockSpec((rows,128),lambda i:(mb,2*G+i)),
            pl.BlockSpec((nx,128),lambda i:(0,i)),
            pl.BlockSpec((nx,128),lambda i:(0,G+i)),
            pl.BlockSpec((rows,128),lambda i:(0,i)),
            pl.BlockSpec((rows,128),lambda i:(0,i))],
        out_specs=[pl.BlockSpec((rows,128),lambda i:(0,i)),pl.BlockSpec((2,rows,128),lambda i:(0,0,i)),pl.BlockSpec((2,nx,128),lambda i:(0,0,i))],
        out_shape=[jax.ShapeDtypeStruct((rows,D),bf),jax.ShapeDtypeStruct((2,rows,D),bf),jax.ShapeDtypeStruct((2,nx,D),bf)],
        cost_estimate=pl.CostEstimate(flops=flops*4,transcendentals=16*rows*(rows+nx),bytes_accessed=rows*D*30),
        name="attn_bwd")(biast,lset,joined,joined,joined,other,other,do,o)

C0=0.7978845608028654; C1=0.044715
def exp_body(capacity, x_ref, g_ref, wi_ref, wo_ref, *refs):
    act_ref, ig_ref, b_ref, s_ref, accr, accd = refs[-6:]
    f=pl.program_id(0)
    @pl.when(f==0)
    def _():
        size=g_ref.shape[2]
        eye=lax.broadcasted_iota(jnp.int32,(size,128),0)==lax.broadcasted_iota(jnp.int32,(size,128),1)
        for e in range(g_ref.shape[0]):
            at=e*size+capacity
            gate=x_ref[at:at+1,:128].astype(f32)+x_ref[at+1:at+2,:128].astype(f32)
            column=jnp.sum(jnp.where(eye,gate,0.0),axis=1,keepdims=True)
            s_ref[e*size:(e+1)*size,:]=(column*g_ref[e,0].astype(f32)).astype(bf)
    x=x_ref[...]; g=s_ref[...]; wi=wi_ref[...].reshape(x_ref.shape[1],wi_ref.shape[3]); wo=wo_ref[0,0]
    v=mm(x,wi,NN)
    ag=mm(g,wo,NT)
    v2=v*v
    t=jnp.tanh(C0*(v*(1.0+C1*v2)))
    h=0.5*(1.0+t)
    act=(v*h).astype(bf)
    dg=h+(0.5*C0)*v*(1.0-t*t)*(1.0+(3*C1)*v2)
    ig=(ag*dg).astype(bf)
    act_ref[...]=act; ig_ref[...]=ig
    r=mm(act,wo,NN); d=mm(ig,wi,NT)
    @pl.when(f==0)
    def _(): accr[...]=r; accd[...]=d
    @pl.when(f>0)
    def _(): accr[...]+=r; accd[...]+=d
    @pl.when(f==pl.num_programs(0)-1)
    def _():
        size=b_ref.shape[1]//2
        for e in range(b_ref.shape[0]):
            b_ref[e,:size,:]=accr[e*size:(e+1)*size,:].astype(bf)
            b_ref[e,size:,:]=accd[e*size:(e+1)*size,:].astype(bf)

def expert(x, g, weights, prev, mb, nmb, capacity):
    rows,D=x.shape; experts,_,size,_=g.shape; n,deep,_=weights.shape; part=deep//2; FF=part*n; fb=min(D,part); per=D//fb
    blk=pl.BlockSpec((rows,fb),lambda f:(mb,f))
    anyspec=pl.BlockSpec(memory_space=pl.ANY)
    ex=() if prev is None else prev
    return pl.pallas_call(partial(exp_body,capacity), grid=(FF//fb,),
        in_specs=[pl.BlockSpec((rows,D),lambda f:(0,0)),pl.BlockSpec((experts,1,size,D),lambda f:(0,mb,0,0)),
                  pl.BlockSpec((n,1,D//n,fb),lambda f:(0,f//per,0,f%per)),
                  pl.BlockSpec((1,1,fb,D),lambda f:(f//(part//fb),part//fb+f%(part//fb),0,0))]+[anyspec]*len(ex),
        out_specs=[blk,blk,pl.BlockSpec((experts,2*size,D),lambda f:(0,0,0)),pl.BlockSpec((rows,D),lambda f:(0,0))],
        out_shape=[jax.ShapeDtypeStruct((nmb*rows,FF),bf)]*2+[jax.ShapeDtypeStruct((experts,2*size,D),bf),jax.ShapeDtypeStruct((rows,D),bf)],
        scratch_shapes=[pltpu.VMEM((rows,D),f32)]*2,
        input_output_aliases={} if prev is None else {4:0,5:1},
        cost_estimate=pl.CostEstimate(flops=8*rows*D*FF,transcendentals=rows*FF,bytes_accessed=4*D*FF+4*rows*FF),
        name="expert")(x,g,weights.reshape(n,2*FF//D,D//n,D),weights.reshape(n,deep//fb,fb,D),*ex)

def in_grads_body(count, *refs):
    in_ref, turned=refs[-2:]; xs=refs[:count]; ig_ref=refs[count]
    n=in_ref.shape[0]; rows,D=xs[0].shape
    @pl.when(pl.program_id(0)==0)
    def _():
        turned[...]=jnp.concatenate([r[...] for r in xs],axis=0).T
    t=mm(turned[...],ig_ref[...],NN).astype(bf)
    for q in range(n): in_ref[q,0,:,:]=t[q*(D//n):(q+1)*(D//n),:]

def in_grads(xs, ig, n, fb=1024):
    rows,D=xs[0].shape; FF=ig.shape[1]; per=D//fb; count=len(xs)
    return pl.pallas_call(partial(in_grads_body,count), grid=(FF//fb,),
        in_specs=[pl.BlockSpec((rows,D),lambda f:(0,0))]*count+[pl.BlockSpec((count*rows,fb),lambda f:(0,f))],
        out_specs=pl.BlockSpec((n,1,D//n,fb),lambda f:(0,f//per,0,f%per)),
        out_shape=jax.ShapeDtypeStruct((n,FF//D,D//n,D),bf),
        scratch_shapes=[pltpu.VMEM((D,count*rows),bf)],
        cost_estimate=pl.CostEstimate(flops=2*count*rows*D*FF,transcendentals=0,bytes_accessed=2*D*FF+2*count*rows*FF),
        name="in_grads")(*xs,ig)

def out_grads_body(count, *refs):
    out_ref, stacked=refs[-2:]; gs=refs[:count]; act_ref=refs[count]; rows=gs[0].shape[0]
    @pl.when(pl.program_id(0)==0)
    def _():
        for m in range(count): stacked[m*rows:(m+1)*rows,:]=gs[m][...]
    out_ref[...]=mm(act_ref[...],stacked[...],TN).astype(bf)

def out_grads(gs, act, fb=1024):
    rows,D=gs[0].shape; FF=act.shape[1]; count=len(gs)
    return pl.pallas_call(partial(out_grads_body,count), grid=(FF//fb,),
        in_specs=[pl.BlockSpec((rows,D),lambda f:(0,0))]*count+[pl.BlockSpec((count*rows,fb),lambda f:(0,f))],
        out_specs=pl.BlockSpec((fb,D),lambda f:(f,0)),
        out_shape=jax.ShapeDtypeStruct((FF,D),bf),
        scratch_shapes=[pltpu.VMEM((count*rows,D),bf)],
        cost_estimate=pl.CostEstimate(flops=2*count*rows*D*FF,transcendentals=0,bytes_accessed=2*D*FF+2*count*rows*FF),
        name="out_grads")(*gs,act)

def project_body(count, parts, per, high_ref, x_ref, *refs):
    j=pl.program_id(0)
    joined_ref,*outs,turned=refs[-6:]
    half=outs[0].shape[0]
    @pl.when(j==0)
    def _(): turned[...]=x_ref[...].T
    rows=x_ref.shape[0]//count
    for m in range(count):
        own=refs[m*(2+parts):(m+1)*(2+parts)]
        @pl.when(j<per)
        def _(): joined_ref[m*rows:(m+1)*rows,:]=own[0][...]
        @pl.when(j>=per)
        def _():
            total=own[1][0].astype(f32)
            for r in own[2:]: total=total+r[0].astype(f32)
            joined_ref[m*rows:(m+1)*rows,:]=total.astype(bf)
    high=high_ref[0]
    right=joined_ref[...]
    send=mm(turned[pl.ds(pl.multiple_of((1-high)*half,half),half),:],right,NN).astype(bf)
    keep=mm(turned[pl.ds(pl.multiple_of(high*half,half),half),:],right,NN).astype(bf)
    middle=pl.num_programs(0)//2
    @pl.when(j<middle)
    def _(): outs[0][...]=keep; outs[1][...]=send
    @pl.when(j>=middle)
    def _(): outs[2][...]=keep; outs[3][...]=send

def project_grads(x, groups, high, fb=512):
    rows,D=x.shape; count=len(groups); R=rows//count; per=D//fb; parts=len(groups[0][2]); steps=3*per; middle=steps//2
    three=pl.BlockSpec((1,R,fb),lambda j,h:(jnp.maximum(j//per-1,0),0,jnp.where(j<per,0,j%per)))
    specs=[pl.BlockSpec((rows,D),lambda j,h:(0,0))]; args=[x]
    for dq,own,away in groups:
        specs+=[pl.BlockSpec((R,fb),lambda j,h:(0,jnp.minimum(j,per-1))),three]+[three]*parts
        args+=[dq,own]+list(away)
    early=pl.BlockSpec((D//2,fb),lambda j,h:(0,jnp.minimum(j,middle-1)))
    late=pl.BlockSpec((D//2,fb),lambda j,h:(0,jnp.maximum(j-middle,0)))
    return pl.pallas_call(partial(project_body,count,parts,per),
        grid_spec=pltpu.PrefetchScalarGridSpec(num_scalar_prefetch=1,grid=(steps,),in_specs=specs,
            out_specs=[pl.BlockSpec((rows,fb),lambda j,h:(0,j)),early,early,late,late],
            scratch_shapes=[pltpu.VMEM((D,rows),bf)]),
        out_shape=[jax.ShapeDtypeStruct((rows,3*D),bf)]+[jax.ShapeDtypeStruct((D//2,middle*fb),bf)]*4,
        cost_estimate=pl.CostEstimate(flops=6*rows*D*D,transcendentals=0,bytes_accessed=rows*D*16+6*D*D),
        name="project_grads")(high,*args)

def widen_body(count, high_ref, *refs):
    out_ref=refs[-1]; start=0
    for r in refs[:count]:
        out_ref[:,start:start+r.shape[1]]=r[...].astype(f32); start+=r.shape[1]

def widen(values, high, prev=None):
    half=values[0].shape[0]; rb=half if len(values)==1 else half//2; per=half//rb; width=sum(v.shape[1] for v in values); count=len(values)
    ex=[] if prev is None else [prev]
    return pl.pallas_call(partial(widen_body,count),
        grid_spec=pltpu.PrefetchScalarGridSpec(num_scalar_prefetch=1,grid=(per,),
            in_specs=[pl.BlockSpec((rb,v.shape[1]),lambda i,h:(i,0)) for v in values]+[pl.BlockSpec(memory_space=pl.ANY)]*len(ex),
            out_specs=pl.BlockSpec((rb,width),lambda i,h:(h[0]*per+i,0))),
        out_shape=jax.ShapeDtypeStruct((2*half,width),f32),
        input_output_aliases={} if prev is None else {1+count:0},
        cost_estimate=pl.CostEstimate(flops=half*width,transcendentals=0,bytes_accessed=half*width*6),
        name="widen")(high,*values,*ex)

def stack_body(in_ref, out_ref, both_ref):
    both_ref[0,0,:,:]=in_ref[...]; both_ref[1,0,:,:]=out_ref[...]

def stack(first, second):
    short,FF=first.shape; D=second.shape[1]; count=FF//D
    both=pl.pallas_call(stack_body, grid=(count,),
        in_specs=[pl.BlockSpec((short,D),lambda k:(0,k)),pl.BlockSpec((short,D),lambda k:(k,0))],
        out_specs=pl.BlockSpec((2,1,short,D),lambda k:(0,k,0,0)),
        out_shape=jax.ShapeDtypeStruct((2,count,short,D),bf),
        cost_estimate=pl.CostEstimate(flops=0,transcendentals=0,bytes_accessed=8*short*FF),
        name="stack")(first,second)
    return both.reshape(2*count*short,D)


HEADS = 16
EPS = 1e-05
HIGH = lax.Precision.HIGHEST


def layer_norm(values, gain, shift):
    center = values - jnp.mean(values, axis=-1, keepdims=True)
    scale = lax.rsqrt(jnp.mean(center * center, axis=-1, keepdims=True) + EPS)
    normal = center * scale
    return (normal * gain + shift, normal, scale)


def norm_back(grad, normal, scale, gain):
    scaled = grad * gain
    inner = (
        scaled
        - jnp.mean(scaled, axis=-1, keepdims=True)
        - normal * jnp.mean(scaled * normal, axis=-1, keepdims=True)
    )
    return (inner * scale, jnp.sum(grad * normal, axis=0), jnp.sum(grad, axis=0))


def swap(values, axis, bit):
    return lax.ppermute(values, axis, [(i, i ^ bit) for i in range(lax.axis_size(axis))])


def bits_of(axis):
    count = lax.axis_size(axis)
    assert count & (count - 1) == 0
    return [(axis, 1 << i) for i in range(count.bit_length() - 1)]


def cut(values, steps, slot):
    sent, kept = [], []
    for value, order in zip(values, steps):
        axis, bit = order[slot]
        high = (lax.axis_index(axis) // bit) % 2
        half = value.shape[0] // 2
        sent.append(lax.dynamic_slice_in_dim(value, (1 - high) * half, half))
        kept.append(lax.dynamic_slice_in_dim(value, high * half, half))
    return tuple(sent), tuple(kept)


def halve(values, steps, slot):
    sent, kept = cut(values, steps, slot)
    return [a + swap(b, *order[slot]) for a, b, order in zip(kept, sent, steps)]


def join(value, other, step):
    axis, bit = step
    high = (lax.axis_index(axis) // bit) % 2
    return jnp.concatenate(
        [jnp.where(high == 0, value, other), jnp.where(high == 0, other, value)], axis=0
    )


def double(values, steps, slot):
    sent = [swap(value, *order[slot]) for value, order in zip(values, steps)]
    return [join(v, o, order[slot]) for v, o, order in zip(values, sent, steps)]


def local(
    tokens,
    out_grad,
    seq_lengths,
    token_order,
    expert_route,
    mixer_gain,
    mixer_shift,
    project_in,
    project_out,
    expert_gain,
    expert_shift,
    router_weight,
    expert_in,
    expert_out,
):
    micro, rows, model = tokens.shape[0], tokens.shape[2], tokens.shape[3]
    contexts = lax.axis_size("context")
    here = lax.axis_index("context")
    experts = expert_in.shape[0] * lax.axis_size("expert")
    capacity = 9 * rows // (8 * experts)
    block = (capacity + 2 + 7) // 8 * 8
    slots = experts * block

    devices = contexts * lax.axis_size("dp")
    weights = lax.all_gather(stack(expert_in[0], expert_out[0]), ("context", "dp"), axis=0)

    router_float = router_weight.astype(f32)
    expert_ids = jnp.arange(experts, dtype=jnp.int32)
    slot_ids = jnp.arange(slots, dtype=jnp.int32)

    routes, ranks, places, place_two = [], [], [], []
    sent_grads = []
    for m in range(micro):
        route = expert_route[m, 0, :, 0]
        choose_int = (route[:, None] == expert_ids[None, :]).astype(jnp.int32)
        earlier = jnp.cumsum(choose_int, axis=0) - choose_int
        rank = jnp.sum(earlier * choose_int, axis=1)
        place = (route * block + rank)[None, :] == slot_ids[:, None]
        routes.append(route)
        ranks.append(rank)
        places.append(place.astype(bf))
        sent_grads.append(
            jnp.dot(places[m], out_grad[m, 0], preferred_element_type=f32)
            .astype(bf)
            .reshape(experts, 1, block, model)
        )
    sent_grads, tokens = lax.optimization_barrier((jnp.concatenate(sent_grads, axis=1), tokens))
    grads_there = lax.all_to_all(sent_grads, "expert", split_axis=0, concat_axis=0, tiled=True)

    flat = tokens.reshape(micro * rows, model)
    normed, normal_one, scale_one = layer_norm(flat.astype(f32), mixer_gain, mixer_shift)
    normed_low = lax.optimization_barrier(normed.astype(bf))
    joined = jnp.dot(normed_low, project_in, preferred_element_type=f32).astype(bf)
    others, biases = [], []
    for m in range(micro):
        pairs = joined[m * rows : (m + 1) * rows, model:]
        parts = [
            lax.ppermute(pairs, "context", [(i, (i + s) % contexts) for i in range(contexts)])
            for s in range(1, contexts)
        ]
        others.append(parts[0] if contexts == 2 else jnp.concatenate(parts, axis=0))
        positions = token_order[m, 0]
        ends = jnp.cumsum(seq_lengths[m, 0])
        segments = jnp.sum((positions[:, None] >= ends[None, :]).astype(jnp.int32), axis=1)
        owners = [(here - s + contexts) % contexts for s in range(contexts)]
        key_positions = jnp.concatenate(
            [lax.dynamic_slice_in_dim(positions, o * rows, rows) for o in owners]
        )
        key_segments = jnp.concatenate(
            [lax.dynamic_slice_in_dim(segments, o * rows, rows) for o in owners]
        )
        query_positions, query_segments = key_positions[:rows], key_segments[:rows]
        biases.append(
            (
                jnp.where(
                    (key_positions[None, :] <= query_positions[:, None])
                    & (key_segments[None, :] == query_segments[:, None]),
                    0.0,
                    -1e30,
                ).astype(f32),
                (key_positions, key_segments),
            )
        )

    saved = []
    before = grads_there
    for m in range(micro):
        attended, mixed_low, lse = attn_fwd(joined, others[m], biases[m][0], m)
        log_total = lse[:, :HEADS].T
        middle = flat[m * rows : (m + 1) * rows].astype(f32) + jnp.dot(
            mixed_low, project_out, preferred_element_type=f32
        )
        second, normal_two, scale_two = layer_norm(middle, expert_gain, expert_shift)
        second_low = second.astype(bf)
        shares = jax.nn.softmax(
            jnp.dot(second_low, router_weight, preferred_element_type=f32), axis=-1
        )
        choose_float = (routes[m][:, None] == expert_ids[None, :]).astype(f32)
        gate = jnp.sum(shares * choose_float, axis=1)
        gate_high = gate.astype(bf)
        gate_low = (gate - gate_high.astype(f32)).astype(bf)
        slot_expert, slot_row = slot_ids // block, slot_ids % block
        mine = slot_expert[:, None] == routes[m][None, :]
        gates = jnp.where(
            mine & (slot_row == capacity)[:, None],
            gate_high[None, :],
            jnp.where(mine & (slot_row == capacity + 1)[:, None], gate_low[None, :], jnp.zeros((), bf)),
        )
        ladder = (ranks[m][:, None] == jnp.arange(model, dtype=jnp.int32)[None, :]).astype(bf)
        sent = jnp.dot(
            jnp.concatenate([places[m], gates], axis=1),
            jnp.concatenate([second_low, ladder], axis=0),
            preferred_element_type=f32,
        ).astype(bf)
        if m + 1 < micro:
            sent, others[m + 1] = lax.optimization_barrier((sent, others[m + 1]))
        if m + 1 == micro:
            logs = tuple(state[2] for state in saved) + (log_total,)
            attended, targets, places_in_pack, logs = lax.optimization_barrier(
                (attended, tuple(r * (2 * block) + k for r, k in zip(routes, ranks)),
                 tuple(b[1] for b in biases), logs)
            )
            wide = jnp.arange(2 * slots, dtype=jnp.int32)[:, None]
            place_two = [
                ((t[None, :] == wide).astype(bf), (t[None, :] + block == wide).astype(bf))
                for t in targets
            ]
            turned = [
                jnp.where(
                    (p[:, None] <= p[None, :rows]) & (g[:, None] == g[None, :rows]), 0.0, -1e30
                ).astype(f32)
                for p, g in places_in_pack
            ]
            sent, logs, turned, place_two = lax.optimization_barrier(
                (sent, logs, turned, place_two)
            )
            place_two = list(place_two)
            log_total = logs[-1]
            for n in range(m):
                saved[n][2] = logs[n]
            biases = [(b[0], t) for b, t in zip(biases, turned)]
        sent, before = lax.optimization_barrier((sent, before))
        if m == 0:
            grads_there = before
        else:
            saved[m - 1][-1] = before
        there = lax.all_to_all(
            sent.reshape(experts, block, model), "expert", split_axis=0, concat_axis=0, tiled=True
        )
        before = there
        saved.append(
            [attended, mixed_low, log_total, middle, second_low, normal_two, scale_two, shares,
             choose_float, gate, there]
        )

    kept = None
    rows_there, scaled_there, returned = [], [], []
    for m in range(micro):
        there = saved[m][-1]
        there = there.reshape(slots, model)
        active, inner_grad, back, scaled = expert(
            there, grads_there, weights, kept, m, micro, capacity
        )
        if m + 1 < micro:
            back, saved[m + 1][-1] = lax.optimization_barrier((back, saved[m + 1][-1]))
        kept = (active, inner_grad)
        rows_there.append(there)
        scaled_there.append(scaled)
        returned.append(
            lax.all_to_all(back, "expert", split_axis=0, concat_axis=0, tiled=True).reshape(
                2 * slots, model
            )
        )
    active, inner_grad = kept
    out_term = out_grads(scaled_there, active)
    out_term, inner_grad, returned[0] = lax.optimization_barrier((out_term, inner_grad, returned[0]))
    grad_out_weight = lax.psum_scatter(
        out_term, ("context", "dp"), scatter_dimension=0, tiled=True
    )

    outputs, middle_grads, branches, groups = [], [], [], []
    small = None
    for m in range(micro):
        (attended, mixed_low, log_total, middle, second_low, normal_two, scale_two, shares,
         choose_float, gate, _) = saved[m]
        grad_out = out_grad[m, 0].astype(f32)
        picked = lax.dot_general(place_two[m][0], returned[m], TN, preferred_element_type=f32)
        outputs.append((middle + gate[:, None] * picked).astype(bf))
        gate_grad = jnp.sum(grad_out * picked, axis=1)
        logit_grad = gate_grad[:, None] * gate[:, None] * (choose_float - shares)
        router_term = jnp.einsum("td,te->de", second_low.astype(f32), logit_grad, precision=HIGH)
        second_grad = jnp.einsum("te,de->td", logit_grad, router_float, precision=HIGH)
        second_grad = second_grad + lax.dot_general(
            place_two[m][1], returned[m], TN, preferred_element_type=f32
        )
        middle_part, gain_two, shift_two = norm_back(second_grad, normal_two, scale_two, expert_gain)
        middle_grad = grad_out + middle_part
        branch = middle_grad.astype(bf)
        mixed_grad = lax.dot_general(branch, project_out, NT, preferred_element_type=f32).astype(bf)
        query_grad, own, away = attn_bwd(
            joined, others[m], biases[m][1], log_total, mixed_grad, attended, m
        )
        parts = [
            lax.ppermute(
                away[:, (s - 1) * rows : s * rows] if contexts > 2 else away,
                "context",
                [(i, (i - s) % contexts) for i in range(contexts)],
            )
            for s in range(1, contexts)
        ]
        groups.append([query_grad, own, parts])
        if m == 0:
            inner_grad, query_grad = lax.optimization_barrier((inner_grad, query_grad))
            in_term = in_grads(rows_there, inner_grad, devices)
        if m + 1 < micro:
            in_term, query_grad, place_two[m + 1] = lax.optimization_barrier(
                (in_term, query_grad, place_two[m + 1])
            )
            groups[m][0] = query_grad
        middle_grads.append(middle_grad)
        branches.append(branch)
        terms = (gain_two, shift_two, router_term)
        small = terms if small is None else tuple(a + b for a, b in zip(small, terms))

    mixed_all = jnp.concatenate([s[1] for s in saved], axis=0)
    out_sum = lax.dot_general(
        mixed_all, jnp.concatenate(branches, axis=0), TN, preferred_element_type=f32
    ).astype(bf)
    near, expert_bits, dp_bits = bits_of("context"), bits_of("expert"), bits_of("dp")
    sent, kept = cut([out_sum], [near], 0)
    sent, kept, groups[-1][2][0] = lax.optimization_barrier((sent, kept, groups[-1][2][0]))
    out_half = kept[0] + swap(sent[0], *near[0])
    high = (here % 2).astype(jnp.int32).reshape(1)
    joined_grad, kept, sent, kept_too, sent_too = project_grads(normed_low, groups, high)
    kept, in_term, grad_out_weight, out_half = lax.optimization_barrier(
        (kept, in_term, grad_out_weight, out_half)
    )
    grad_in = lax.psum_scatter(in_term, ("context", "dp"), scatter_dimension=0, tiled=True)[0]
    halves = [kept + swap(sent, *near[0]), kept_too + swap(sent_too, *near[0])]
    halves.append(out_half)
    for slot in range(1, len(near)):
        halves = halve(halves, [near] * 3, slot)
    chunks = tuple(halves)

    orders = (
        expert_bits[:1] + dp_bits + expert_bits[1:],
        expert_bits[1:2] + expert_bits[:1] + dp_bits + expert_bits[2:],
        dp_bits + expert_bits[1:] + expert_bits[:1],
    )
    count = len(orders[0])
    steps = near + dp_bits + expert_bits
    for slot in range(count - 1):
        chunks = halve(chunks, orders, slot)
        if slot == 0:
            chunks, joined_grad = lax.optimization_barrier((chunks, joined_grad))
            normed_grad = lax.dot_general(joined_grad, project_in, NT, preferred_element_type=f32)
            input_part, gain_one, shift_one = norm_back(normed_grad, normal_one, scale_one, mixer_gain)
            grad_tokens = jnp.concatenate(middle_grads, axis=0) + input_part
            small = jnp.concatenate(
                [gain_one[None], shift_one[None], small[0][None], small[1][None], small[2].T], axis=0
            )
        elif slot == 1:
            chunks, small, grad_tokens = lax.optimization_barrier((chunks, small, grad_tokens))
        else:
            chunks = lax.optimization_barrier(chunks)
    for step in steps:
        small = small + swap(small, *step)
    chunks = lax.optimization_barrier(
        tuple(chunk + swap(chunk, *order[-1]) for chunk, order in zip(chunks, orders))
    )
    for slot in reversed(range(count - 1)):
        chunks = double(chunks, orders, slot)
        if slot == 1:
            chunks, small = lax.optimization_barrier((tuple(chunks), small))
        else:
            chunks = lax.optimization_barrier(tuple(chunks))
        if slot == count - 2:
            chunks, grad_in, grad_out_weight = lax.optimization_barrier(
                (chunks, grad_in, grad_out_weight)
            )
            grad_in = jnp.concatenate([grad_in[k] for k in range(grad_in.shape[0])], axis=1).astype(f32)
            grad_out_weight = grad_out_weight.astype(f32)
        if slot == 1:
            chunks, grad_in, grad_out_weight = lax.optimization_barrier(
                (chunks, grad_in, grad_out_weight)
            )
    for slot in reversed(range(1, len(near))):
        chunks = double(chunks, (near,) * 3, slot)
    arrived = [swap(chunk, *near[0]) for chunk in chunks]
    out_sum = widen(chunks[2:], high)
    in_sum = widen(chunks[:2], high)
    arrived, out_sum, in_sum = lax.optimization_barrier((arrived, out_sum, in_sum))
    out_sum = widen(arrived[2:], 1 - high, out_sum)
    in_sum = widen(arrived[:2], 1 - high, in_sum)
    return (
        jnp.stack(outputs)[:, None],
        grad_tokens.reshape(micro, 1, rows, model),
        small[0],
        small[1],
        in_sum,
        out_sum,
        small[2],
        small[3],
        small[4:].T,
        grad_in[None],
        grad_out_weight[None],
    )


def solution(mesh):
    tokens = P(None, ("expert", "dp"), "context", None)
    packs = P(None, ("expert", "dp"), None)
    weights = P("expert", ("context", "dp"), None)
    in_specs = (tokens, tokens, packs, packs, tokens) + (P(),) * 7 + (weights, weights)
    out_specs = (tokens, tokens) + (P(),) * 7 + (weights, weights)
    return jax.shard_map(local, mesh=mesh, in_specs=in_specs, out_specs=out_specs, check_vma=False)
```

```python
from functools import partial

import jax
import jax.numpy as jnp
from jax import lax
from jax.sharding import PartitionSpec as P
from jax.experimental import pallas as pl
from jax.experimental.pallas import tpu as pltpu
bf=jnp.bfloat16; f32=jnp.float32
NT=(((1,),(1,)),((),()))
TN=(((0,),(0,)),((),()))
NN=(((1,),(0,)),((),()))
def mm(a,b,dims): return lax.dot_general(a,b,dims,preferred_element_type=f32)

def fwd_body(rb, bias_ref, q_ref, ko_ref, vo_ref, kx_ref, vx_ref, o_ref, ol_ref, lse_ref):
    i=pl.program_id(0)
    rows=q_ref.shape[0]
    lane=lax.broadcasted_iota(jnp.int32,(1,128),1)
    masks=[(lane<64).astype(bf)*0.125,(lane>=64).astype(bf)*0.125]
    ko=ko_ref[...]; vo=vo_ref[...]; kx=kx_ref[...]; vx=vx_ref[...]
    for r in range(0,rows,rb):
        q=q_ref[r:r+rb,:]
        bo=bias_ref[r:r+rb,:rows]; bx=bias_ref[r:r+rb,rows:]
        outs=[]
        old=lse_ref[r:r+rb,:]
        for j in range(2):
            qj=q*masks[j]
            so=mm(qj,ko,NT)+bo
            sx=mm(qj,kx,NT)+bx
            m=jnp.maximum(jnp.max(so,-1,keepdims=True),jnp.max(sx,-1,keepdims=True))
            po=jnp.exp(so-m); px=jnp.exp(sx-m)
            l=jnp.sum(po,-1,keepdims=True)+jnp.sum(px,-1,keepdims=True)
            w=mm(po.astype(bf),vo,NN)+mm(px.astype(bf),vx,NN)
            outs.append(w/l)
            old=jnp.where(lane==2*i+j,m+jnp.log(l),old)
        lse_ref[r:r+rb,:]=old
        o=jnp.where(lane<64,outs[0],outs[1])
        o_ref[r:r+rb,:]=o
        ol_ref[r:r+rb,:]=o.astype(bf)

def attn_fwd(joined, other, bias, mb, rb=None):
    rows=bias.shape[0]; nx=other.shape[0]; D=other.shape[1]//2; G=D//128
    flops=4*rows*(rows+nx)*D
    rb=rb or rows
    return pl.pallas_call(partial(fwd_body,rb),
        grid=(G,),
        in_specs=[pl.BlockSpec(bias.shape,lambda i:(0,0)),
            pl.BlockSpec((rows,128),lambda i:(mb,i)),
            pl.BlockSpec((rows,128),lambda i:(mb,G+i)),
            pl.BlockSpec((rows,128),lambda i:(mb,2*G+i)),
            pl.BlockSpec((nx,128),lambda i:(0,i)),
            pl.BlockSpec((nx,128),lambda i:(0,G+i))],
        out_specs=[pl.BlockSpec((rows,128),lambda i:(0,i)),pl.BlockSpec((rows,128),lambda i:(0,i)),pl.BlockSpec((rows,128),lambda i:(0,0))],
        out_shape=[jax.ShapeDtypeStruct((rows,D),f32),jax.ShapeDtypeStruct((rows,D),bf),jax.ShapeDtypeStruct((rows,128),f32)],
        cost_estimate=pl.CostEstimate(flops=rows,transcendentals=0,bytes_accessed=rows),
        name="attn_fwd")(bias,joined,joined,joined,other,other)

def bwd_body(kb, biast_ref, lse_ref, q_ref, ko_ref, vo_ref, kx_ref, vx_ref, do_ref, o_ref, dq_ref, dko_ref, dx_ref):
    i=pl.program_id(0)
    rows=q_ref.shape[0]; nx=kx_ref.shape[0]
    lane=lax.broadcasted_iota(jnp.int32,(1,128),1)
    masks=[(lane<64).astype(bf),(lane>=64).astype(bf)]
    q=q_ref[...]; do=do_ref[...]
    prod=do.astype(f32)*o_ref[...]
    q2=jnp.concatenate([q*(m*0.125) for m in masks],axis=0)
    do2=jnp.concatenate([do*m for m in masks],axis=0)
    sel=(lax.broadcasted_iota(jnp.int32,(8,128),1)//64==lax.broadcasted_iota(jnp.int32,(8,128),0)).astype(f32)
    delta=lax.dot_general(sel,prod,NT,precision=lax.Precision.HIGHEST,preferred_element_type=f32)
    delta=jnp.concatenate([delta[0:1,:],delta[1:2,:]],axis=1)
    lse=jnp.concatenate([lse_ref[pl.ds(2*i+j,1),:] for j in range(2)],axis=1)
    ks=jnp.concatenate([ko_ref[...],kx_ref[...]],axis=0)
    vs=jnp.concatenate([vo_ref[...],vx_ref[...]],axis=0)
    dq=None
    for b in range(0,rows+nx,kb):
        k=ks[b:b+kb,:]; v=vs[b:b+kb,:]
        bt=biast_ref[b:b+kb,:]
        s=mm(k,q2,NT)+jnp.concatenate([bt,bt],axis=1)
        p=jnp.exp(s-lse)
        dp=mm(v,do2,NT)
        ds=(p*(dp-delta)).astype(bf)
        dv=mm(p.astype(bf),do2,NN).astype(bf)
        dk=mm(ds,q2,NN).astype(bf)
        e=mm(k,ds,TN)
        dq=e if dq is None else dq+e
        cut=min(max(rows-b,0),kb)
        if cut:
            dko_ref[0,b:b+cut,:]=dk[:cut]; dko_ref[1,b:b+cut,:]=dv[:cut]
        if cut<kb:
            at=b+cut-rows
            dx_ref[0,at:at+kb-cut,:]=dk[cut:]; dx_ref[1,at:at+kb-cut,:]=dv[cut:]
    dq=dq.T
    dq_ref[...]=(jnp.where(lane<64,dq[:rows],dq[rows:])*0.125).astype(bf)

def attn_bwd(joined, other, biast, lset, do, o, mb, kb=None):
    rows=biast.shape[1]; nx=other.shape[0]; D=other.shape[1]//2; G=D//128
    flops=10*rows*(rows+nx)*D
    kb=kb or 2*rows
    return pl.pallas_call(partial(bwd_body,kb),
        grid=(G,),
        in_specs=[pl.BlockSpec(biast.shape,lambda i:(0,0)),
            pl.BlockSpec(lset.shape,lambda i:(0,0)),
            pl.BlockSpec((rows,128),lambda i:(mb,i)),
            pl.BlockSpec((rows,128),lambda i:(mb,G+i)),
            pl.BlockSpec((rows,128),lambda i:(mb,2*G+i)),
            pl.BlockSpec((nx,128),lambda i:(0,i)),
            pl.BlockSpec((nx,128),lambda i:(0,G+i)),
            pl.BlockSpec((rows,128),lambda i:(0,i)),
            pl.BlockSpec((rows,128),lambda i:(0,i))],
        out_specs=[pl.BlockSpec((rows,128),lambda i:(0,i)),pl.BlockSpec((2,rows,128),lambda i:(0,0,i)),pl.BlockSpec((2,nx,128),lambda i:(0,0,i))],
        out_shape=[jax.ShapeDtypeStruct((rows,D),bf),jax.ShapeDtypeStruct((2,rows,D),bf),jax.ShapeDtypeStruct((2,nx,D),bf)],
        cost_estimate=pl.CostEstimate(flops=flops*4,transcendentals=16*rows*(rows+nx),bytes_accessed=rows*D*30),
        name="attn_bwd")(biast,lset,joined,joined,joined,other,other,do,o)

C0=0.7978845608028654; C1=0.044715
def exp_body(capacity, x_ref, g_ref, wi_ref, wo_ref, *refs):
    act_ref, ig_ref, b_ref, s_ref, accr, accd = refs[-6:]
    f=pl.program_id(0)
    @pl.when(f==0)
    def _():
        size=g_ref.shape[2]
        eye=lax.broadcasted_iota(jnp.int32,(size,128),0)==lax.broadcasted_iota(jnp.int32,(size,128),1)
        for e in range(g_ref.shape[0]):
            at=e*size+capacity
            gate=x_ref[at:at+1,:128].astype(f32)+x_ref[at+1:at+2,:128].astype(f32)
            column=jnp.sum(jnp.where(eye,gate,0.0),axis=1,keepdims=True)
            s_ref[e*size:(e+1)*size,:]=(column*g_ref[e,0].astype(f32)).astype(bf)
    x=x_ref[...]; g=s_ref[...]; wi=wi_ref[...].reshape(x_ref.shape[1],wi_ref.shape[3]); wo=wo_ref[0,0]
    v=mm(x,wi,NN)
    ag=mm(g,wo,NT)
    v2=v*v
    t=jnp.tanh(C0*(v*(1.0+C1*v2)))
    h=0.5*(1.0+t)
    act=(v*h).astype(bf)
    dg=h+(0.5*C0)*v*(1.0-t*t)*(1.0+(3*C1)*v2)
    ig=(ag*dg).astype(bf)
    act_ref[...]=act; ig_ref[...]=ig
    r=mm(act,wo,NN); d=mm(ig,wi,NT)
    @pl.when(f==0)
    def _(): accr[...]=r; accd[...]=d
    @pl.when(f>0)
    def _(): accr[...]+=r; accd[...]+=d
    @pl.when(f==pl.num_programs(0)-1)
    def _():
        size=b_ref.shape[1]//2
        for e in range(b_ref.shape[0]):
            b_ref[e,:size,:]=accr[e*size:(e+1)*size,:].astype(bf)
            b_ref[e,size:,:]=accd[e*size:(e+1)*size,:].astype(bf)

def expert(x, g, weights, prev, mb, nmb, capacity):
    rows,D=x.shape; experts,_,size,_=g.shape; n,deep,_=weights.shape; part=deep//2; FF=part*n; fb=min(D,part); per=D//fb
    blk=pl.BlockSpec((rows,fb),lambda f:(mb,f))
    anyspec=pl.BlockSpec(memory_space=pl.ANY)
    ex=() if prev is None else prev
    return pl.pallas_call(partial(exp_body,capacity), grid=(FF//fb,),
        in_specs=[pl.BlockSpec((rows,D),lambda f:(0,0)),pl.BlockSpec((experts,1,size,D),lambda f:(0,mb,0,0)),
                  pl.BlockSpec((n,1,D//n,fb),lambda f:(0,f//per,0,f%per)),
                  pl.BlockSpec((1,1,fb,D),lambda f:(f//(part//fb),part//fb+f%(part//fb),0,0))]+[anyspec]*len(ex),
        out_specs=[blk,blk,pl.BlockSpec((experts,2*size,D),lambda f:(0,0,0)),pl.BlockSpec((rows,D),lambda f:(0,0))],
        out_shape=[jax.ShapeDtypeStruct((nmb*rows,FF),bf)]*2+[jax.ShapeDtypeStruct((experts,2*size,D),bf),jax.ShapeDtypeStruct((rows,D),bf)],
        scratch_shapes=[pltpu.VMEM((rows,D),f32)]*2,
        input_output_aliases={} if prev is None else {4:0,5:1},
        cost_estimate=pl.CostEstimate(flops=8*rows*D*FF,transcendentals=rows*FF,bytes_accessed=4*D*FF+4*rows*FF),
        name="expert")(x,g,weights.reshape(n,2*FF//D,D//n,D),weights.reshape(n,deep//fb,fb,D),*ex)

def in_grads_body(count, *refs):
    in_ref, turned=refs[-2:]; xs=refs[:count]; ig_ref=refs[count]
    n=in_ref.shape[0]; rows,D=xs[0].shape
    @pl.when(pl.program_id(0)==0)
    def _():
        turned[...]=jnp.concatenate([r[...] for r in xs],axis=0).T
    t=mm(turned[...],ig_ref[...],NN).astype(bf)
    for q in range(n): in_ref[q,0,:,:]=t[q*(D//n):(q+1)*(D//n),:]

def in_grads(xs, ig, n, fb=1024):
    rows,D=xs[0].shape; FF=ig.shape[1]; per=D//fb; count=len(xs)
    return pl.pallas_call(partial(in_grads_body,count), grid=(FF//fb,),
        in_specs=[pl.BlockSpec((rows,D),lambda f:(0,0))]*count+[pl.BlockSpec((count*rows,fb),lambda f:(0,f))],
        out_specs=pl.BlockSpec((n,1,D//n,fb),lambda f:(0,f//per,0,f%per)),
        out_shape=jax.ShapeDtypeStruct((n,FF//D,D//n,D),bf),
        scratch_shapes=[pltpu.VMEM((D,count*rows),bf)],
        cost_estimate=pl.CostEstimate(flops=2*count*rows*D*FF,transcendentals=0,bytes_accessed=2*D*FF+2*count*rows*FF),
        name="in_grads")(*xs,ig)

def out_grads_body(count, *refs):
    out_ref, stacked=refs[-2:]; gs=refs[:count]; act_ref=refs[count]; rows=gs[0].shape[0]
    @pl.when(pl.program_id(0)==0)
    def _():
        for m in range(count): stacked[m*rows:(m+1)*rows,:]=gs[m][...]
    out_ref[...]=mm(act_ref[...],stacked[...],TN).astype(bf)

def out_grads(gs, act, fb=1024):
    rows,D=gs[0].shape; FF=act.shape[1]; count=len(gs)
    return pl.pallas_call(partial(out_grads_body,count), grid=(FF//fb,),
        in_specs=[pl.BlockSpec((rows,D),lambda f:(0,0))]*count+[pl.BlockSpec((count*rows,fb),lambda f:(0,f))],
        out_specs=pl.BlockSpec((fb,D),lambda f:(f,0)),
        out_shape=jax.ShapeDtypeStruct((FF,D),bf),
        scratch_shapes=[pltpu.VMEM((count*rows,D),bf)],
        cost_estimate=pl.CostEstimate(flops=2*count*rows*D*FF,transcendentals=0,bytes_accessed=2*D*FF+2*count*rows*FF),
        name="out_grads")(*gs,act)

def project_body(count, parts, per, high_ref, x_ref, *refs):
    j=pl.program_id(0)
    joined_ref,*outs,turned=refs[-6:]
    half=outs[0].shape[0]
    @pl.when(j==0)
    def _(): turned[...]=x_ref[...].T
    rows=x_ref.shape[0]//count
    for m in range(count):
        own=refs[m*(2+parts):(m+1)*(2+parts)]
        @pl.when(j<per)
        def _(): joined_ref[m*rows:(m+1)*rows,:]=own[0][...]
        @pl.when(j>=per)
        def _():
            total=own[1][0].astype(f32)
            for r in own[2:]: total=total+r[0].astype(f32)
            joined_ref[m*rows:(m+1)*rows,:]=total.astype(bf)
    high=high_ref[0]
    right=joined_ref[...]
    send=mm(turned[pl.ds(pl.multiple_of((1-high)*half,half),half),:],right,NN).astype(bf)
    keep=mm(turned[pl.ds(pl.multiple_of(high*half,half),half),:],right,NN).astype(bf)
    middle=pl.num_programs(0)//2
    @pl.when(j<middle)
    def _(): outs[0][...]=keep; outs[1][...]=send
    @pl.when(j>=middle)
    def _(): outs[2][...]=keep; outs[3][...]=send

def project_grads(x, groups, high, fb=512):
    rows,D=x.shape; count=len(groups); R=rows//count; per=D//fb; parts=len(groups[0][2]); steps=3*per; middle=steps//2
    three=pl.BlockSpec((1,R,fb),lambda j,h:(jnp.maximum(j//per-1,0),0,jnp.where(j<per,0,j%per)))
    specs=[pl.BlockSpec((rows,D),lambda j,h:(0,0))]; args=[x]
    for dq,own,away in groups:
        specs+=[pl.BlockSpec((R,fb),lambda j,h:(0,jnp.minimum(j,per-1))),three]+[three]*parts
        args+=[dq,own]+list(away)
    early=pl.BlockSpec((D//2,fb),lambda j,h:(0,jnp.minimum(j,middle-1)))
    late=pl.BlockSpec((D//2,fb),lambda j,h:(0,jnp.maximum(j-middle,0)))
    return pl.pallas_call(partial(project_body,count,parts,per),
        grid_spec=pltpu.PrefetchScalarGridSpec(num_scalar_prefetch=1,grid=(steps,),in_specs=specs,
            out_specs=[pl.BlockSpec((rows,fb),lambda j,h:(0,j)),early,early,late,late],
            scratch_shapes=[pltpu.VMEM((D,rows),bf)]),
        out_shape=[jax.ShapeDtypeStruct((rows,3*D),bf)]+[jax.ShapeDtypeStruct((D//2,middle*fb),bf)]*4,
        cost_estimate=pl.CostEstimate(flops=6*rows*D*D,transcendentals=0,bytes_accessed=rows*D*16+6*D*D),
        name="project_grads")(high,*args)

def widen_body(counts, high_ref, *refs):
    outs=refs[len(refs)-len(counts):]; at=0
    for out_ref,count in zip(outs,counts):
        start=0
        for r in refs[at:at+count]:
            out_ref[:,start:start+r.shape[1]]=r[...].astype(f32); start+=r.shape[1]
        at+=count

def widen(groups, high, prev=()):
    half=groups[0][0].shape[0]; rb=half//2; flat=[v for g in groups for v in g]
    widths=[sum(v.shape[1] for v in g) for g in groups]
    return pl.pallas_call(partial(widen_body,[len(g) for g in groups]),
        grid_spec=pltpu.PrefetchScalarGridSpec(num_scalar_prefetch=1,grid=(2,),
            in_specs=[pl.BlockSpec((rb,v.shape[1]),lambda i,h:(i,0)) for v in flat]+[pl.BlockSpec(memory_space=pl.ANY)]*len(prev),
            out_specs=[pl.BlockSpec((rb,w),lambda i,h:(h[0]*2+i,0)) for w in widths]),
        out_shape=[jax.ShapeDtypeStruct((2*half,w),f32) for w in widths],
        input_output_aliases={1+len(flat)+k:k for k in range(len(prev))},
        cost_estimate=pl.CostEstimate(flops=half*sum(widths),transcendentals=0,bytes_accessed=half*sum(widths)*6),
        name="widen")(high,*flat,*prev)

def stack_body(in_ref, out_ref, both_ref):
    both_ref[0,0,:,:]=in_ref[...]; both_ref[1,0,:,:]=out_ref[...]

def stack(first, second):
    short,FF=first.shape; D=second.shape[1]; count=FF//D
    both=pl.pallas_call(stack_body, grid=(count,),
        in_specs=[pl.BlockSpec((short,D),lambda k:(0,k)),pl.BlockSpec((short,D),lambda k:(k,0))],
        out_specs=pl.BlockSpec((2,1,short,D),lambda k:(0,k,0,0)),
        out_shape=jax.ShapeDtypeStruct((2,count,short,D),bf),
        cost_estimate=pl.CostEstimate(flops=0,transcendentals=0,bytes_accessed=8*short*FF),
        name="stack")(first,second)
    return both.reshape(2*count*short,D)


HEADS = 16
EPS = 1e-05
HIGH = lax.Precision.HIGHEST


def layer_norm(values, gain, shift):
    center = values - jnp.mean(values, axis=-1, keepdims=True)
    scale = lax.rsqrt(jnp.mean(center * center, axis=-1, keepdims=True) + EPS)
    normal = center * scale
    return (normal * gain + shift, normal, scale)


def norm_back(grad, normal, scale, gain):
    scaled = grad * gain
    inner = (
        scaled
        - jnp.mean(scaled, axis=-1, keepdims=True)
        - normal * jnp.mean(scaled * normal, axis=-1, keepdims=True)
    )
    return (inner * scale, jnp.sum(grad * normal, axis=0), jnp.sum(grad, axis=0))


def swap(values, axis, bit):
    return lax.ppermute(values, axis, [(i, i ^ bit) for i in range(lax.axis_size(axis))])


def bits_of(axis):
    count = lax.axis_size(axis)
    assert count & (count - 1) == 0
    return [(axis, 1 << i) for i in range(count.bit_length() - 1)]


def cut(values, steps, slot):
    sent, kept = [], []
    for value, order in zip(values, steps):
        axis, bit = order[slot]
        high = (lax.axis_index(axis) // bit) % 2
        half = value.shape[0] // 2
        sent.append(lax.dynamic_slice_in_dim(value, (1 - high) * half, half))
        kept.append(lax.dynamic_slice_in_dim(value, high * half, half))
    return tuple(sent), tuple(kept)


def halve(values, steps, slot):
    sent, kept = cut(values, steps, slot)
    return [a + swap(b, *order[slot]) for a, b, order in zip(kept, sent, steps)]


def join(value, other, step):
    axis, bit = step
    high = (lax.axis_index(axis) // bit) % 2
    return jnp.concatenate(
        [jnp.where(high == 0, value, other), jnp.where(high == 0, other, value)], axis=0
    )


def double(values, steps, slot):
    sent = [swap(value, *order[slot]) for value, order in zip(values, steps)]
    return [join(v, o, order[slot]) for v, o, order in zip(values, sent, steps)]


def local(
    tokens,
    out_grad,
    seq_lengths,
    token_order,
    expert_route,
    mixer_gain,
    mixer_shift,
    project_in,
    project_out,
    expert_gain,
    expert_shift,
    router_weight,
    expert_in,
    expert_out,
):
    micro, rows, model = tokens.shape[0], tokens.shape[2], tokens.shape[3]
    contexts = lax.axis_size("context")
    here = lax.axis_index("context")
    experts = expert_in.shape[0] * lax.axis_size("expert")
    capacity = 9 * rows // (8 * experts)
    block = (capacity + 2 + 7) // 8 * 8
    slots = experts * block

    devices = contexts * lax.axis_size("dp")
    weights = lax.all_gather(stack(expert_in[0], expert_out[0]), ("context", "dp"), axis=0)

    router_float = router_weight.astype(f32)
    expert_ids = jnp.arange(experts, dtype=jnp.int32)
    slot_ids = jnp.arange(slots, dtype=jnp.int32)

    routes, ranks, places, place_two = [], [], [], []
    sent_grads = []
    for m in range(micro):
        route = expert_route[m, 0, :, 0]
        choose_int = (route[:, None] == expert_ids[None, :]).astype(jnp.int32)
        earlier = jnp.cumsum(choose_int, axis=0) - choose_int
        rank = jnp.sum(earlier * choose_int, axis=1)
        place = (route * block + rank)[None, :] == slot_ids[:, None]
        routes.append(route)
        ranks.append(rank)
        places.append(place.astype(bf))
        sent_grads.append(
            jnp.dot(places[m], out_grad[m, 0], preferred_element_type=f32)
            .astype(bf)
            .reshape(experts, 1, block, model)
        )
    sent_grads, tokens = lax.optimization_barrier((jnp.concatenate(sent_grads, axis=1), tokens))
    grads_there = lax.all_to_all(sent_grads, "expert", split_axis=0, concat_axis=0, tiled=True)

    flat = tokens.reshape(micro * rows, model)
    normed, normal_one, scale_one = layer_norm(flat.astype(f32), mixer_gain, mixer_shift)
    normed_low = lax.optimization_barrier(normed.astype(bf))
    joined = jnp.dot(normed_low, project_in, preferred_element_type=f32).astype(bf)
    others, biases = [], []
    for m in range(micro):
        pairs = joined[m * rows : (m + 1) * rows, model:]
        parts = [
            lax.ppermute(pairs, "context", [(i, (i + s) % contexts) for i in range(contexts)])
            for s in range(1, contexts)
        ]
        others.append(parts[0] if contexts == 2 else jnp.concatenate(parts, axis=0))
        positions = token_order[m, 0]
        ends = jnp.cumsum(seq_lengths[m, 0])
        segments = jnp.sum((positions[:, None] >= ends[None, :]).astype(jnp.int32), axis=1)
        owners = [(here - s + contexts) % contexts for s in range(contexts)]
        key_positions = jnp.concatenate(
            [lax.dynamic_slice_in_dim(positions, o * rows, rows) for o in owners]
        )
        key_segments = jnp.concatenate(
            [lax.dynamic_slice_in_dim(segments, o * rows, rows) for o in owners]
        )
        query_positions, query_segments = key_positions[:rows], key_segments[:rows]
        biases.append(
            (
                jnp.where(
                    (key_positions[None, :] <= query_positions[:, None])
                    & (key_segments[None, :] == query_segments[:, None]),
                    0.0,
                    -1e30,
                ).astype(f32),
                (key_positions, key_segments),
            )
        )

    saved = []
    before = grads_there
    for m in range(micro):
        attended, mixed_low, lse = attn_fwd(joined, others[m], biases[m][0], m)
        log_total = lse[:, :HEADS].T
        middle = flat[m * rows : (m + 1) * rows].astype(f32) + jnp.dot(
            mixed_low, project_out, preferred_element_type=f32
        )
        second, normal_two, scale_two = layer_norm(middle, expert_gain, expert_shift)
        second_low = second.astype(bf)
        shares = jax.nn.softmax(
            jnp.dot(second_low, router_weight, preferred_element_type=f32), axis=-1
        )
        choose_float = (routes[m][:, None] == expert_ids[None, :]).astype(f32)
        gate = jnp.sum(shares * choose_float, axis=1)
        gate_high = gate.astype(bf)
        gate_low = (gate - gate_high.astype(f32)).astype(bf)
        slot_expert, slot_row = slot_ids // block, slot_ids % block
        mine = slot_expert[:, None] == routes[m][None, :]
        gates = jnp.where(
            mine & (slot_row == capacity)[:, None],
            gate_high[None, :],
            jnp.where(mine & (slot_row == capacity + 1)[:, None], gate_low[None, :], jnp.zeros((), bf)),
        )
        ladder = (ranks[m][:, None] == jnp.arange(model, dtype=jnp.int32)[None, :]).astype(bf)
        sent = jnp.dot(
            jnp.concatenate([places[m], gates], axis=1),
            jnp.concatenate([second_low, ladder], axis=0),
            preferred_element_type=f32,
        ).astype(bf)
        if m + 1 < micro:
            sent, others[m + 1] = lax.optimization_barrier((sent, others[m + 1]))
        if m + 1 == micro:
            logs = tuple(state[2] for state in saved) + (log_total,)
            attended, targets, places_in_pack, logs = lax.optimization_barrier(
                (attended, tuple(r * (2 * block) + k for r, k in zip(routes, ranks)),
                 tuple(b[1] for b in biases), logs)
            )
            wide = jnp.arange(2 * slots, dtype=jnp.int32)[:, None]
            place_two = [
                ((t[None, :] == wide).astype(bf), (t[None, :] + block == wide).astype(bf))
                for t in targets
            ]
            turned = [
                jnp.where(
                    (p[:, None] <= p[None, :rows]) & (g[:, None] == g[None, :rows]), 0.0, -1e30
                ).astype(f32)
                for p, g in places_in_pack
            ]
            sent, logs, turned, place_two = lax.optimization_barrier(
                (sent, logs, turned, place_two)
            )
            place_two = list(place_two)
            log_total = logs[-1]
            for n in range(m):
                saved[n][2] = logs[n]
            biases = [(b[0], t) for b, t in zip(biases, turned)]
        sent, before = lax.optimization_barrier((sent, before))
        if m == 0:
            grads_there = before
        else:
            saved[m - 1][-1] = before
        there = lax.all_to_all(
            sent.reshape(experts, block, model), "expert", split_axis=0, concat_axis=0, tiled=True
        )
        before = there
        saved.append(
            [attended, mixed_low, log_total, middle, second_low, normal_two, scale_two, shares,
             choose_float, gate, there]
        )

    kept = None
    rows_there, scaled_there, returned = [], [], []
    for m in range(micro):
        there = saved[m][-1]
        there = there.reshape(slots, model)
        active, inner_grad, back, scaled = expert(
            there, grads_there, weights, kept, m, micro, capacity
        )
        if m + 1 < micro:
            back, saved[m + 1][-1] = lax.optimization_barrier((back, saved[m + 1][-1]))
        kept = (active, inner_grad)
        rows_there.append(there)
        scaled_there.append(scaled)
        returned.append(
            lax.all_to_all(back, "expert", split_axis=0, concat_axis=0, tiled=True).reshape(
                2 * slots, model
            )
        )
    active, inner_grad = kept
    out_term = out_grads(scaled_there, active)
    out_term, inner_grad, returned[0] = lax.optimization_barrier((out_term, inner_grad, returned[0]))
    grad_out_weight = lax.psum_scatter(
        out_term, ("context", "dp"), scatter_dimension=0, tiled=True
    )

    outputs, middle_grads, branches, groups = [], [], [], []
    small = None
    for m in range(micro):
        (attended, mixed_low, log_total, middle, second_low, normal_two, scale_two, shares,
         choose_float, gate, _) = saved[m]
        grad_out = out_grad[m, 0].astype(f32)
        picked = lax.dot_general(place_two[m][0], returned[m], TN, preferred_element_type=f32)
        outputs.append((middle + gate[:, None] * picked).astype(bf))
        gate_grad = jnp.sum(grad_out * picked, axis=1)
        logit_grad = gate_grad[:, None] * gate[:, None] * (choose_float - shares)
        router_term = jnp.einsum("td,te->de", second_low.astype(f32), logit_grad, precision=HIGH)
        second_grad = jnp.einsum("te,de->td", logit_grad, router_float, precision=HIGH)
        second_grad = second_grad + lax.dot_general(
            place_two[m][1], returned[m], TN, preferred_element_type=f32
        )
        middle_part, gain_two, shift_two = norm_back(second_grad, normal_two, scale_two, expert_gain)
        middle_grad = grad_out + middle_part
        branch = middle_grad.astype(bf)
        mixed_grad = lax.dot_general(branch, project_out, NT, preferred_element_type=f32).astype(bf)
        query_grad, own, away = attn_bwd(
            joined, others[m], biases[m][1], log_total, mixed_grad, attended, m
        )
        parts = [
            lax.ppermute(
                away[:, (s - 1) * rows : s * rows] if contexts > 2 else away,
                "context",
                [(i, (i - s) % contexts) for i in range(contexts)],
            )
            for s in range(1, contexts)
        ]
        groups.append([query_grad, own, parts])
        if m == 0:
            inner_grad, query_grad = lax.optimization_barrier((inner_grad, query_grad))
            in_term = in_grads(rows_there, inner_grad, devices)
        if m + 1 < micro:
            in_term, query_grad, place_two[m + 1] = lax.optimization_barrier(
                (in_term, query_grad, place_two[m + 1])
            )
            groups[m][0] = query_grad
        middle_grads.append(middle_grad)
        branches.append(branch)
        terms = (gain_two, shift_two, router_term)
        small = terms if small is None else tuple(a + b for a, b in zip(small, terms))

    mixed_all = jnp.concatenate([s[1] for s in saved], axis=0)
    out_sum = lax.dot_general(
        mixed_all, jnp.concatenate(branches, axis=0), TN, preferred_element_type=f32
    ).astype(bf)
    near, expert_bits, dp_bits = bits_of("context"), bits_of("expert"), bits_of("dp")
    sent, kept = cut([out_sum], [near], 0)
    sent, kept, groups[-1][2][0] = lax.optimization_barrier((sent, kept, groups[-1][2][0]))
    out_half = kept[0] + swap(sent[0], *near[0])
    high = (here % 2).astype(jnp.int32).reshape(1)
    joined_grad, kept, sent, kept_too, sent_too = project_grads(normed_low, groups, high)
    kept, in_term, grad_out_weight, out_half = lax.optimization_barrier(
        (kept, in_term, grad_out_weight, out_half)
    )
    grad_in = lax.psum_scatter(in_term, ("context", "dp"), scatter_dimension=0, tiled=True)[0]
    halves = [kept + swap(sent, *near[0]), kept_too + swap(sent_too, *near[0])]
    halves.append(out_half)
    for slot in range(1, len(near)):
        halves = halve(halves, [near] * 3, slot)
    chunks = tuple(halves)

    orders = (
        expert_bits[:1] + dp_bits + expert_bits[1:],
        expert_bits[1:2] + expert_bits[:1] + dp_bits + expert_bits[2:],
        dp_bits + expert_bits[1:] + expert_bits[:1],
    )
    count = len(orders[0])
    steps = near + dp_bits + expert_bits
    for slot in range(count - 1):
        chunks = halve(chunks, orders, slot)
        if slot == 0:
            chunks, joined_grad = lax.optimization_barrier((chunks, joined_grad))
            normed_grad = lax.dot_general(joined_grad, project_in, NT, preferred_element_type=f32)
            input_part, gain_one, shift_one = norm_back(normed_grad, normal_one, scale_one, mixer_gain)
            grad_tokens = jnp.concatenate(middle_grads, axis=0) + input_part
            small = jnp.concatenate(
                [gain_one[None], shift_one[None], small[0][None], small[1][None], small[2].T], axis=0
            )
        elif slot == 1:
            chunks, small, grad_tokens = lax.optimization_barrier((chunks, small, grad_tokens))
        else:
            chunks = lax.optimization_barrier(chunks)
    for step in steps:
        small = small + swap(small, *step)
    chunks = lax.optimization_barrier(
        tuple(chunk + swap(chunk, *order[-1]) for chunk, order in zip(chunks, orders))
    )
    for slot in reversed(range(count - 1)):
        chunks = double(chunks, orders, slot)
        if slot == 1:
            chunks, small = lax.optimization_barrier((tuple(chunks), small))
        else:
            chunks = lax.optimization_barrier(tuple(chunks))
        if slot == count - 2:
            chunks, grad_in, grad_out_weight = lax.optimization_barrier(
                (chunks, grad_in, grad_out_weight)
            )
            grad_in = jnp.concatenate([grad_in[k] for k in range(grad_in.shape[0])], axis=1).astype(f32)
            grad_out_weight = grad_out_weight.astype(f32)
        if slot == 1:
            chunks, grad_in, grad_out_weight = lax.optimization_barrier(
                (chunks, grad_in, grad_out_weight)
            )
    for slot in reversed(range(1, len(near))):
        chunks = double(chunks, (near,) * 3, slot)
    arrived = [swap(chunk, *near[0]) for chunk in chunks]
    in_sum, out_sum = widen((chunks[:2], chunks[2:]), high)
    arrived, out_sum, in_sum = lax.optimization_barrier((arrived, out_sum, in_sum))
    in_sum, out_sum = widen((arrived[:2], arrived[2:]), 1 - high, (in_sum, out_sum))
    return (
        jnp.stack(outputs)[:, None],
        grad_tokens.reshape(micro, 1, rows, model),
        small[0],
        small[1],
        in_sum,
        out_sum,
        small[2],
        small[3],
        small[4:].T,
        grad_in[None],
        grad_out_weight[None],
    )


def solution(mesh):
    tokens = P(None, ("expert", "dp"), "context", None)
    packs = P(None, ("expert", "dp"), None)
    weights = P("expert", ("context", "dp"), None)
    in_specs = (tokens, tokens, packs, packs, tokens) + (P(),) * 7 + (weights, weights)
    out_specs = (tokens, tokens) + (P(),) * 7 + (weights, weights)
    return jax.shard_map(local, mesh=mesh, in_specs=in_specs, out_specs=out_specs, check_vma=False)
```

```python
from functools import partial

import jax
import jax.numpy as jnp
from jax import lax
from jax.sharding import PartitionSpec as P
from jax.experimental import pallas as pl
from jax.experimental.pallas import tpu as pltpu
bf=jnp.bfloat16; f32=jnp.float32
NT=(((1,),(1,)),((),()))
TN=(((0,),(0,)),((),()))
NN=(((1,),(0,)),((),()))
def mm(a,b,dims): return lax.dot_general(a,b,dims,preferred_element_type=f32)

def fwd_body(rb, bias_ref, q_ref, ko_ref, vo_ref, kx_ref, vx_ref, o_ref, ol_ref, lse_ref):
    i=pl.program_id(0)
    rows=q_ref.shape[0]
    lane=lax.broadcasted_iota(jnp.int32,(1,128),1)
    masks=[(lane<64).astype(bf)*0.125,(lane>=64).astype(bf)*0.125]
    ko=ko_ref[...]; vo=vo_ref[...]; kx=kx_ref[...]; vx=vx_ref[...]
    for r in range(0,rows,rb):
        q=q_ref[r:r+rb,:]
        bo=bias_ref[r:r+rb,:rows]; bx=bias_ref[r:r+rb,rows:]
        outs=[]
        old=lse_ref[r:r+rb,:]
        for j in range(2):
            qj=q*masks[j]
            so=mm(qj,ko,NT)+bo
            sx=mm(qj,kx,NT)+bx
            m=jnp.maximum(jnp.max(so,-1,keepdims=True),jnp.max(sx,-1,keepdims=True))
            po=jnp.exp(so-m); px=jnp.exp(sx-m)
            l=jnp.sum(po,-1,keepdims=True)+jnp.sum(px,-1,keepdims=True)
            w=mm(po.astype(bf),vo,NN)+mm(px.astype(bf),vx,NN)
            outs.append(w/l)
            old=jnp.where(lane==2*i+j,m+jnp.log(l),old)
        lse_ref[r:r+rb,:]=old
        o=jnp.where(lane<64,outs[0],outs[1])
        o_ref[r:r+rb,:]=o
        ol_ref[r:r+rb,:]=o.astype(bf)

def attn_fwd(joined, other, bias, mb, rb=None):
    rows=bias.shape[0]; nx=other.shape[0]; D=other.shape[1]//2; G=D//128
    flops=4*rows*(rows+nx)*D
    rb=rb or rows
    return pl.pallas_call(partial(fwd_body,rb),
        grid=(G,),
        in_specs=[pl.BlockSpec(bias.shape,lambda i:(0,0)),
            pl.BlockSpec((rows,128),lambda i:(mb,i)),
            pl.BlockSpec((rows,128),lambda i:(mb,G+i)),
            pl.BlockSpec((rows,128),lambda i:(mb,2*G+i)),
            pl.BlockSpec((nx,128),lambda i:(0,i)),
            pl.BlockSpec((nx,128),lambda i:(0,G+i))],
        out_specs=[pl.BlockSpec((rows,128),lambda i:(0,i)),pl.BlockSpec((rows,128),lambda i:(0,i)),pl.BlockSpec((rows,128),lambda i:(0,0))],
        out_shape=[jax.ShapeDtypeStruct((rows,D),f32),jax.ShapeDtypeStruct((rows,D),bf),jax.ShapeDtypeStruct((rows,128),f32)],
        cost_estimate=pl.CostEstimate(flops=rows,transcendentals=0,bytes_accessed=rows),
        name="attn_fwd")(bias,joined,joined,joined,other,other)

def bwd_body(kb, biast_ref, lse_ref, q_ref, ko_ref, vo_ref, kx_ref, vx_ref, do_ref, o_ref, dq_ref, dko_ref, dx_ref):
    i=pl.program_id(0)
    rows=q_ref.shape[0]; nx=kx_ref.shape[0]
    lane=lax.broadcasted_iota(jnp.int32,(1,128),1)
    masks=[(lane<64).astype(bf),(lane>=64).astype(bf)]
    q=q_ref[...]; do=do_ref[...]
    prod=do.astype(f32)*o_ref[...]
    q2=jnp.concatenate([q*(m*0.125) for m in masks],axis=0)
    do2=jnp.concatenate([do*m for m in masks],axis=0)
    sel=(lax.broadcasted_iota(jnp.int32,(8,128),1)//64==lax.broadcasted_iota(jnp.int32,(8,128),0)).astype(f32)
    delta=lax.dot_general(sel,prod,NT,precision=lax.Precision.HIGHEST,preferred_element_type=f32)
    delta=jnp.concatenate([delta[0:1,:],delta[1:2,:]],axis=1)
    lse=jnp.concatenate([lse_ref[pl.ds(2*i+j,1),:] for j in range(2)],axis=1)
    ks=jnp.concatenate([ko_ref[...],kx_ref[...]],axis=0)
    vs=jnp.concatenate([vo_ref[...],vx_ref[...]],axis=0)
    dq=None
    for b in range(0,rows+nx,kb):
        k=ks[b:b+kb,:]; v=vs[b:b+kb,:]
        bt=biast_ref[b:b+kb,:]
        s=mm(k,q2,NT)+jnp.concatenate([bt,bt],axis=1)
        p=jnp.exp(s-lse)
        dp=mm(v,do2,NT)
        ds=(p*(dp-delta)).astype(bf)
        dv=mm(p.astype(bf),do2,NN).astype(bf)
        dk=mm(ds,q2,NN).astype(bf)
        e=mm(k,ds,TN)
        dq=e if dq is None else dq+e
        cut=min(max(rows-b,0),kb)
        if cut:
            dko_ref[0,b:b+cut,:]=dk[:cut]; dko_ref[1,b:b+cut,:]=dv[:cut]
        if cut<kb:
            at=b+cut-rows
            dx_ref[0,at:at+kb-cut,:]=dk[cut:]; dx_ref[1,at:at+kb-cut,:]=dv[cut:]
    dq=dq.T
    dq_ref[...]=(jnp.where(lane<64,dq[:rows],dq[rows:])*0.125).astype(bf)

def attn_bwd(joined, other, biast, lset, do, o, mb, kb=None):
    rows=biast.shape[1]; nx=other.shape[0]; D=other.shape[1]//2; G=D//128
    flops=10*rows*(rows+nx)*D
    kb=kb or 2*rows
    return pl.pallas_call(partial(bwd_body,kb),
        grid=(G,),
        in_specs=[pl.BlockSpec(biast.shape,lambda i:(0,0)),
            pl.BlockSpec(lset.shape,lambda i:(0,0)),
            pl.BlockSpec((rows,128),lambda i:(mb,i)),
            pl.BlockSpec((rows,128),lambda i:(mb,G+i)),
            pl.BlockSpec((rows,128),lambda i:(mb,2*G+i)),
            pl.BlockSpec((nx,128),lambda i:(0,i)),
            pl.BlockSpec((nx,128),lambda i:(0,G+i)),
            pl.BlockSpec((rows,128),lambda i:(0,i)),
            pl.BlockSpec((rows,128),lambda i:(0,i))],
        out_specs=[pl.BlockSpec((rows,128),lambda i:(0,i)),pl.BlockSpec((2,rows,128),lambda i:(0,0,i)),pl.BlockSpec((2,nx,128),lambda i:(0,0,i))],
        out_shape=[jax.ShapeDtypeStruct((rows,D),bf),jax.ShapeDtypeStruct((2,rows,D),bf),jax.ShapeDtypeStruct((2,nx,D),bf)],
        cost_estimate=pl.CostEstimate(flops=flops*4,transcendentals=16*rows*(rows+nx),bytes_accessed=rows*D*30),
        name="attn_bwd")(biast,lset,joined,joined,joined,other,other,do,o)

C0=0.7978845608028654; C1=0.044715
def exp_body(capacity, x_ref, g_ref, wi_ref, wo_ref, *refs):
    act_ref, ig_ref, b_ref, s_ref, accr, accd = refs[-6:]
    f=pl.program_id(0)
    @pl.when(f==0)
    def _():
        size=g_ref.shape[2]
        eye=lax.broadcasted_iota(jnp.int32,(size,128),0)==lax.broadcasted_iota(jnp.int32,(size,128),1)
        for e in range(g_ref.shape[0]):
            at=e*size+capacity
            gate=x_ref[at:at+1,:128].astype(f32)+x_ref[at+1:at+2,:128].astype(f32)
            column=jnp.sum(jnp.where(eye,gate,0.0),axis=1,keepdims=True)
            s_ref[e*size:(e+1)*size,:]=(column*g_ref[e,0].astype(f32)).astype(bf)
    x=x_ref[...]; g=s_ref[...]; wi=wi_ref[...].reshape(x_ref.shape[1],wi_ref.shape[3]); wo=wo_ref[0,0]
    v=mm(x,wi,NN)
    ag=mm(g,wo,NT)
    v2=v*v
    t=jnp.tanh(C0*(v*(1.0+C1*v2)))
    h=0.5*(1.0+t)
    act=(v*h).astype(bf)
    dg=h+(0.5*C0)*v*(1.0-t*t)*(1.0+(3*C1)*v2)
    ig=(ag*dg).astype(bf)
    act_ref[...]=act; ig_ref[...]=ig
    r=mm(act,wo,NN); d=mm(ig,wi,NT)
    @pl.when(f==0)
    def _(): accr[...]=r; accd[...]=d
    @pl.when(f>0)
    def _(): accr[...]+=r; accd[...]+=d
    @pl.when(f==pl.num_programs(0)-1)
    def _():
        size=b_ref.shape[1]//2
        for e in range(b_ref.shape[0]):
            b_ref[e,:size,:]=accr[e*size:(e+1)*size,:].astype(bf)
            b_ref[e,size:,:]=accd[e*size:(e+1)*size,:].astype(bf)

def expert(x, g, weights, prev, mb, nmb, capacity):
    rows,D=x.shape; experts,_,size,_=g.shape; n,deep,_=weights.shape; part=deep//2; FF=part*n; fb=min(D,part); per=D//fb
    blk=pl.BlockSpec((rows,fb),lambda f:(mb,f))
    anyspec=pl.BlockSpec(memory_space=pl.ANY)
    ex=() if prev is None else prev
    return pl.pallas_call(partial(exp_body,capacity), grid=(FF//fb,),
        in_specs=[pl.BlockSpec((rows,D),lambda f:(0,0)),pl.BlockSpec((experts,1,size,D),lambda f:(0,mb,0,0)),
                  pl.BlockSpec((n,1,D//n,fb),lambda f:(0,f//per,0,f%per)),
                  pl.BlockSpec((1,1,fb,D),lambda f:(f//(part//fb),part//fb+f%(part//fb),0,0))]+[anyspec]*len(ex),
        out_specs=[blk,blk,pl.BlockSpec((experts,2*size,D),lambda f:(0,0,0)),pl.BlockSpec((rows,D),lambda f:(0,0))],
        out_shape=[jax.ShapeDtypeStruct((nmb*rows,FF),bf)]*2+[jax.ShapeDtypeStruct((experts,2*size,D),bf),jax.ShapeDtypeStruct((rows,D),bf)],
        scratch_shapes=[pltpu.VMEM((rows,D),f32)]*2,
        input_output_aliases={} if prev is None else {4:0,5:1},
        cost_estimate=pl.CostEstimate(flops=8*rows*D*FF,transcendentals=rows*FF,bytes_accessed=4*D*FF+4*rows*FF),
        name="expert")(x,g,weights.reshape(n,2*FF//D,D//n,D),weights.reshape(n,deep//fb,fb,D),*ex)

def in_grads_body(count, *refs):
    in_ref, turned=refs[-2:]; xs=refs[:count]; ig_ref=refs[count]
    n=in_ref.shape[0]; rows,D=xs[0].shape
    @pl.when(pl.program_id(0)==0)
    def _():
        turned[...]=jnp.concatenate([r[...] for r in xs],axis=0).T
    t=mm(turned[...],ig_ref[...],NN).astype(bf)
    for q in range(n): in_ref[q,0,:,:]=t[q*(D//n):(q+1)*(D//n),:]

def in_grads(xs, ig, n, fb=1024):
    rows,D=xs[0].shape; FF=ig.shape[1]; per=D//fb; count=len(xs)
    return pl.pallas_call(partial(in_grads_body,count), grid=(FF//fb,),
        in_specs=[pl.BlockSpec((rows,D),lambda f:(0,0))]*count+[pl.BlockSpec((count*rows,fb),lambda f:(0,f))],
        out_specs=pl.BlockSpec((n,1,D//n,fb),lambda f:(0,f//per,0,f%per)),
        out_shape=jax.ShapeDtypeStruct((n,FF//D,D//n,D),bf),
        scratch_shapes=[pltpu.VMEM((D,count*rows),bf)],
        cost_estimate=pl.CostEstimate(flops=2*count*rows*D*FF,transcendentals=0,bytes_accessed=2*D*FF+2*count*rows*FF),
        name="in_grads")(*xs,ig)

def out_grads_body(count, *refs):
    out_ref, stacked=refs[-2:]; gs=refs[:count]; act_ref=refs[count]; rows=gs[0].shape[0]
    @pl.when(pl.program_id(0)==0)
    def _():
        for m in range(count): stacked[m*rows:(m+1)*rows,:]=gs[m][...]
    out_ref[...]=mm(act_ref[...],stacked[...],TN).astype(bf)

def out_grads(gs, act, fb=1024):
    rows,D=gs[0].shape; FF=act.shape[1]; count=len(gs)
    return pl.pallas_call(partial(out_grads_body,count), grid=(FF//fb,),
        in_specs=[pl.BlockSpec((rows,D),lambda f:(0,0))]*count+[pl.BlockSpec((count*rows,fb),lambda f:(0,f))],
        out_specs=pl.BlockSpec((fb,D),lambda f:(f,0)),
        out_shape=jax.ShapeDtypeStruct((FF,D),bf),
        scratch_shapes=[pltpu.VMEM((count*rows,D),bf)],
        cost_estimate=pl.CostEstimate(flops=2*count*rows*D*FF,transcendentals=0,bytes_accessed=2*D*FF+2*count*rows*FF),
        name="out_grads")(*gs,act)

def project_body(count, parts, per, high_ref, x_ref, *refs):
    j=pl.program_id(0)
    joined_ref,*outs,turned=refs[-6:]
    half=outs[0].shape[0]
    @pl.when(j==0)
    def _(): turned[...]=x_ref[...].T
    rows=x_ref.shape[0]//count
    for m in range(count):
        own=refs[m*(2+parts):(m+1)*(2+parts)]
        @pl.when(j<per)
        def _(): joined_ref[m*rows:(m+1)*rows,:]=own[0][...]
        @pl.when(j>=per)
        def _():
            total=own[1][0].astype(f32)
            for r in own[2:]: total=total+r[0].astype(f32)
            joined_ref[m*rows:(m+1)*rows,:]=total.astype(bf)
    high=high_ref[0]
    right=joined_ref[...]
    send=mm(turned[pl.ds(pl.multiple_of((1-high)*half,half),half),:],right,NN).astype(bf)
    keep=mm(turned[pl.ds(pl.multiple_of(high*half,half),half),:],right,NN).astype(bf)
    middle=pl.num_programs(0)//2
    @pl.when(j<middle)
    def _(): outs[0][...]=keep; outs[1][...]=send
    @pl.when(j>=middle)
    def _(): outs[2][...]=keep; outs[3][...]=send

def project_grads(x, groups, high, fb=512):
    rows,D=x.shape; count=len(groups); R=rows//count; per=D//fb; parts=len(groups[0][2]); steps=3*per; middle=steps//2
    three=pl.BlockSpec((1,R,fb),lambda j,h:(jnp.maximum(j//per-1,0),0,jnp.where(j<per,0,j%per)))
    specs=[pl.BlockSpec((rows,D),lambda j,h:(0,0))]; args=[x]
    for dq,own,away in groups:
        specs+=[pl.BlockSpec((R,fb),lambda j,h:(0,jnp.minimum(j,per-1))),three]+[three]*parts
        args+=[dq,own]+list(away)
    early=pl.BlockSpec((D//2,fb),lambda j,h:(0,jnp.minimum(j,middle-1)))
    late=pl.BlockSpec((D//2,fb),lambda j,h:(0,jnp.maximum(j-middle,0)))
    return pl.pallas_call(partial(project_body,count,parts,per),
        grid_spec=pltpu.PrefetchScalarGridSpec(num_scalar_prefetch=1,grid=(steps,),in_specs=specs,
            out_specs=[pl.BlockSpec((rows,fb),lambda j,h:(0,j)),early,early,late,late],
            scratch_shapes=[pltpu.VMEM((D,rows),bf)]),
        out_shape=[jax.ShapeDtypeStruct((rows,3*D),bf)]+[jax.ShapeDtypeStruct((D//2,middle*fb),bf)]*4,
        cost_estimate=pl.CostEstimate(flops=6*rows*D*D,transcendentals=0,bytes_accessed=rows*D*16+6*D*D),
        name="project_grads")(high,*args)

def widen_body(counts, high_ref, *refs):
    outs=refs[len(refs)-len(counts):]; at=0
    for out_ref,count in zip(outs,counts):
        start=0
        for r in refs[at:at+count]:
            out_ref[:,start:start+r.shape[1]]=r[...].astype(f32); start+=r.shape[1]
        at+=count

def widen(groups, high, prev=()):
    half=groups[0][0].shape[0]; rb=half//2; flat=[v for g in groups for v in g]
    widths=[sum(v.shape[1] for v in g) for g in groups]
    return pl.pallas_call(partial(widen_body,[len(g) for g in groups]),
        grid_spec=pltpu.PrefetchScalarGridSpec(num_scalar_prefetch=1,grid=(2,),
            in_specs=[pl.BlockSpec((rb,v.shape[1]),lambda i,h:(i,0)) for v in flat]+[pl.BlockSpec(memory_space=pl.ANY)]*len(prev),
            out_specs=[pl.BlockSpec((rb,w),lambda i,h:(h[0]*2+i,0)) for w in widths]),
        out_shape=[jax.ShapeDtypeStruct((2*half,w),f32) for w in widths],
        input_output_aliases={1+len(flat)+k:k for k in range(len(prev))},
        cost_estimate=pl.CostEstimate(flops=half*sum(widths),transcendentals=0,bytes_accessed=half*sum(widths)*6),
        name="widen")(high,*flat,*prev)

def stack_body(in_ref, out_ref, both_ref):
    both_ref[0,0,:,:]=in_ref[...]; both_ref[1,0,:,:]=out_ref[...]

def stack(first, second):
    short,FF=first.shape; D=second.shape[1]; count=FF//D
    both=pl.pallas_call(stack_body, grid=(count,),
        in_specs=[pl.BlockSpec((short,D),lambda k:(0,k)),pl.BlockSpec((short,D),lambda k:(k,0))],
        out_specs=pl.BlockSpec((2,1,short,D),lambda k:(0,k,0,0)),
        out_shape=jax.ShapeDtypeStruct((2,count,short,D),bf),
        cost_estimate=pl.CostEstimate(flops=0,transcendentals=0,bytes_accessed=8*short*FF),
        name="stack")(first,second)
    return both.reshape(2*count*short,D)


HEADS = 16
EPS = 1e-05
HIGH = lax.Precision.HIGHEST


def layer_norm(values, gain, shift):
    center = values - jnp.mean(values, axis=-1, keepdims=True)
    scale = lax.rsqrt(jnp.mean(center * center, axis=-1, keepdims=True) + EPS)
    normal = center * scale
    return (normal * gain + shift, normal, scale)


def norm_back(grad, normal, scale, gain):
    scaled = grad * gain
    inner = (
        scaled
        - jnp.mean(scaled, axis=-1, keepdims=True)
        - normal * jnp.mean(scaled * normal, axis=-1, keepdims=True)
    )
    return (inner * scale, jnp.sum(grad * normal, axis=0), jnp.sum(grad, axis=0))


def swap(values, axis, bit):
    return lax.ppermute(values, axis, [(i, i ^ bit) for i in range(lax.axis_size(axis))])


def bits_of(axis):
    count = lax.axis_size(axis)
    assert count & (count - 1) == 0
    return [(axis, 1 << i) for i in range(count.bit_length() - 1)]


def cut(values, steps, slot):
    sent, kept = [], []
    for value, order in zip(values, steps):
        axis, bit = order[slot]
        high = (lax.axis_index(axis) // bit) % 2
        half = value.shape[0] // 2
        sent.append(lax.dynamic_slice_in_dim(value, (1 - high) * half, half))
        kept.append(lax.dynamic_slice_in_dim(value, high * half, half))
    return tuple(sent), tuple(kept)


def halve(values, steps, slot):
    sent, kept = cut(values, steps, slot)
    return [a + swap(b, *order[slot]) for a, b, order in zip(kept, sent, steps)]


def join(value, other, step):
    axis, bit = step
    high = (lax.axis_index(axis) // bit) % 2
    return jnp.concatenate(
        [jnp.where(high == 0, value, other), jnp.where(high == 0, other, value)], axis=0
    )


def double(values, steps, slot):
    sent = [swap(value, *order[slot]) for value, order in zip(values, steps)]
    return [join(v, o, order[slot]) for v, o, order in zip(values, sent, steps)]


def local(
    tokens,
    out_grad,
    seq_lengths,
    token_order,
    expert_route,
    mixer_gain,
    mixer_shift,
    project_in,
    project_out,
    expert_gain,
    expert_shift,
    router_weight,
    expert_in,
    expert_out,
):
    micro, rows, model = tokens.shape[0], tokens.shape[2], tokens.shape[3]
    contexts = lax.axis_size("context")
    here = lax.axis_index("context")
    experts = expert_in.shape[0] * lax.axis_size("expert")
    capacity = 9 * rows // (8 * experts)
    block = (capacity + 2 + 7) // 8 * 8
    slots = experts * block

    devices = contexts * lax.axis_size("dp")
    weights = lax.all_gather(stack(expert_in[0], expert_out[0]), ("context", "dp"), axis=0)

    router_float = router_weight.astype(f32)
    expert_ids = jnp.arange(experts, dtype=jnp.int32)
    slot_ids = jnp.arange(slots, dtype=jnp.int32)

    routes, ranks, places, place_two = [], [], [], []
    sent_grads = []
    for m in range(micro):
        route = expert_route[m, 0, :, 0]
        choose_int = (route[:, None] == expert_ids[None, :]).astype(jnp.int32)
        earlier = jnp.cumsum(choose_int, axis=0) - choose_int
        rank = jnp.sum(earlier * choose_int, axis=1)
        place = (route * block + rank)[None, :] == slot_ids[:, None]
        routes.append(route)
        ranks.append(rank)
        places.append(place.astype(bf))
        sent_grads.append(
            jnp.dot(places[m], out_grad[m, 0], preferred_element_type=f32)
            .astype(bf)
            .reshape(experts, 1, block, model)
        )
    sent_grads, tokens = lax.optimization_barrier((jnp.concatenate(sent_grads, axis=1), tokens))
    grads_there = lax.all_to_all(sent_grads, "expert", split_axis=0, concat_axis=0, tiled=True)

    flat = tokens.reshape(micro * rows, model)
    normed, normal_one, scale_one = layer_norm(flat.astype(f32), mixer_gain, mixer_shift)
    normed_low = lax.optimization_barrier(normed.astype(bf))
    joined = jnp.dot(normed_low, project_in, preferred_element_type=f32).astype(bf)
    others, biases = [], []
    for m in range(micro):
        pairs = joined[m * rows : (m + 1) * rows, model:]
        parts = [
            lax.ppermute(pairs, "context", [(i, (i + s) % contexts) for i in range(contexts)])
            for s in range(1, contexts)
        ]
        others.append(parts[0] if contexts == 2 else jnp.concatenate(parts, axis=0))
        positions = token_order[m, 0]
        ends = jnp.cumsum(seq_lengths[m, 0])
        segments = jnp.sum((positions[:, None] >= ends[None, :]).astype(jnp.int32), axis=1)
        owners = [(here - s + contexts) % contexts for s in range(contexts)]
        key_positions = jnp.concatenate(
            [lax.dynamic_slice_in_dim(positions, o * rows, rows) for o in owners]
        )
        key_segments = jnp.concatenate(
            [lax.dynamic_slice_in_dim(segments, o * rows, rows) for o in owners]
        )
        query_positions, query_segments = key_positions[:rows], key_segments[:rows]
        biases.append(
            (
                jnp.where(
                    (key_positions[None, :] <= query_positions[:, None])
                    & (key_segments[None, :] == query_segments[:, None]),
                    0.0,
                    -1e30,
                ).astype(f32),
                (key_positions, key_segments),
            )
        )

    saved = []
    before = grads_there
    for m in range(micro):
        attended, mixed_low, lse = attn_fwd(joined, others[m], biases[m][0], m)
        log_total = lse[:, :HEADS].T
        middle = flat[m * rows : (m + 1) * rows].astype(f32) + jnp.dot(
            mixed_low, project_out, preferred_element_type=f32
        )
        second, normal_two, scale_two = layer_norm(middle, expert_gain, expert_shift)
        second_low = second.astype(bf)
        shares = jax.nn.softmax(
            jnp.dot(second_low, router_weight, preferred_element_type=f32), axis=-1
        )
        choose_float = (routes[m][:, None] == expert_ids[None, :]).astype(f32)
        gate = jnp.sum(shares * choose_float, axis=1)
        gate_high = gate.astype(bf)
        gate_low = (gate - gate_high.astype(f32)).astype(bf)
        slot_expert, slot_row = slot_ids // block, slot_ids % block
        mine = slot_expert[:, None] == routes[m][None, :]
        gates = jnp.where(
            mine & (slot_row == capacity)[:, None],
            gate_high[None, :],
            jnp.where(mine & (slot_row == capacity + 1)[:, None], gate_low[None, :], jnp.zeros((), bf)),
        )
        ladder = (ranks[m][:, None] == jnp.arange(model, dtype=jnp.int32)[None, :]).astype(bf)
        sent = jnp.dot(
            jnp.concatenate([places[m], gates], axis=1),
            jnp.concatenate([second_low, ladder], axis=0),
            preferred_element_type=f32,
        ).astype(bf)
        if m + 1 < micro:
            sent, others[m + 1] = lax.optimization_barrier((sent, others[m + 1]))
        if m + 1 == micro:
            logs = tuple(state[2] for state in saved) + (log_total,)
            attended, targets, places_in_pack, logs = lax.optimization_barrier(
                (attended, tuple(r * (2 * block) + k for r, k in zip(routes, ranks)),
                 tuple(b[1] for b in biases), logs)
            )
            wide = jnp.arange(2 * slots, dtype=jnp.int32)[:, None]
            place_two = [
                ((t[None, :] == wide).astype(bf), (t[None, :] + block == wide).astype(bf))
                for t in targets
            ]
            turned = [
                jnp.where(
                    (p[:, None] <= p[None, :rows]) & (g[:, None] == g[None, :rows]), 0.0, -1e30
                ).astype(f32)
                for p, g in places_in_pack
            ]
            sent, logs, turned, place_two = lax.optimization_barrier(
                (sent, logs, turned, place_two)
            )
            place_two = list(place_two)
            log_total = logs[-1]
            for n in range(m):
                saved[n][2] = logs[n]
            biases = [(b[0], t) for b, t in zip(biases, turned)]
        sent, before = lax.optimization_barrier((sent, before))
        if m == 0:
            grads_there = before
        else:
            saved[m - 1][-1] = before
        there = lax.all_to_all(
            sent.reshape(experts, block, model), "expert", split_axis=0, concat_axis=0, tiled=True
        )
        before = there
        saved.append(
            [attended, mixed_low, log_total, middle, second_low, normal_two, scale_two, shares,
             choose_float, gate, there]
        )

    kept = None
    rows_there, scaled_there, returned = [], [], []
    for m in range(micro):
        there = saved[m][-1]
        there = there.reshape(slots, model)
        active, inner_grad, back, scaled = expert(
            there, grads_there, weights, kept, m, micro, capacity
        )
        if m + 1 < micro:
            back, saved[m + 1][-1] = lax.optimization_barrier((back, saved[m + 1][-1]))
        kept = (active, inner_grad)
        rows_there.append(there)
        scaled_there.append(scaled)
        returned.append(
            lax.all_to_all(back, "expert", split_axis=0, concat_axis=0, tiled=True).reshape(
                2 * slots, model
            )
        )
    active, inner_grad = kept
    out_term = out_grads(scaled_there, active)
    out_term, inner_grad, returned[0] = lax.optimization_barrier((out_term, inner_grad, returned[0]))
    grad_out_weight = lax.psum_scatter(
        out_term, ("context", "dp"), scatter_dimension=0, tiled=True
    )

    outputs, middle_grads, branches, groups = [], [], [], []
    small = None
    for m in range(micro):
        (attended, mixed_low, log_total, middle, second_low, normal_two, scale_two, shares,
         choose_float, gate, _) = saved[m]
        grad_out = out_grad[m, 0].astype(f32)
        picked = lax.dot_general(place_two[m][0], returned[m], TN, preferred_element_type=f32)
        outputs.append((middle + gate[:, None] * picked).astype(bf))
        gate_grad = jnp.sum(grad_out * picked, axis=1)
        logit_grad = gate_grad[:, None] * gate[:, None] * (choose_float - shares)
        router_term = jnp.einsum("td,te->de", second_low.astype(f32), logit_grad, precision=HIGH)
        second_grad = jnp.einsum("te,de->td", logit_grad, router_float, precision=HIGH)
        second_grad = second_grad + lax.dot_general(
            place_two[m][1], returned[m], TN, preferred_element_type=f32
        )
        middle_part, gain_two, shift_two = norm_back(second_grad, normal_two, scale_two, expert_gain)
        middle_grad = grad_out + middle_part
        branch = middle_grad.astype(bf)
        mixed_grad = lax.dot_general(branch, project_out, NT, preferred_element_type=f32).astype(bf)
        query_grad, own, away = attn_bwd(
            joined, others[m], biases[m][1], log_total, mixed_grad, attended, m
        )
        parts = [
            lax.ppermute(
                away[:, (s - 1) * rows : s * rows] if contexts > 2 else away,
                "context",
                [(i, (i - s) % contexts) for i in range(contexts)],
            )
            for s in range(1, contexts)
        ]
        groups.append([query_grad, own, parts])
        if m == 0:
            inner_grad, query_grad = lax.optimization_barrier((inner_grad, query_grad))
            in_term = in_grads(rows_there, inner_grad, devices)
        if m + 1 < micro:
            in_term, query_grad, place_two[m + 1] = lax.optimization_barrier(
                (in_term, query_grad, place_two[m + 1])
            )
            groups[m][0] = query_grad
        middle_grads.append(middle_grad)
        branches.append(branch)
        terms = (gain_two, shift_two, router_term)
        small = terms if small is None else tuple(a + b for a, b in zip(small, terms))

    mixed_all = jnp.concatenate([s[1] for s in saved], axis=0)
    out_sum = lax.dot_general(
        mixed_all, jnp.concatenate(branches, axis=0), TN, preferred_element_type=f32
    ).astype(bf)
    near, expert_bits, dp_bits = bits_of("context"), bits_of("expert"), bits_of("dp")
    sent, kept = cut([out_sum], [near], 0)
    sent, kept, groups[-1][2][0] = lax.optimization_barrier((sent, kept, groups[-1][2][0]))
    out_half = kept[0] + swap(sent[0], *near[0])
    high = (here % 2).astype(jnp.int32).reshape(1)
    joined_grad, kept, sent, kept_too, sent_too = project_grads(normed_low, groups, high)
    kept, in_term, grad_out_weight, out_half = lax.optimization_barrier(
        (kept, in_term, grad_out_weight, out_half)
    )
    grad_in = lax.psum_scatter(in_term, ("context", "dp"), scatter_dimension=0, tiled=True)[0]
    halves = [kept + swap(sent, *near[0]), kept_too + swap(sent_too, *near[0])]
    halves.append(out_half)
    for slot in range(1, len(near)):
        halves = halve(halves, [near] * 3, slot)
    chunks = tuple(halves)

    orders = (
        expert_bits[:1] + dp_bits + expert_bits[1:],
        expert_bits[1:2] + expert_bits[:1] + dp_bits + expert_bits[2:],
        dp_bits + expert_bits[1:] + expert_bits[:1],
    )
    count = len(orders[0])
    steps = near + dp_bits + expert_bits
    for slot in range(count - 1):
        chunks = halve(chunks, orders, slot)
        if slot == 0:
            chunks, joined_grad = lax.optimization_barrier((chunks, joined_grad))
            normed_grad = lax.dot_general(joined_grad, project_in, NT, preferred_element_type=f32)
            input_part, gain_one, shift_one = norm_back(normed_grad, normal_one, scale_one, mixer_gain)
            grad_tokens = jnp.concatenate(middle_grads, axis=0) + input_part
            small = jnp.concatenate(
                [gain_one[None], shift_one[None], small[0][None], small[1][None], small[2].T], axis=0
            )
        elif slot == 1:
            chunks, small, grad_tokens = lax.optimization_barrier((chunks, small, grad_tokens))
        else:
            chunks = lax.optimization_barrier(chunks)
    for step in steps:
        small = small + swap(small, *step)
    chunks = lax.optimization_barrier(
        tuple(chunk + swap(chunk, *order[-1]) for chunk, order in zip(chunks, orders))
    )
    for slot in reversed(range(count - 1)):
        chunks = double(chunks, orders, slot)
        if slot == 0:
            done = (small[0], small[1], small[2], small[3], small[4:].T, jnp.stack(outputs)[:, None])
            chunks, done = lax.optimization_barrier((tuple(chunks), done))
            continue
        if slot == 1:
            chunks, small = lax.optimization_barrier((tuple(chunks), small))
        else:
            chunks = lax.optimization_barrier(tuple(chunks))
        if slot == count - 2:
            chunks, grad_in, grad_out_weight = lax.optimization_barrier(
                (chunks, grad_in, grad_out_weight)
            )
            grad_in = jnp.concatenate([grad_in[k] for k in range(grad_in.shape[0])], axis=1).astype(f32)
            grad_out_weight = grad_out_weight.astype(f32)
        if slot == 1:
            chunks, grad_in, grad_out_weight = lax.optimization_barrier(
                (chunks, grad_in, grad_out_weight)
            )
    for slot in reversed(range(1, len(near))):
        chunks = double(chunks, (near,) * 3, slot)
    arrived = [swap(chunk, *near[0]) for chunk in chunks]
    in_sum, out_sum = widen((chunks[:2], chunks[2:]), high)
    arrived, out_sum, in_sum = lax.optimization_barrier((arrived, out_sum, in_sum))
    in_sum, out_sum = widen((arrived[:2], arrived[2:]), 1 - high, (in_sum, out_sum))
    return (
        done[5],
        grad_tokens.reshape(micro, 1, rows, model),
        done[0],
        done[1],
        in_sum,
        out_sum,
        done[2],
        done[3],
        done[4],
        grad_in[None],
        grad_out_weight[None],
    )


def solution(mesh):
    tokens = P(None, ("expert", "dp"), "context", None)
    packs = P(None, ("expert", "dp"), None)
    weights = P("expert", ("context", "dp"), None)
    in_specs = (tokens, tokens, packs, packs, tokens) + (P(),) * 7 + (weights, weights)
    out_specs = (tokens, tokens) + (P(),) * 7 + (weights, weights)
    return jax.shard_map(local, mesh=mesh, in_specs=in_specs, out_specs=out_specs, check_vma=False)
```
